512 devices in a mesh: band: 8 (over y, z_hi), chan: 64 (over z_lo, x, core).
Axes of the slice: x: 4, y: 4, z: 16 (z_hi: 2, z_lo: 8; z = z_hi * 8 + z_lo), core: 2. Of those that a mesh axis runs over, the one named last changes fastest.
Arguments:
- field: bfloat16 [256, 16, 128, 360], P('chan', None, 'band'), may hold values from -6 to 6
- noise_level: int32 [16], replicated, may hold values from 0 to 19
- conv_kernel: float32 [2, 256, 7, 7], P(None, 'chan'), may hold values from -0.875 to 0.875
- conv_bias: float32 [2, 256], P(None, 'chan'), may hold values from -3 to 3
- modulation: float32 [2, 20, 2, 256], replicated, may hold values from -3 to 3
- expand_weight: bfloat16 [2, 256, 1024], replicated, may hold values from -0.375 to 0.375
- expand_bias: float32 [2, 1024], replicated, may hold values from -3 to 3
- project_weight: bfloat16 [2, 1024, 256], replicated, may hold values from -0.1875 to 0.1875
- project_bias: float32 [2, 256], replicated, may hold values from -3 to 3
- layer_scale: float32 [2, 256], replicated, may hold values from 0.3 to 1.5
Outputs:
- updated: bfloat16 [256, 16, 128, 360], P('chan', None, 'band')
The draws below stay inside these ranges and needn't reach their ends.
All inputs are finite; a program needn't handle non-finite values.
Results may differ from the reference program's by a relative error of at most 0.0069.
Values may be sent and summed in bfloat16 or wider, within the bound.
No kernel may reach another device: no remote copies, remote signals or barrier semaphores. Data moves between devices by JAX's collectives and lax.ppermute only.
A program may use at most 64 MiB of HBM per device.

```python
import math
import jax
import jax.numpy as jnp
from jax import lax

C = 256
F = 1024
NLEV = 20
LAYERS = 2
W = 360
B = 16
H = 128


def plant(entries, own_key, smallest, largest):
    extent = entries.shape
    place = [jax.random.randint(jax.random.fold_in(own_key, axis), (), 0, extent[axis]) for axis in range(len(extent))]
    entries = entries.at[tuple(place)].set(smallest)
    longest = extent.index(max(extent))
    place[longest] = (place[longest] + 1) % extent[longest]
    return entries.at[tuple(place)].set(largest)


def level_of(rng, extent, shards, least, high):
    level, own = 1.0, jax.random.fold_in(rng, 6)
    for axis_at, blocks in shards:
        heights = jnp.exp(jax.random.uniform(jax.random.fold_in(own, axis_at), (blocks,), jnp.float32, least / len(shards), high / len(shards)))
        level = level * jnp.repeat(heights, extent[axis_at] // blocks).reshape([-1 if axis == axis_at else 1 for axis in range(len(extent))])
    return level


def normal_values(rng, dims, scale, most, pieces=(), kind=jnp.bfloat16):
    gain = level_of(rng, dims, pieces, -0.22, 0.18) if pieces else 1.0
    drawn = jax.random.normal(rng, dims, jnp.float32) * scale * gain
    return jnp.minimum(jnp.maximum(drawn, -most), most).astype(kind)


def setup_inputs(seed: int = 0) -> dict:
    key_list = jax.random.split(jax.random.key(seed), 11)
    field = normal_values(key_list[0], (C, B, H, W), 1.0, 6.0, ((0, 64), (2, 8)))
    noise_level = plant(jax.random.randint(key_list[1], (B,), 0, NLEV), jax.random.fold_in(key_list[1], 1), 0, NLEV - 1).astype(jnp.int32)
    conv_kernel = normal_values(key_list[2], (LAYERS, C, 7, 7), 49 ** -0.5, 0.875, ((1, 64),), jnp.float32)
    conv_bias = normal_values(key_list[3], (LAYERS, C), 0.5, 3.0, ((1, 64),), jnp.float32)
    modulation = normal_values(key_list[4], (LAYERS, NLEV, 2, C), 0.5, 3.0, (), jnp.float32)
    expand_weight = normal_values(key_list[5], (LAYERS, C, F), C ** -0.5, 0.375)
    expand_bias = normal_values(key_list[6], (LAYERS, F), 0.5, 3.0, (), jnp.float32)
    project_weight = normal_values(key_list[7], (LAYERS, F, C), F ** -0.5, 0.1875)
    project_bias = normal_values(key_list[8], (LAYERS, C), 0.5, 3.0, (), jnp.float32)
    layer_scale = jnp.clip(jnp.exp(jax.random.uniform(key_list[9], (LAYERS, C), jnp.float32, math.log(0.3), math.log(1.5))), 0.3, 1.5)
    return {"field": field, "noise_level": noise_level, "conv_kernel": conv_kernel, "conv_bias": conv_bias, "modulation": modulation, "expand_weight": expand_weight, "expand_bias": expand_bias, "project_weight": project_weight, "project_bias": project_bias, "layer_scale": layer_scale}


epsilon = 1e-06

def depthwise(padded, kernel, bias_vec):
    lat_rows = padded.shape[-2] - 6
    lon_cols = padded.shape[-1]
    wrapped = jnp.concatenate([padded[..., -3:], padded, padded[..., :3]], axis=-1).astype(jnp.float32)
    kernel_shape = (kernel.shape[0],) + (1,) * (padded.ndim - 1)
    accum_sum = jnp.zeros(padded.shape[:-2] + (lat_rows, lon_cols), jnp.float32)
    for tap_row in range(7):
        for tap_col in range(7):
            window = wrapped[..., tap_row:tap_row + lat_rows, tap_col:tap_col + lon_cols]
            accum_sum = accum_sum + kernel[:, tap_row, tap_col].reshape(kernel_shape) * window
    return (accum_sum + bias_vec.reshape(kernel_shape)).astype(jnp.bfloat16)

def member_branch(mixed, level, block_num, modulation, expand_weight, expand_bias, project_weight, project_bias, layer_scale):
    widened = mixed.astype(jnp.float32)
    average = lax.optimization_barrier(jnp.mean(widened, axis=0, keepdims=True))
    centered = widened - average
    variance = lax.optimization_barrier(jnp.mean(centered * centered, axis=0, keepdims=True))
    scales = modulation[block_num][level]
    normed = (centered * lax.rsqrt(variance + epsilon) * (1.0 + scales[0][:, None, None]) + scales[1][:, None, None]).astype(jnp.bfloat16)
    hidden = jnp.einsum('cf,chw->fhw', expand_weight[block_num].astype(jnp.float32), normed.astype(jnp.float32), precision=lax.Precision.HIGHEST) + expand_bias[block_num][:, None, None]
    active = jax.nn.gelu(hidden, approximate=False).astype(jnp.bfloat16)
    result_c = jnp.einsum('fc,fhw->chw', project_weight[block_num].astype(jnp.float32), active.astype(jnp.float32), precision=lax.Precision.HIGHEST) + project_bias[block_num][:, None, None]
    return (layer_scale[block_num][:, None, None] * result_c).astype(jnp.bfloat16)

def reference(field, noise_level, conv_kernel, conv_bias, modulation, expand_weight, expand_bias, project_weight, project_bias, layer_scale):

    def one_member(inputs):
        current, level = inputs
        for block_num in range(LAYERS):
            padded = jnp.pad(current, ((0, 0), (3, 3), (0, 0)))
            mixed = depthwise(padded, conv_kernel[block_num], conv_bias[block_num])
            branch = member_branch(mixed, level, block_num, modulation, expand_weight, expand_bias, project_weight, project_bias, layer_scale)
            current = (current.astype(jnp.float32) + branch.astype(jnp.float32)).astype(jnp.bfloat16)
        return current
    stacked = lax.map(one_member, (jnp.moveaxis(field, 1, 0), noise_level))
    return jnp.moveaxis(stacked, 0, 1)
```

```python
import jax
import jax.numpy as jnp
from jax import lax
from jax.experimental import pallas as pl
from jax.experimental.pallas import tpu as pltpu
from jax.sharding import Mesh, PartitionSpec as P

EPS = 1e-06
LANES = 128
TAPS = 7
REACH = 3
LEFT = 8


def lane_iota(rows):
    return lax.broadcasted_iota(jnp.int32, (rows, LANES), 1)


def moved_lanes(load, spans, rows):
    lanes = lane_iota(rows)
    tile = jnp.zeros((rows, LANES), jnp.float32)
    for source, src, dst, width in spans:
        done = 0
        while done < width:
            part, lane = divmod(src + done, LANES)
            take = min(width - done, LANES - lane)
            value = load(source, part)
            shift = (dst + done - lane) % LANES
            if shift:
                value = pltpu.roll(value, shift, 1)
            lo, hi = dst + done, dst + done + take
            tile = jnp.where((lanes >= lo) & (lanes < hi), value, tile)
            done += take
    return tile


def spans_of(total, count, stride, width, tile_index, start_of):
    spans = []
    for item in range(count):
        lo = max(item * stride, tile_index * LANES)
        hi = min(item * stride + width, (tile_index + 1) * LANES)
        if lo < hi:
            spans.append((item, start_of(item) + lo - item * stride, lo - tile_index * LANES, hi - lo))
    return spans


def cut_kernel(field_ref, out_ref, wide, cut, *, seg, slot):
    chans, members, lats, lons = field_ref.shape
    rows = chans * members
    parts = -(-lons // LANES)
    segs = lons // seg
    tiles = lats * slot // LANES
    for a in range(parts):
        lo, hi = a * LANES, min((a + 1) * LANES, lons)
        piece = field_ref[:, :, :, lo:hi].astype(jnp.float32).reshape(rows * lats, hi - lo)
        wide[a, :, 0 : hi - lo] = piece
    for s in range(segs):
        for t in range(tiles):
            spans = spans_of(0, lats, slot, seg, t, lambda item: s * seg)

            def load(lat, part):
                return wide[part, pl.ds(lat, rows, stride=lats), :]

            tile = moved_lanes(load, spans, rows)
            for c in range(chans):
                start = s * chans * tiles + c * tiles + t
                cut[pl.ds(start, members, stride=segs * chans * tiles), :] = tile[
                    c * members : (c + 1) * members
                ]
    out_ref[...] = cut[...].astype(jnp.bfloat16)


def paste_kernel(in_ref, out_ref, cut, wide, *, seg, slot):
    chans, members, lats, lons = out_ref.shape
    rows = chans * members
    parts = -(-lons // LANES)
    segs = lons // seg
    tiles = lats * slot // LANES
    cut[...] = in_ref[...].astype(jnp.float32)
    for lat in range(lats):
        for a in range(parts):
            spans = spans_of(0, segs, seg, seg, a, lambda item: lat * slot)

            def load(s, part):
                return jnp.concatenate(
                    [
                        cut[
                            pl.ds(
                                s * chans * tiles + c * tiles + part,
                                members,
                                stride=segs * chans * tiles,
                            ),
                            :,
                        ]
                        for c in range(chans)
                    ],
                    axis=0,
                )

            wide[a, pl.ds(lat, rows, stride=lats), :] = moved_lanes(load, spans, rows)
    for a in range(parts):
        lo, hi = a * LANES, min((a + 1) * LANES, lons)
        out_ref[:, :, :, lo:hi] = (
            wide[a, :, 0 : hi - lo].reshape(chans, members, lats, hi - lo).astype(jnp.bfloat16)
        )


def to_cells_kernel(in_ref, out_ref, rows32, *, tiles):
    channels = out_ref.shape[1]
    halves = in_ref.shape[0] // (channels * tiles)
    rows32[...] = in_ref[...].astype(jnp.float32)
    for half in range(halves):
        for t in range(tiles):
            block = rows32[pl.ds(half * channels * tiles + t, channels, stride=tiles), :]
            start = (half * tiles + t) * LANES
            out_ref[start : start + LANES, :] = block.T.astype(jnp.bfloat16)


def to_channels_kernel(in_ref, out_ref, rows32, *, tiles):
    channels = in_ref.shape[1]
    halves = out_ref.shape[0] // (channels * tiles)
    for half in range(halves):
        for t in range(tiles):
            start = (half * tiles + t) * LANES
            block = in_ref[start : start + LANES, :].astype(jnp.float32)
            rows32[pl.ds(half * channels * tiles + t, channels, stride=tiles), :] = block.T
    out_ref[...] = rows32[...].astype(jnp.bfloat16)


def block_kernel(
    x_ref, top_ref, bottom_ref, left_ref, right_ref, taps_ref, mod_ref,
    up_ref, up_bias_ref, down_ref, down_bias_ref, scale_ref,
    out_ref, padded, spread, mixed,
):
    lats, slot, channels = x_ref.shape
    groups = channels // LANES
    col_tiles = slot // 8
    row_block = 8
    for g in range(groups):
        ch = slice(g * LANES, (g + 1) * LANES)
        padded[g, 0:REACH, LEFT : LEFT + slot, :] = top_ref[:, :, ch].astype(jnp.float32)
        padded[g, REACH : REACH + lats, LEFT : LEFT + slot, :] = x_ref[:, :, ch].astype(jnp.float32)
        padded[g, REACH + lats :, LEFT : LEFT + slot, :] = bottom_ref[:, :, ch].astype(jnp.float32)
        padded[g, :, LEFT + slot :, :] = jnp.zeros(
            (lats + 2 * REACH, padded.shape[2] - LEFT - slot, LANES), jnp.float32
        )
        padded[g, :, LEFT - REACH : LEFT, :] = left_ref[:, :, ch].astype(jnp.float32)
        right_at = LEFT + slot - REACH
        padded[g, :, right_at : right_at + REACH, :] = right_ref[:, :, ch].astype(jnp.float32)
        for k in range(TAPS * TAPS + 1):
            spread[g, k] = jnp.broadcast_to(taps_ref[k : k + 1, ch], (8, LANES))

    def conv_step(step, carry):
        g = step // (lats // row_block)
        row = (step % (lats // row_block)) * row_block
        for k in range(col_tiles):
            sums = [spread[g, TAPS * TAPS]] * row_block
            for j in range(TAPS):
                col = LEFT - REACH + j + 8 * k
                weights = [spread[g, i * TAPS + j] for i in range(TAPS)]
                for r in range(row_block + TAPS - 1):
                    value = padded[g, row + r, col : col + 8, :]
                    for i in range(TAPS):
                        if 0 <= r - i < row_block:
                            sums[r - i] = sums[r - i] + weights[i] * value
            for r in range(row_block):
                mixed[g, row + r, 8 * k : 8 * k + 8, :] = sums[r]
        return carry

    lax.fori_loop(0, groups * (lats // row_block), conv_step, 0)
    mlp_rows = 8
    cells = mlp_rows * slot
    average_matrix = jnp.full((channels, channels), 1.0 / channels, jnp.bfloat16)

    def mlp_step(step, carry):
        row = step * mlp_rows
        parts = [
            mixed[g, pl.ds(row, mlp_rows), :, :].reshape(cells, LANES) for g in range(groups)
        ]
        rounded = jnp.concatenate(parts, axis=1).astype(jnp.bfloat16)
        average = jnp.dot(rounded, average_matrix, preferred_element_type=jnp.float32)
        centered = rounded.astype(jnp.float32) - average
        variance = jnp.dot(
            (centered * centered).astype(jnp.bfloat16),
            average_matrix,
            preferred_element_type=jnp.float32,
        )
        normed = centered * lax.rsqrt(variance + EPS) * (1.0 + mod_ref[0:1, :]) + mod_ref[1:2, :]
        hidden = (
            jnp.dot(normed.astype(jnp.bfloat16), up_ref[0], preferred_element_type=jnp.float32)
            + up_bias_ref[...]
        )
        active = (0.5 * hidden * (1.0 + lax.erf(hidden * 0.7071067811865476))).astype(jnp.bfloat16)
        result = (
            jnp.dot(active, down_ref[0], preferred_element_type=jnp.float32) + down_bias_ref[...]
        )
        branch = (scale_ref[...] * result).astype(jnp.bfloat16).astype(jnp.float32)
        current = x_ref[pl.ds(row, mlp_rows), :, :].astype(jnp.float32)
        out_ref[pl.ds(row, mlp_rows), :, :] = (
            current + branch.reshape(mlp_rows, slot, channels)
        ).astype(jnp.bfloat16)
        return carry

    lax.fori_loop(0, lats // mlp_rows, mlp_step, 0)


def whole(shape):
    return pl.BlockSpec(shape, lambda *_: (0,) * len(shape))


def run_cut(field, seg, slot):
    chans, members, lats, lons = field.shape
    tiles = lats * slot // LANES
    rows = members * (lons // seg) * chans * tiles
    return pl.pallas_call(
        lambda *refs: cut_kernel(*refs, seg=seg, slot=slot),
        out_shape=jax.ShapeDtypeStruct((rows, LANES), jnp.bfloat16),
        scratch_shapes=[
            pltpu.VMEM((-(-lons // LANES), chans * members * lats, LANES), jnp.float32),
            pltpu.VMEM((rows, LANES), jnp.float32),
        ],
        name="cut",
    )(field)


def run_paste(pieces, shape, seg, slot):
    chans, members, lats, lons = shape
    return pl.pallas_call(
        lambda *refs: paste_kernel(*refs, seg=seg, slot=slot),
        out_shape=jax.ShapeDtypeStruct(shape, jnp.bfloat16),
        scratch_shapes=[
            pltpu.VMEM(pieces.shape, jnp.float32),
            pltpu.VMEM((-(-lons // LANES), chans * members * lats, LANES), jnp.float32),
        ],
        name="paste",
    )(pieces)


def run_to_cells(pieces, cells, channels, tiles):
    return pl.pallas_call(
        lambda *refs: to_cells_kernel(*refs, tiles=tiles),
        out_shape=jax.ShapeDtypeStruct((cells, channels), jnp.bfloat16),
        scratch_shapes=[pltpu.VMEM(pieces.shape, jnp.float32)],
        name="to_cells",
    )(pieces)


def run_to_channels(x, tiles):
    rows = x.shape[0] * x.shape[1] // LANES
    return pl.pallas_call(
        lambda *refs: to_channels_kernel(*refs, tiles=tiles),
        out_shape=jax.ShapeDtypeStruct((rows, LANES), jnp.bfloat16),
        scratch_shapes=[pltpu.VMEM((rows, LANES), jnp.float32)],
        name="to_channels",
    )(x)


def run_block(x, halos, taps, mod, layer, up, up_bias, down, down_bias, scale):
    lats, slot, channels = x.shape
    groups = channels // LANES
    hidden = up.shape[2]
    arrays = (x, *halos, taps, mod)
    return pl.pallas_call(
        block_kernel,
        grid=(1,),
        out_shape=jax.ShapeDtypeStruct(x.shape, jnp.bfloat16),
        in_specs=[whole(a.shape) for a in arrays]
        + [
            pl.BlockSpec((1, channels, hidden), lambda _: (layer, 0, 0)),
            whole((1, hidden)),
            pl.BlockSpec((1, hidden, channels), lambda _: (layer, 0, 0)),
            whole((1, channels)),
            whole((1, channels)),
        ],
        out_specs=whole(x.shape),
        scratch_shapes=[
            pltpu.VMEM((groups, lats + 2 * REACH, LEFT + slot + 8, LANES), jnp.float32),
            pltpu.VMEM((groups, TAPS * TAPS + 1, 8, LANES), jnp.float32),
            pltpu.VMEM((groups, lats, slot, LANES), jnp.float32),
        ],
        name="block",
    )(
        *arrays,
        up, up_bias[layer][None], down, down_bias[layer][None], scale[layer][None],
    )


def halo_of(x, seg):
    rows, segs = lax.axis_size("y"), lax.axis_size("xc")
    down = [(i, i + 1) for i in range(rows - 1)]
    up = [(j, i) for i, j in down]
    top = lax.ppermute(x[-REACH:], "y", down)
    bottom = lax.ppermute(x[:REACH], "y", up)
    east = [(i, (i + 1) % segs) for i in range(segs)]
    west = [(j, i) for i, j in east]

    def columns(lo):
        return jnp.concatenate(
            [part[:, lo : lo + REACH] for part in (top, x, bottom)], axis=0
        )

    left = lax.ppermute(columns(seg - REACH), "xc", east)
    right = lax.ppermute(columns(0), "xc", west)
    return top, bottom, left, right


def on_device(
    field, noise_level, conv_kernel, conv_bias, modulation,
    expand_weight, expand_bias, project_weight, project_bias, layer_scale,
):
    chans, members, lats, lons = field.shape
    layers = conv_kernel.shape[0]
    halves = lax.axis_size("zh")
    segs = lax.axis_size("xc")
    peers = halves * lax.axis_size("zl") * segs
    channels = chans * lax.axis_size("zl") * segs
    seg = lons // segs
    slot = -(-seg // 8) * 8
    tiles = lats * slot // LANES
    member = lax.axis_index("zh") * lax.axis_size("zl") + lax.axis_index("zl")
    mods = modulation[:, noise_level[member]]

    filters = jnp.concatenate(
        [conv_kernel.reshape(layers, chans, TAPS * TAPS), conv_bias[:, :, None]], axis=2
    )
    filters = jnp.broadcast_to(filters.reshape(1, -1), (channels // chans, filters.size))
    filters = lax.all_to_all(filters, ("zl", "xc"), 0, 0, tiled=True)
    filters = filters.reshape(channels // chans, layers, chans, TAPS * TAPS + 1)
    filters = filters.transpose(1, 3, 0, 2).reshape(layers, TAPS * TAPS + 1, channels)

    pieces = run_cut(field, seg, slot)
    shape = (peers, chans * tiles, LANES)
    around = ("zh", "zl", "xc")
    pieces = lax.all_to_all(pieces.reshape(shape), around, 0, 0, tiled=True).reshape(-1, LANES)
    x = run_to_cells(pieces, halves * lats * slot, channels, tiles)
    x = x.reshape(halves * lats, slot, channels)
    for layer in range(layers):
        halos = halo_of(x, seg)
        x = run_block(
            x, halos, filters[layer], mods[layer], layer,
            expand_weight, expand_bias, project_weight, project_bias, layer_scale,
        )
    pieces = run_to_channels(x.reshape(-1, channels), tiles)
    pieces = lax.all_to_all(pieces.reshape(shape), around, 0, 0, tiled=True).reshape(-1, LANES)
    return run_paste(pieces, field.shape, seg, slot)


def solution(mesh):
    bands, chan = mesh.shape["band"], mesh.shape["chan"]
    split = Mesh(mesh.devices.reshape(bands // 2, 2, chan // 8, 8), ("y", "zh", "zl", "xc"))
    band, group = ("y", "zh"), ("zl", "xc")
    return jax.shard_map(
        on_device,
        mesh=split,
        in_specs=(
            P(group, None, band, None),
            P(),
            P(None, group, None, None),
            P(None, group),
            P(), P(), P(), P(), P(), P(),
        ),
        out_specs=P(group, None, band, None),
        check_vma=False,
    )
```

```python
import jax
import jax.numpy as jnp
from jax import lax
from jax.experimental import pallas as pl
from jax.experimental.pallas import tpu as pltpu
from jax.sharding import Mesh, PartitionSpec as P

EPS = 1e-06
LANES = 128
TAPS = 7
REACH = 3
LEFT = 8
ROWS = 8


def lane_iota(rows):
    return lax.broadcasted_iota(jnp.int32, (rows, LANES), 1)


def moved_lanes(load, spans, rows):
    lanes = lane_iota(rows)
    tile = jnp.zeros((rows, LANES), jnp.float32)
    for source, src, dst, width in spans:
        done = 0
        while done < width:
            part, lane = divmod(src + done, LANES)
            take = min(width - done, LANES - lane)
            value = load(source, part)
            shift = (dst + done - lane) % LANES
            if shift:
                value = pltpu.roll(value, shift, 1)
            lo, hi = dst + done, dst + done + take
            tile = jnp.where((lanes >= lo) & (lanes < hi), value, tile)
            done += take
    return tile


def spans_of(total, count, stride, width, tile_index, start_of):
    spans = []
    for item in range(count):
        lo = max(item * stride, tile_index * LANES)
        hi = min(item * stride + width, (tile_index + 1) * LANES)
        if lo < hi:
            spans.append((item, start_of(item) + lo - item * stride, lo - tile_index * LANES, hi - lo))
    return spans


def cut_kernel(field_ref, out_ref, wide, cut, *, seg, slot):
    chans, members, lats, lons = field_ref.shape
    rows = chans * members
    parts = -(-lons // LANES)
    segs = lons // seg
    tiles = lats * slot // LANES
    for a in range(parts):
        lo, hi = a * LANES, min((a + 1) * LANES, lons)
        piece = field_ref[:, :, :, lo:hi].astype(jnp.float32).reshape(rows * lats, hi - lo)
        wide[a, :, 0 : hi - lo] = piece
    for s in range(segs):
        for t in range(tiles):
            spans = spans_of(0, lats, slot, seg, t, lambda item: s * seg)

            def load(lat, part):
                return wide[part, pl.ds(lat, rows, stride=lats), :]

            tile = moved_lanes(load, spans, rows)
            for c in range(chans):
                start = s * chans * tiles + c * tiles + t
                cut[pl.ds(start, members, stride=segs * chans * tiles), :] = tile[
                    c * members : (c + 1) * members
                ]
    out_ref[...] = cut[...].astype(jnp.bfloat16)


def paste_kernel(in_ref, out_ref, cut, wide, *, seg, slot):
    chans, members, lats, lons = out_ref.shape
    rows = chans * members
    parts = -(-lons // LANES)
    segs = lons // seg
    tiles = lats * slot // LANES
    cut[...] = in_ref[...].astype(jnp.float32)
    for lat in range(lats):
        for a in range(parts):
            spans = spans_of(0, segs, seg, seg, a, lambda item: lat * slot)

            def load(s, part):
                return jnp.concatenate(
                    [
                        cut[
                            pl.ds(
                                s * chans * tiles + c * tiles + part,
                                members,
                                stride=segs * chans * tiles,
                            ),
                            :,
                        ]
                        for c in range(chans)
                    ],
                    axis=0,
                )

            wide[a, pl.ds(lat, rows, stride=lats), :] = moved_lanes(load, spans, rows)
    for a in range(parts):
        lo, hi = a * LANES, min((a + 1) * LANES, lons)
        out_ref[:, :, :, lo:hi] = (
            wide[a, :, 0 : hi - lo].reshape(chans, members, lats, hi - lo).astype(jnp.bfloat16)
        )


def to_cells_kernel(in_ref, out_ref, rows32, *, tiles):
    channels = out_ref.shape[1]
    halves = in_ref.shape[0] // (channels * tiles)
    rows32[...] = in_ref[...].astype(jnp.float32)
    for half in range(halves):
        for t in range(tiles):
            block = rows32[pl.ds(half * channels * tiles + t, channels, stride=tiles), :]
            start = (half * tiles + t) * LANES
            out_ref[start : start + LANES, :] = block.T.astype(jnp.bfloat16)


def taps_over(load, spread, layer, group, cols, sums):
    rows = len(sums)
    for j in range(TAPS):
        weights = [spread[layer, group, i * TAPS + j] for i in range(TAPS)]
        for r in range(rows + TAPS - 1):
            value = load(r, cols + j)
            for i in range(TAPS):
                if 0 <= r - i < rows:
                    sums[r - i] = sums[r - i] + weights[i] * value
    return sums


def depthwise(source, spread, mixed, layer, lats, col_tiles, first_col):
    groups = source.shape[0]
    steps = -(-lats // ROWS)

    def step_of(step, carry):
        g = step // steps
        row = jnp.minimum((step % steps) * ROWS, lats - ROWS)
        for k in range(col_tiles):
            sums = [spread[layer, g, TAPS * TAPS]] * ROWS
            sums = taps_over(
                lambda r, col: source[g, row + r, col : col + 8, :],
                spread, layer, g, first_col + 8 * k, sums,
            )
            for r in range(ROWS):
                mixed[g, row + r, 8 * k : 8 * k + 8, :] = sums[r]
        return carry

    lax.fori_loop(0, groups * steps, step_of, 0)


def pointwise(mixed, layer, lats, slot, residual, store, weights):
    mod_ref, up_ref, up_bias_ref, down_ref, down_bias_ref, scale_ref = weights
    groups = mixed.shape[0]
    channels = groups * LANES
    cells = ROWS * slot
    steps = -(-lats // ROWS)
    average_matrix = jnp.full((channels, channels), 1.0 / channels, jnp.bfloat16)

    def step_of(step, carry):
        row = jnp.minimum(step * ROWS, lats - ROWS)
        parts = [mixed[g, pl.ds(row, ROWS), 0:slot, :].reshape(cells, LANES) for g in range(groups)]
        rounded = jnp.concatenate(parts, axis=1).astype(jnp.bfloat16)
        average = jnp.dot(rounded, average_matrix, preferred_element_type=jnp.float32)
        centered = rounded.astype(jnp.float32) - average
        variance = jnp.dot(
            (centered * centered).astype(jnp.bfloat16),
            average_matrix,
            preferred_element_type=jnp.float32,
        )
        gain = 1.0 + mod_ref[2 * layer : 2 * layer + 1, :]
        shift = mod_ref[2 * layer + 1 : 2 * layer + 2, :]
        normed = (centered * lax.rsqrt(variance + EPS) * gain + shift).astype(jnp.bfloat16)
        hidden = (
            jnp.dot(normed, up_ref[layer], preferred_element_type=jnp.float32)
            + up_bias_ref[layer : layer + 1, :]
        )
        active = (0.5 * hidden * (1.0 + lax.erf(hidden * 0.7071067811865476))).astype(jnp.bfloat16)
        result = (
            jnp.dot(active, down_ref[layer], preferred_element_type=jnp.float32)
            + down_bias_ref[layer : layer + 1, :]
        )
        branch = (scale_ref[layer : layer + 1, :] * result).astype(jnp.bfloat16).astype(jnp.float32)
        for g in range(groups):
            part = branch[:, g * LANES : (g + 1) * LANES].reshape(ROWS, slot, LANES)
            store(g, row, (residual(g, row) + part).astype(jnp.bfloat16).astype(jnp.float32))
        return carry

    lax.fori_loop(0, steps, step_of, 0)


def blocks_kernel(
    edge_ref, x_ref, top_ref, bottom_ref, left_ref, right_ref, taps_ref, mod_ref,
    up_ref, up_bias_ref, down_ref, down_bias_ref, scale_ref,
    out_ref, first, second, spread, mixed, final, rows32, *, tiles,
):
    lats, slot, channels = x_ref.shape
    groups = channels // LANES
    reach = 2 * REACH
    wide = lats + reach
    right_at = LEFT + slot - REACH
    for g in range(groups):
        ch = slice(g * LANES, (g + 1) * LANES)
        first[g, 0:reach, LEFT : LEFT + slot, :] = top_ref[:, :, ch].astype(jnp.float32)
        first[g, reach : reach + lats, LEFT : LEFT + slot, :] = x_ref[:, :, ch].astype(jnp.float32)
        first[g, reach + lats :, LEFT : LEFT + slot, :] = bottom_ref[:, :, ch].astype(jnp.float32)
        first[g, :, LEFT + slot :, :] = jnp.zeros(
            (lats + 2 * reach, first.shape[2] - LEFT - slot, LANES), jnp.float32
        )
        first[g, :, LEFT - reach : LEFT, :] = left_ref[:, :, ch].astype(jnp.float32)
        first[g, :, right_at : right_at + reach, :] = right_ref[:, :, ch].astype(jnp.float32)
        for layer in range(taps_ref.shape[0]):
            for k in range(TAPS * TAPS + 1):
                spread[layer, g, k] = jnp.broadcast_to(taps_ref[layer, k : k + 1, ch], (8, LANES))
    weights = (mod_ref, up_ref, up_bias_ref, down_ref, down_bias_ref, scale_ref)

    wide_slot = slot + 8
    depthwise(first, spread, mixed, 0, wide, wide_slot // 8, LEFT - reach)

    def first_store(g, row, value):
        second[g, pl.ds(row, ROWS), :, :] = value

    pointwise(
        mixed, 0, wide, wide_slot,
        lambda g, row: first[g, pl.ds(row + REACH, ROWS), LEFT - REACH : LEFT - REACH + wide_slot, :],
        first_store, weights,
    )

    @pl.when(edge_ref[0] == 1)
    def _():
        second[:, 0:REACH, :, :] = jnp.zeros((groups, REACH, wide_slot, LANES), jnp.float32)

    @pl.when(edge_ref[1] == 1)
    def _():
        second[:, REACH + lats :, :, :] = jnp.zeros((groups, REACH, wide_slot, LANES), jnp.float32)

    depthwise(second, spread, mixed, 1, lats, slot // 8, 0)

    def final_store(g, row, value):
        final[g, pl.ds(row, ROWS), :, :] = value

    pointwise(
        mixed, 1, lats, slot,
        lambda g, row: second[g, pl.ds(row + REACH, ROWS), REACH : REACH + slot, :],
        final_store, weights,
    )
    flat = lats * slot // tiles // LANES
    rows_per = LANES * 3 // slot
    for half in range(flat):
        for g in range(groups):
            for part in range(tiles // 3):
                lat = (half * tiles + part * 3) * LANES // slot
                block = final[g, lat : lat + rows_per, :, :].reshape(rows_per * slot, LANES)
                for t in range(3):
                    start = half * channels * tiles + g * LANES * tiles + part * 3 + t
                    rows32[pl.ds(start, LANES, stride=tiles), :] = block[
                        t * LANES : (t + 1) * LANES
                    ].T
    out_ref[...] = rows32[...].astype(jnp.bfloat16)


def run_cut(field, seg, slot):
    chans, members, lats, lons = field.shape
    tiles = lats * slot // LANES
    rows = members * (lons // seg) * chans * tiles
    return pl.pallas_call(
        lambda *refs: cut_kernel(*refs, seg=seg, slot=slot),
        out_shape=jax.ShapeDtypeStruct((rows, LANES), jnp.bfloat16),
        scratch_shapes=[
            pltpu.VMEM((-(-lons // LANES), chans * members * lats, LANES), jnp.float32),
            pltpu.VMEM((rows, LANES), jnp.float32),
        ],
        name="cut",
    )(field)


def run_paste(pieces, shape, seg, slot):
    chans, members, lats, lons = shape
    return pl.pallas_call(
        lambda *refs: paste_kernel(*refs, seg=seg, slot=slot),
        out_shape=jax.ShapeDtypeStruct(shape, jnp.bfloat16),
        scratch_shapes=[
            pltpu.VMEM(pieces.shape, jnp.float32),
            pltpu.VMEM((-(-lons // LANES), chans * members * lats, LANES), jnp.float32),
        ],
        name="paste",
    )(pieces)


def run_to_cells(pieces, cells, channels, tiles):
    return pl.pallas_call(
        lambda *refs: to_cells_kernel(*refs, tiles=tiles),
        out_shape=jax.ShapeDtypeStruct((cells, channels), jnp.bfloat16),
        scratch_shapes=[pltpu.VMEM(pieces.shape, jnp.float32)],
        name="to_cells",
    )(pieces)


def run_blocks(edges, x, halos, taps, mods, up, up_bias, down, down_bias, scale, tiles):
    lats, slot, channels = x.shape
    groups = channels // LANES
    rows = lats * slot * channels // LANES
    vmem = pl.BlockSpec(memory_space=pltpu.VMEM)
    arrays = (x, *halos, taps, mods, up, up_bias, down, down_bias, scale)
    wide_slot = slot + 8
    return pl.pallas_call(
        lambda *refs: blocks_kernel(*refs, tiles=tiles),
        out_shape=jax.ShapeDtypeStruct((rows, LANES), jnp.bfloat16),
        in_specs=[pl.BlockSpec(memory_space=pltpu.SMEM)] + [vmem] * len(arrays),
        scratch_shapes=[
            pltpu.VMEM((groups, lats + 4 * REACH, LEFT + wide_slot, LANES), jnp.float32),
            pltpu.VMEM((groups, lats + 2 * REACH, wide_slot, LANES), jnp.float32),
            pltpu.VMEM((taps.shape[0], groups, TAPS * TAPS + 1, 8, LANES), jnp.float32),
            pltpu.VMEM((groups, lats + 2 * REACH, wide_slot, LANES), jnp.float32),
            pltpu.VMEM((groups, lats, slot, LANES), jnp.float32),
            pltpu.VMEM((rows, LANES), jnp.float32),
        ],
        name="blocks",
    )(edges, *arrays)


def halo_of(x, seg):
    rows, segs = lax.axis_size("y"), lax.axis_size("xc")
    reach = 2 * REACH
    down = [(i, i + 1) for i in range(rows - 1)]
    up = [(j, i) for i, j in down]
    top = lax.ppermute(x[-reach:], "y", down)
    bottom = lax.ppermute(x[:reach], "y", up)
    east = [(i, (i + 1) % segs) for i in range(segs)]
    west = [(j, i) for i, j in east]

    def columns(lo):
        return jnp.concatenate(
            [part[:, lo : lo + reach] for part in (top, x, bottom)], axis=0
        )

    left = lax.ppermute(columns(seg - reach), "xc", east)
    right = lax.ppermute(columns(0), "xc", west)
    return top, bottom, left, right


def on_device(
    field, noise_level, conv_kernel, conv_bias, modulation,
    expand_weight, expand_bias, project_weight, project_bias, layer_scale,
):
    chans, members, lats, lons = field.shape
    layers = conv_kernel.shape[0]
    halves = lax.axis_size("zh")
    segs = lax.axis_size("xc")
    peers = halves * lax.axis_size("zl") * segs
    channels = chans * lax.axis_size("zl") * segs
    seg = lons // segs
    slot = -(-seg // 8) * 8
    tiles = lats * slot // LANES
    member = lax.axis_index("zh") * lax.axis_size("zl") + lax.axis_index("zl")
    mods = modulation[:, noise_level[member]].reshape(2 * layers, channels)
    band = lax.axis_index("y")
    edges = jnp.stack([band == 0, band == lax.axis_size("y") - 1]).astype(jnp.int32)

    pieces = run_cut(field, seg, slot)
    filters = jnp.concatenate(
        [conv_kernel.reshape(layers, chans, TAPS * TAPS), conv_bias[:, :, None]], axis=2
    )
    pieces, filters = lax.optimization_barrier((pieces, filters))
    shape = (peers, chans * tiles, LANES)
    around = ("zh", "zl", "xc")
    pieces = lax.all_to_all(pieces.reshape(shape), around, 0, 0, tiled=True).reshape(-1, LANES)

    filters = jnp.broadcast_to(filters.reshape(1, -1), (channels // chans, filters.size))
    filters = lax.all_to_all(filters, ("zl", "xc"), 0, 0, tiled=True)
    filters = filters.reshape(channels // chans, layers, chans, TAPS * TAPS + 1)
    filters = filters.transpose(1, 3, 0, 2).reshape(layers, TAPS * TAPS + 1, channels)

    x = run_to_cells(pieces, halves * lats * slot, channels, tiles)
    x = x.reshape(halves * lats, slot, channels)
    pieces = run_blocks(
        edges, x, halo_of(x, seg), filters, mods,
        expand_weight, expand_bias, project_weight, project_bias, layer_scale, tiles,
    )
    pieces = lax.all_to_all(pieces.reshape(shape), around, 0, 0, tiled=True).reshape(-1, LANES)
    return run_paste(pieces, field.shape, seg, slot)


def solution(mesh):
    bands, chan = mesh.shape["band"], mesh.shape["chan"]
    split = Mesh(mesh.devices.reshape(bands // 2, 2, chan // 8, 8), ("y", "zh", "zl", "xc"))
    band, group = ("y", "zh"), ("zl", "xc")
    return jax.shard_map(
        on_device,
        mesh=split,
        in_specs=(
            P(group, None, band, None),
            P(),
            P(None, group, None, None),
            P(None, group),
            P(), P(), P(), P(), P(), P(),
        ),
        out_specs=P(group, None, band, None),
        check_vma=False,
    )
```

```python
import jax
import jax.numpy as jnp
from jax import lax
from jax.experimental import pallas as pl
from jax.experimental.pallas import tpu as pltpu
from jax.sharding import Mesh, PartitionSpec as P

EPS = 1e-06
LANES = 128
TAPS = 7
REACH = 3
LEFT = 8
ROWS = 8


def lane_iota(rows):
    return lax.broadcasted_iota(jnp.int32, (rows, LANES), 1)


def moved_lanes(load, spans, rows, rolled):
    lanes = lane_iota(rows)
    tile = None
    for source, src, dst, width in spans:
        done = 0
        while done < width:
            part, lane = divmod(src + done, LANES)
            take = min(width - done, LANES - lane)
            shift = (dst + done - lane) % LANES
            key = (source, part, shift)
            if key not in rolled:
                value = load(source, part)
                rolled[key] = pltpu.roll(value, shift, 1) if shift else value
            value = rolled[key]
            tile = value if tile is None else jnp.where(lanes >= dst + done, value, tile)
            done += take
    return tile


def spans_of(count, stride, width, tile_index, start_of):
    spans = []
    for item in range(count):
        lo = max(item * stride, tile_index * LANES)
        hi = min(item * stride + width, (tile_index + 1) * LANES)
        if lo < hi:
            spans.append((item, start_of(item) + lo - item * stride, lo - tile_index * LANES, hi - lo))
    return spans


def cut_kernel(field_ref, out_ref, wide, cut, *, seg, slot):
    chans, members, lats, lons = field_ref.shape
    rows = chans * members
    parts = -(-lons // LANES)
    segs = lons // seg
    tiles = lats * slot // LANES
    for a in range(parts):
        lo, hi = a * LANES, min((a + 1) * LANES, lons)
        piece = field_ref[:, :, :, lo:hi].astype(jnp.float32).reshape(rows * lats, hi - lo)
        wide[a, :, 0 : hi - lo] = piece
        if hi - lo < LANES:
            wide[a, :, hi - lo :] = jnp.zeros((rows * lats, LANES - hi + lo), jnp.float32)
    for s in range(segs):
        rolled = {}
        for t in range(tiles):
            spans = spans_of(lats, slot, seg, t, lambda item: s * seg)

            def load(lat, part):
                return wide[part, pl.ds(lat, rows, stride=lats), :]

            tile = moved_lanes(load, spans, rows, rolled)
            for c in range(chans):
                start = s * chans * tiles + c * tiles + t
                cut[pl.ds(start, members, stride=segs * chans * tiles), :] = tile[
                    c * members : (c + 1) * members
                ]
    out_ref[...] = cut[...].astype(jnp.bfloat16)


def paste_kernel(in_ref, out_ref, cut, wide, *, seg, slot):
    chans, members, lats, lons = out_ref.shape
    rows = chans * members
    parts = -(-lons // LANES)
    segs = lons // seg
    tiles = lats * slot // LANES
    cut[...] = in_ref[...].astype(jnp.float32)
    for lat in range(lats):
        rolled = {}
        for a in range(parts):
            spans = spans_of(segs, seg, seg, a, lambda item: lat * slot)

            def load(s, part):
                return jnp.concatenate(
                    [
                        cut[
                            pl.ds(
                                s * chans * tiles + c * tiles + part,
                                members,
                                stride=segs * chans * tiles,
                            ),
                            :,
                        ]
                        for c in range(chans)
                    ],
                    axis=0,
                )

            wide[a, pl.ds(lat, rows, stride=lats), :] = moved_lanes(load, spans, rows, rolled)
    for a in range(parts):
        lo, hi = a * LANES, min((a + 1) * LANES, lons)
        out_ref[:, :, :, lo:hi] = (
            wide[a, :, 0 : hi - lo].reshape(chans, members, lats, hi - lo).astype(jnp.bfloat16)
        )


def to_cells_kernel(in_ref, out_ref, north_ref, south_ref, rows32, *, tiles):
    cells, channels = out_ref.shape
    halves = in_ref.shape[0] // (channels * tiles)
    rows32[...] = in_ref[...].astype(jnp.float32)
    for half in range(halves):
        for t in range(tiles):
            block = rows32[pl.ds(half * channels * tiles + t, channels, stride=tiles), :]
            start = (half * tiles + t) * LANES
            out_ref[start : start + LANES, :] = block.T.astype(jnp.bfloat16)
    edge = north_ref.shape[0]
    north_ref[...] = out_ref[0:edge, :]
    south_ref[...] = out_ref[cells - edge :, :]


def depthwise(source, spread, mixed, layer, lats, rows, col_tiles, first_col):
    groups = source.shape[0]
    steps = -(-lats // rows)
    for k in range(col_tiles):

        def step_of(step, carry):
            g = step // steps
            row = jnp.minimum((step % steps) * rows, lats - rows)
            sums = [spread[layer, g, TAPS * TAPS]] * rows
            for j in range(TAPS):
                col = first_col + 8 * k + j
                weights = [spread[layer, g, i * TAPS + j] for i in range(TAPS)]
                for r in range(rows + TAPS - 1):
                    value = source[g, row + r, col : col + 8, :]
                    for i in range(TAPS):
                        if 0 <= r - i < rows:
                            sums[r - i] = sums[r - i] + weights[i] * value
            for r in range(rows):
                mixed[g, row + r, 8 * k : 8 * k + 8, :] = sums[r]
            return carry

        lax.fori_loop(0, groups * steps, step_of, 0)


def pointwise(mixed, layer, lats, slot, residual, store, weights):
    mod_ref, up_ref, up_bias_ref, down_ref, down_bias_ref, scale_ref = weights
    groups = mixed.shape[0]
    channels = groups * LANES
    cells = ROWS * slot
    steps = -(-lats // ROWS)
    average_matrix = jnp.full((channels, channels), 1.0 / channels, jnp.bfloat16)

    def step_of(step, carry):
        row = jnp.minimum(step * ROWS, lats - ROWS)
        parts = [mixed[g, pl.ds(row, ROWS), 0:slot, :].reshape(cells, LANES) for g in range(groups)]
        rounded = jnp.concatenate(parts, axis=1).astype(jnp.bfloat16)
        average = jnp.dot(rounded, average_matrix, preferred_element_type=jnp.float32)
        centered = rounded.astype(jnp.float32) - average
        variance = jnp.dot(
            (centered * centered).astype(jnp.bfloat16),
            average_matrix,
            preferred_element_type=jnp.float32,
        )
        gain = 1.0 + mod_ref[2 * layer : 2 * layer + 1, :]
        shift = mod_ref[2 * layer + 1 : 2 * layer + 2, :]
        normed = (centered * lax.rsqrt(variance + EPS) * gain + shift).astype(jnp.bfloat16)
        hidden = (
            jnp.dot(normed, up_ref[layer], preferred_element_type=jnp.float32)
            + up_bias_ref[layer : layer + 1, :]
        )
        active = (0.5 * hidden * (1.0 + lax.erf(hidden * 0.7071067811865476))).astype(jnp.bfloat16)
        result = (
            jnp.dot(active, down_ref[layer], preferred_element_type=jnp.float32)
            + down_bias_ref[layer : layer + 1, :]
        )
        branch = (scale_ref[layer : layer + 1, :] * result).astype(jnp.bfloat16).astype(jnp.float32)
        for g in range(groups):
            part = branch[:, g * LANES : (g + 1) * LANES].reshape(ROWS, slot, LANES)
            store(g, row, (residual(g, row) + part).astype(jnp.bfloat16).astype(jnp.float32))
        return carry

    lax.fori_loop(0, steps, step_of, 0)


def blocks_kernel(
    edge_ref, x_ref, top_ref, bottom_ref, left_ref, right_ref, taps_ref, mod_ref,
    up_ref, up_bias_ref, down_ref, down_bias_ref, scale_ref,
    out_ref, first, second, spread, mixed, final, rows32, *, tiles,
):
    lats, slot, channels = x_ref.shape
    groups = channels // LANES
    reach = 2 * REACH
    wide = lats + reach
    right_at = LEFT + slot - REACH
    for g in range(groups):
        ch = slice(g * LANES, (g + 1) * LANES)
        first[g, 0:reach, LEFT : LEFT + slot, :] = top_ref[:, :, ch].astype(jnp.float32)
        first[g, reach : reach + lats, LEFT : LEFT + slot, :] = x_ref[:, :, ch].astype(jnp.float32)
        first[g, reach + lats :, LEFT : LEFT + slot, :] = bottom_ref[:, :, ch].astype(jnp.float32)
        first[g, :, LEFT + slot :, :] = jnp.zeros(
            (lats + 2 * reach, first.shape[2] - LEFT - slot, LANES), jnp.float32
        )
        first[g, :, LEFT - reach : LEFT, :] = left_ref[:, :, ch].astype(jnp.float32)
        first[g, :, right_at : right_at + reach, :] = right_ref[:, :, ch].astype(jnp.float32)
        for layer in range(taps_ref.shape[0]):
            for k in range(TAPS * TAPS + 1):
                spread[layer, g, k] = jnp.broadcast_to(taps_ref[layer, k : k + 1, ch], (8, LANES))
    weights = (mod_ref, up_ref, up_bias_ref, down_ref, down_bias_ref, scale_ref)

    wide_slot = slot + 8
    depthwise(first, spread, mixed, 0, wide, 13, wide_slot // 8, LEFT - reach)

    def first_store(g, row, value):
        second[g, pl.ds(row, ROWS), :, :] = value

    pointwise(
        mixed, 0, wide, wide_slot,
        lambda g, row: first[g, pl.ds(row + REACH, ROWS), LEFT - REACH : LEFT - REACH + wide_slot, :],
        first_store, weights,
    )

    @pl.when(edge_ref[0] == 1)
    def _():
        second[:, 0:REACH, :, :] = jnp.zeros((groups, REACH, wide_slot, LANES), jnp.float32)

    @pl.when(edge_ref[1] == 1)
    def _():
        second[:, REACH + lats :, :, :] = jnp.zeros((groups, REACH, wide_slot, LANES), jnp.float32)

    depthwise(second, spread, mixed, 1, lats, 16, slot // 8, 0)

    def final_store(g, row, value):
        final[g, pl.ds(row, ROWS), :, :] = value

    pointwise(
        mixed, 1, lats, slot,
        lambda g, row: second[g, pl.ds(row + REACH, ROWS), REACH : REACH + slot, :],
        final_store, weights,
    )
    flat = lats * slot // tiles // LANES
    rows_per = LANES * 3 // slot
    for half in range(flat):
        for g in range(groups):
            for part in range(tiles // 3):
                lat = (half * tiles + part * 3) * LANES // slot
                block = final[g, lat : lat + rows_per, :, :].reshape(rows_per * slot, LANES)
                for t in range(3):
                    start = half * channels * tiles + g * LANES * tiles + part * 3 + t
                    rows32[pl.ds(start, LANES, stride=tiles), :] = block[
                        t * LANES : (t + 1) * LANES
                    ].T
    out_ref[...] = rows32[...].astype(jnp.bfloat16)


def run_cut(field, seg, slot):
    chans, members, lats, lons = field.shape
    tiles = lats * slot // LANES
    rows = members * (lons // seg) * chans * tiles
    return pl.pallas_call(
        lambda *refs: cut_kernel(*refs, seg=seg, slot=slot),
        out_shape=jax.ShapeDtypeStruct((rows, LANES), jnp.bfloat16),
        scratch_shapes=[
            pltpu.VMEM((-(-lons // LANES), chans * members * lats, LANES), jnp.float32),
            pltpu.VMEM((rows, LANES), jnp.float32),
        ],
        name="cut",
    )(field)


def run_paste(pieces, shape, seg, slot):
    chans, members, lats, lons = shape
    return pl.pallas_call(
        lambda *refs: paste_kernel(*refs, seg=seg, slot=slot),
        out_shape=jax.ShapeDtypeStruct(shape, jnp.bfloat16),
        scratch_shapes=[
            pltpu.VMEM(pieces.shape, jnp.float32),
            pltpu.VMEM((-(-lons // LANES), chans * members * lats, LANES), jnp.float32),
        ],
        name="paste",
    )(pieces)


def run_to_cells(pieces, cells, channels, tiles, edge):
    outs = [(cells, channels), (edge, channels), (edge, channels)]
    return pl.pallas_call(
        lambda *refs: to_cells_kernel(*refs, tiles=tiles),
        out_shape=[jax.ShapeDtypeStruct(out, jnp.bfloat16) for out in outs],
        scratch_shapes=[pltpu.VMEM(pieces.shape, jnp.float32)],
        name="to_cells",
    )(pieces)


def run_blocks(edges, x, halos, taps, mods, up, up_bias, down, down_bias, scale, tiles):
    lats, slot, channels = x.shape
    groups = channels // LANES
    rows = lats * slot * channels // LANES
    vmem = pl.BlockSpec(memory_space=pltpu.VMEM)
    arrays = (x, *halos, taps, mods, up, up_bias, down, down_bias, scale)
    wide_slot = slot + 8
    return pl.pallas_call(
        lambda *refs: blocks_kernel(*refs, tiles=tiles),
        out_shape=jax.ShapeDtypeStruct((rows, LANES), jnp.bfloat16),
        in_specs=[pl.BlockSpec(memory_space=pltpu.SMEM)] + [vmem] * len(arrays),
        scratch_shapes=[
            pltpu.VMEM((groups, lats + 4 * REACH, LEFT + wide_slot, LANES), jnp.float32),
            pltpu.VMEM((groups, lats + 2 * REACH, wide_slot, LANES), jnp.float32),
            pltpu.VMEM((taps.shape[0], groups, TAPS * TAPS + 1, 8, LANES), jnp.float32),
            pltpu.VMEM((groups, lats + 2 * REACH, wide_slot, LANES), jnp.float32),
            pltpu.VMEM((groups, lats, slot, LANES), jnp.float32),
            pltpu.VMEM((rows, LANES), jnp.float32),
        ],
        name="blocks",
    )(edges, *arrays)


def halo_of(x, north, south, seg):
    rows, segs = lax.axis_size("y"), lax.axis_size("xc")
    reach = 2 * REACH
    down = [(i, i + 1) for i in range(rows - 1)]
    up = [(j, i) for i, j in down]
    top = lax.ppermute(south, "y", down)
    bottom = lax.ppermute(north, "y", up)
    east = [(i, (i + 1) % segs) for i in range(segs)]
    west = [(j, i) for i, j in east]

    def columns(lo):
        return jnp.concatenate(
            [part[:, lo : lo + reach] for part in (top, x, bottom)], axis=0
        )

    left = lax.ppermute(columns(seg - reach), "xc", east)
    right = lax.ppermute(columns(0), "xc", west)
    return top, bottom, left, right


def gathered(row, axis):
    copies = jnp.broadcast_to(row, (lax.axis_size(axis), row.shape[1]))
    return lax.all_to_all(copies, axis, 0, 0, tiled=True)


def on_device(
    field, noise_level, conv_kernel, conv_bias, modulation,
    expand_weight, expand_bias, project_weight, project_bias, layer_scale,
):
    chans, members, lats, lons = field.shape
    layers = conv_kernel.shape[0]
    halves = lax.axis_size("zh")
    segs = lax.axis_size("xc")
    peers = halves * lax.axis_size("zl") * segs
    channels = chans * lax.axis_size("zl") * segs
    seg = lons // segs
    slot = -(-seg // 8) * 8
    tiles = lats * slot // LANES
    member = lax.axis_index("zh") * lax.axis_size("zl") + lax.axis_index("zl")
    mods = modulation[:, noise_level[member]].reshape(2 * layers, channels)
    band = lax.axis_index("y")
    edges = jnp.stack([band == 0, band == lax.axis_size("y") - 1]).astype(jnp.int32)

    filters = jnp.concatenate(
        [conv_kernel.reshape(layers, chans, TAPS * TAPS), conv_bias[:, :, None]], axis=2
    )
    filters = gathered(filters.reshape(1, -1), "xc")
    pieces = run_cut(field, seg, slot)
    shape = (peers, chans * tiles, LANES)
    around = ("zh", "zl", "xc")
    pieces = lax.all_to_all(pieces.reshape(shape), around, 0, 0, tiled=True).reshape(-1, LANES)
    pieces, filters = lax.optimization_barrier((pieces, filters))
    filters = gathered(filters.reshape(1, -1), "zl")
    filters = filters.reshape(channels // chans, layers, chans, TAPS * TAPS + 1)
    filters = filters.transpose(1, 3, 0, 2).reshape(layers, TAPS * TAPS + 1, channels)

    cells = run_to_cells(pieces, halves * lats * slot, channels, tiles, 2 * REACH * slot)
    x, north, south = [part.reshape(-1, slot, channels) for part in cells]
    pieces = run_blocks(
        edges, x, halo_of(x, north, south, seg), filters, mods,
        expand_weight, expand_bias, project_weight, project_bias, layer_scale, tiles,
    )
    pieces = lax.all_to_all(pieces.reshape(shape), around, 0, 0, tiled=True).reshape(-1, LANES)
    return run_paste(pieces, field.shape, seg, slot)


def solution(mesh):
    bands, chan = mesh.shape["band"], mesh.shape["chan"]
    split = Mesh(mesh.devices.reshape(bands // 2, 2, chan // 8, 8), ("y", "zh", "zl", "xc"))
    band, group = ("y", "zh"), ("zl", "xc")
    return jax.shard_map(
        on_device,
        mesh=split,
        in_specs=(
            P(group, None, band, None),
            P(),
            P(None, group, None, None),
            P(None, group),
            P(), P(), P(), P(), P(), P(),
        ),
        out_specs=P(group, None, band, None),
        check_vma=False,
    )
```

```python
import jax
import jax.numpy as jnp
from jax import lax
from jax.experimental import pallas as pl
from jax.experimental.pallas import tpu as pltpu
from jax.sharding import Mesh, PartitionSpec as P

EPS = 1e-06
LANES = 128
TAPS = 7
REACH = 3
LEFT = 8
ROWS = 8


def lane_iota(rows):
    return lax.broadcasted_iota(jnp.int32, (rows, LANES), 1)


def moved_lanes(load, spans, rows, rolled):
    lanes = lane_iota(rows)
    tile = None
    for source, src, dst, width in spans:
        done = 0
        while done < width:
            part, lane = divmod(src + done, LANES)
            take = min(width - done, LANES - lane)
            shift = (dst + done - lane) % LANES
            key = (source, part, shift)
            if key not in rolled:
                value = load(source, part)
                rolled[key] = pltpu.roll(value, shift, 1) if shift else value
            value = rolled[key]
            tile = value if tile is None else jnp.where(lanes >= dst + done, value, tile)
            done += take
    return tile


def spans_of(count, stride, width, tile_index, start_of):
    spans = []
    for item in range(count):
        lo = max(item * stride, tile_index * LANES)
        hi = min(item * stride + width, (tile_index + 1) * LANES)
        if lo < hi:
            spans.append((item, start_of(item) + lo - item * stride, lo - tile_index * LANES, hi - lo))
    return spans


def cut_kernel(field_ref, out_ref, wide, cut, *, seg, slot):
    chans, members, lats, lons = field_ref.shape
    rows = chans * members
    parts = -(-lons // LANES)
    segs = lons // seg
    tiles = lats * slot // LANES
    for a in range(parts):
        lo, hi = a * LANES, min((a + 1) * LANES, lons)
        piece = field_ref[:, :, :, lo:hi].astype(jnp.float32).reshape(rows * lats, hi - lo)
        wide[a, :, 0 : hi - lo] = piece
        if hi - lo < LANES:
            wide[a, :, hi - lo :] = jnp.zeros((rows * lats, LANES - hi + lo), jnp.float32)
    for s in range(segs):
        rolled = {}
        for t in range(tiles):
            spans = spans_of(lats, slot, seg, t, lambda item: s * seg)

            def load(lat, part):
                return wide[part, pl.ds(lat, rows, stride=lats), :]

            tile = moved_lanes(load, spans, rows, rolled)
            for c in range(chans):
                start = s * chans * tiles + c * tiles + t
                cut[pl.ds(start, members, stride=segs * chans * tiles), :] = tile[
                    c * members : (c + 1) * members
                ]
    out_ref[...] = cut[...].astype(jnp.bfloat16)


def paste_kernel(in_ref, out_ref, cut, wide, *, seg, slot):
    chans, members, lats, lons = out_ref.shape
    rows = chans * members
    parts = -(-lons // LANES)
    segs = lons // seg
    tiles = lats * slot // LANES
    cut[...] = in_ref[...].astype(jnp.float32)
    for lat in range(lats):
        rolled = {}
        for a in range(parts):
            spans = spans_of(segs, seg, seg, a, lambda item: lat * slot)

            def load(s, part):
                return jnp.concatenate(
                    [
                        cut[
                            pl.ds(
                                s * chans * tiles + c * tiles + part,
                                members,
                                stride=segs * chans * tiles,
                            ),
                            :,
                        ]
                        for c in range(chans)
                    ],
                    axis=0,
                )

            wide[a, pl.ds(lat, rows, stride=lats), :] = moved_lanes(load, spans, rows, rolled)
    for a in range(parts):
        lo, hi = a * LANES, min((a + 1) * LANES, lons)
        out_ref[:, :, :, lo:hi] = (
            wide[a, :, 0 : hi - lo].reshape(chans, members, lats, hi - lo).astype(jnp.bfloat16)
        )


def to_cells_kernel(in_ref, out_ref, north_ref, south_ref, rows32, *, tiles):
    cells, channels = out_ref.shape
    halves = in_ref.shape[0] // (channels * tiles)
    rows32[...] = in_ref[...].astype(jnp.float32)
    for half in range(halves):
        for t in range(tiles):
            block = rows32[pl.ds(half * channels * tiles + t, channels, stride=tiles), :]
            start = (half * tiles + t) * LANES
            out_ref[start : start + LANES, :] = block.T.astype(jnp.bfloat16)
    edge = north_ref.shape[0]
    north_ref[...] = out_ref[0:edge, :]
    south_ref[...] = out_ref[cells - edge :, :]


def depthwise(source, spread, mixed, layer, lats, rows, col_tiles, first_col):
    groups = source.shape[0]
    steps = -(-lats // rows)
    for k in range(col_tiles):

        def step_of(step, carry):
            g = step // steps
            row = jnp.minimum((step % steps) * rows, lats - rows)
            def column_of(j, sums):
                sums = list(sums)
                weights = [spread[layer, g, i * TAPS + j] for i in range(TAPS)]
                for r in range(rows + TAPS - 1):
                    value = source[g, row + r, pl.ds(first_col + 8 * k + j, 8), :]
                    for i in range(TAPS):
                        if 0 <= r - i < rows:
                            sums[r - i] = sums[r - i] + weights[i] * value
                return tuple(sums)

            start = (spread[layer, g, TAPS * TAPS],) * rows
            sums = lax.fori_loop(0, TAPS, column_of, start)
            for r in range(rows):
                mixed[g, row + r, 8 * k : 8 * k + 8, :] = sums[r]
            return carry

        lax.fori_loop(0, groups * steps, step_of, 0)


def pointwise(mixed, layer, lats, slot, residual, store, weights):
    mod_ref, up_ref, up_bias_ref, down_ref, down_bias_ref, scale_ref = weights
    groups = mixed.shape[0]
    channels = groups * LANES
    cells = ROWS * slot
    steps = -(-lats // ROWS)
    average_matrix = jnp.full((channels, channels), 1.0 / channels, jnp.bfloat16)

    def step_of(step, carry):
        row = jnp.minimum(step * ROWS, lats - ROWS)
        parts = [mixed[g, pl.ds(row, ROWS), 0:slot, :].reshape(cells, LANES) for g in range(groups)]
        rounded = jnp.concatenate(parts, axis=1).astype(jnp.bfloat16)
        average = jnp.dot(rounded, average_matrix, preferred_element_type=jnp.float32)
        centered = rounded.astype(jnp.float32) - average
        variance = jnp.dot(
            (centered * centered).astype(jnp.bfloat16),
            average_matrix,
            preferred_element_type=jnp.float32,
        )
        gain = 1.0 + mod_ref[2 * layer : 2 * layer + 1, :]
        shift = mod_ref[2 * layer + 1 : 2 * layer + 2, :]
        normed = (centered * lax.rsqrt(variance + EPS) * gain + shift).astype(jnp.bfloat16)
        hidden = (
            jnp.dot(normed, up_ref[layer], preferred_element_type=jnp.float32)
            + up_bias_ref[layer : layer + 1, :]
        )
        active = (0.5 * hidden * (1.0 + lax.erf(hidden * 0.7071067811865476))).astype(jnp.bfloat16)
        result = (
            jnp.dot(active, down_ref[layer], preferred_element_type=jnp.float32)
            + down_bias_ref[layer : layer + 1, :]
        )
        branch = (scale_ref[layer : layer + 1, :] * result).astype(jnp.bfloat16).astype(jnp.float32)
        for g in range(groups):
            part = branch[:, g * LANES : (g + 1) * LANES].reshape(ROWS, slot, LANES)
            store(g, row, (residual(g, row) + part).astype(jnp.bfloat16).astype(jnp.float32))
        return carry

    lax.fori_loop(0, steps, step_of, 0)


def blocks_kernel(
    edge_ref, x_ref, top_ref, bottom_ref, left_ref, right_ref, taps_ref, mod_ref,
    up_ref, up_bias_ref, down_ref, down_bias_ref, scale_ref,
    out_ref, first, second, spread, mixed, final, rows32, *, tiles,
):
    lats, slot, channels = x_ref.shape
    groups = channels // LANES
    reach = 2 * REACH
    wide = lats + reach
    right_at = LEFT + slot - REACH
    for g in range(groups):
        ch = slice(g * LANES, (g + 1) * LANES)
        first[g, 0:reach, LEFT : LEFT + slot, :] = top_ref[:, :, ch].astype(jnp.float32)
        first[g, reach : reach + lats, LEFT : LEFT + slot, :] = x_ref[:, :, ch].astype(jnp.float32)
        first[g, reach + lats :, LEFT : LEFT + slot, :] = bottom_ref[:, :, ch].astype(jnp.float32)
        first[g, :, LEFT + slot :, :] = jnp.zeros(
            (lats + 2 * reach, first.shape[2] - LEFT - slot, LANES), jnp.float32
        )
        first[g, :, LEFT - reach : LEFT, :] = left_ref[:, :, ch].astype(jnp.float32)
        first[g, :, right_at : right_at + reach, :] = right_ref[:, :, ch].astype(jnp.float32)
        for layer in range(taps_ref.shape[0]):
            for k in range(TAPS * TAPS + 1):
                spread[layer, g, k] = jnp.broadcast_to(taps_ref[layer, k : k + 1, ch], (8, LANES))
    weights = (mod_ref, up_ref, up_bias_ref, down_ref, down_bias_ref, scale_ref)

    wide_slot = slot + 8
    depthwise(first, spread, mixed, 0, wide, 19, wide_slot // 8, LEFT - reach)

    def first_store(g, row, value):
        second[g, pl.ds(row, ROWS), :, :] = value

    pointwise(
        mixed, 0, wide, wide_slot,
        lambda g, row: first[g, pl.ds(row + REACH, ROWS), LEFT - REACH : LEFT - REACH + wide_slot, :],
        first_store, weights,
    )

    @pl.when(edge_ref[0] == 1)
    def _():
        second[:, 0:REACH, :, :] = jnp.zeros((groups, REACH, wide_slot, LANES), jnp.float32)

    @pl.when(edge_ref[1] == 1)
    def _():
        second[:, REACH + lats :, :, :] = jnp.zeros((groups, REACH, wide_slot, LANES), jnp.float32)

    depthwise(second, spread, mixed, 1, lats, 32, slot // 8, 0)

    def final_store(g, row, value):
        final[g, pl.ds(row, ROWS), :, :] = value

    pointwise(
        mixed, 1, lats, slot,
        lambda g, row: second[g, pl.ds(row + REACH, ROWS), REACH : REACH + slot, :],
        final_store, weights,
    )
    flat = lats * slot // tiles // LANES
    rows_per = LANES * 3 // slot
    for half in range(flat):
        for g in range(groups):
            for part in range(tiles // 3):
                lat = (half * tiles + part * 3) * LANES // slot
                block = final[g, lat : lat + rows_per, :, :].reshape(rows_per * slot, LANES)
                for t in range(3):
                    start = half * channels * tiles + g * LANES * tiles + part * 3 + t
                    rows32[pl.ds(start, LANES, stride=tiles), :] = block[
                        t * LANES : (t + 1) * LANES
                    ].T
    out_ref[...] = rows32[...].astype(jnp.bfloat16)


def near(x):
    return pltpu.with_memory_space_constraint(x, pltpu.VMEM)


def run_cut(field, seg, slot):
    chans, members, lats, lons = field.shape
    tiles = lats * slot // LANES
    rows = members * (lons // seg) * chans * tiles
    return pl.pallas_call(
        lambda *refs: cut_kernel(*refs, seg=seg, slot=slot),
        out_shape=pltpu.VMEM((rows, LANES), jnp.bfloat16),
        scratch_shapes=[
            pltpu.VMEM((-(-lons // LANES), chans * members * lats, LANES), jnp.float32),
            pltpu.VMEM((rows, LANES), jnp.float32),
        ],
        name="cut",
    )(field)


def run_paste(pieces, shape, seg, slot):
    chans, members, lats, lons = shape
    return pl.pallas_call(
        lambda *refs: paste_kernel(*refs, seg=seg, slot=slot),
        out_shape=jax.ShapeDtypeStruct(shape, jnp.bfloat16),
        scratch_shapes=[
            pltpu.VMEM(pieces.shape, jnp.float32),
            pltpu.VMEM((-(-lons // LANES), chans * members * lats, LANES), jnp.float32),
        ],
        name="paste",
    )(near(pieces))


def run_to_cells(pieces, cells, channels, tiles, edge):
    outs = [(cells, channels), (edge, channels), (edge, channels)]
    return pl.pallas_call(
        lambda *refs: to_cells_kernel(*refs, tiles=tiles),
        out_shape=[pltpu.VMEM(out, jnp.bfloat16) for out in outs],
        scratch_shapes=[pltpu.VMEM(pieces.shape, jnp.float32)],
        name="to_cells",
    )(near(pieces))


def run_blocks(edges, x, halos, taps, mods, up, up_bias, down, down_bias, scale, tiles):
    lats, slot, channels = x.shape
    groups = channels // LANES
    rows = lats * slot * channels // LANES
    vmem = pl.BlockSpec(memory_space=pltpu.VMEM)
    arrays = (x, *halos, taps, mods, up, up_bias, down, down_bias, scale)
    wide_slot = slot + 8
    return pl.pallas_call(
        lambda *refs: blocks_kernel(*refs, tiles=tiles),
        out_shape=pltpu.VMEM((rows, LANES), jnp.bfloat16),
        in_specs=[pl.BlockSpec(memory_space=pltpu.SMEM)] + [vmem] * len(arrays),
        scratch_shapes=[
            pltpu.VMEM((groups, lats + 4 * REACH, LEFT + wide_slot, LANES), jnp.float32),
            pltpu.VMEM((groups, lats + 2 * REACH, wide_slot, LANES), jnp.float32),
            pltpu.VMEM((taps.shape[0], groups, TAPS * TAPS + 1, 8, LANES), jnp.float32),
            pltpu.VMEM((groups, lats + 2 * REACH, wide_slot, LANES), jnp.float32),
            pltpu.VMEM((groups, lats, slot, LANES), jnp.float32),
            pltpu.VMEM((rows, LANES), jnp.float32),
        ],
        compiler_params=pltpu.CompilerParams(vmem_limit_bytes=40 * 2**20),
        name="blocks",
    )(edges, *[near(a) for a in arrays])


def halo_of(x, north, south, seg):
    rows, segs = lax.axis_size("y"), lax.axis_size("xc")
    reach = 2 * REACH
    down = [(i, i + 1) for i in range(rows - 1)]
    up = [(j, i) for i, j in down]
    top = lax.ppermute(south, "y", down)
    bottom = lax.ppermute(north, "y", up)
    east = [(i, (i + 1) % segs) for i in range(segs)]
    west = [(j, i) for i, j in east]

    def columns(lo):
        return jnp.concatenate(
            [part[:, lo : lo + reach] for part in (top, x, bottom)], axis=0
        )

    left = lax.ppermute(columns(seg - reach), "xc", east)
    right = lax.ppermute(columns(0), "xc", west)
    return top, bottom, left, right


def on_device(
    field, noise_level, conv_kernel, conv_bias, modulation,
    expand_weight, expand_bias, project_weight, project_bias, layer_scale,
):
    chans, members, lats, lons = field.shape
    layers = conv_kernel.shape[0]
    halves = lax.axis_size("zh")
    segs = lax.axis_size("xc")
    peers = halves * lax.axis_size("zl") * segs
    channels = chans * lax.axis_size("zl") * segs
    seg = lons // segs
    slot = -(-seg // 8) * 8
    tiles = lats * slot // LANES
    member = lax.axis_index("zh") * lax.axis_size("zl") + lax.axis_index("zl")
    mods = modulation[:, noise_level[member]].reshape(2 * layers, channels)
    band = lax.axis_index("y")
    edges = jnp.stack([band == 0, band == lax.axis_size("y") - 1]).astype(jnp.int32)

    filters = jnp.concatenate(
        [conv_kernel.reshape(layers, chans, TAPS * TAPS), conv_bias[:, :, None]], axis=2
    )
    pieces = run_cut(field, seg, slot)
    pieces, filters = lax.optimization_barrier((pieces, filters))
    shape = (peers, chans * tiles, LANES)
    around = ("zh", "zl", "xc")
    pieces = lax.all_to_all(pieces.reshape(shape), around, 0, 0, tiled=True).reshape(-1, LANES)
    filters = jnp.broadcast_to(filters.reshape(1, -1), (channels // chans, filters.size))
    filters = lax.all_to_all(filters, ("zl", "xc"), 0, 0, tiled=True)
    filters = filters.reshape(channels // chans, layers, chans, TAPS * TAPS + 1)
    filters = filters.transpose(1, 3, 0, 2).reshape(layers, TAPS * TAPS + 1, channels)

    cells = run_to_cells(pieces, halves * lats * slot, channels, tiles, 2 * REACH * slot)
    x, north, south = [part.reshape(-1, slot, channels) for part in cells]
    pieces = run_blocks(
        edges, x, halo_of(x, north, south, seg), filters, mods,
        expand_weight, expand_bias, project_weight, project_bias, layer_scale, tiles,
    )
    pieces = lax.all_to_all(pieces.reshape(shape), around, 0, 0, tiled=True).reshape(-1, LANES)
    return run_paste(pieces, field.shape, seg, slot)


def solution(mesh):
    bands, chan = mesh.shape["band"], mesh.shape["chan"]
    split = Mesh(mesh.devices.reshape(bands // 2, 2, chan // 8, 8), ("y", "zh", "zl", "xc"))
    band, group = ("y", "zh"), ("zl", "xc")
    return jax.shard_map(
        on_device,
        mesh=split,
        in_specs=(
            P(group, None, band, None),
            P(),
            P(None, group, None, None),
            P(None, group),
            P(), P(), P(), P(), P(), P(),
        ),
        out_specs=P(group, None, band, None),
        check_vma=False,
    )
```

```python
import jax
import jax.numpy as jnp
from jax import lax
from jax.experimental import pallas as pl
from jax.experimental.pallas import tpu as pltpu
from jax.sharding import Mesh, PartitionSpec as P

EPS = 1e-06
LANES = 128
TAPS = 7
REACH = 3
LEFT = 8
ROWS = 8


def lane_iota(rows):
    return lax.broadcasted_iota(jnp.int32, (rows, LANES), 1)


def moved_lanes(load, spans, rows, rolled):
    lanes = lane_iota(rows)
    tile = None
    for source, src, dst, width in spans:
        done = 0
        while done < width:
            part, lane = divmod(src + done, LANES)
            take = min(width - done, LANES - lane)
            shift = (dst + done - lane) % LANES
            key = (source, part, shift)
            if key not in rolled:
                value = load(source, part)
                rolled[key] = pltpu.roll(value, shift, 1) if shift else value
            value = rolled[key]
            tile = value if tile is None else jnp.where(lanes >= dst + done, value, tile)
            done += take
    return tile


def spans_of(count, stride, width, tile_index, start_of):
    spans = []
    for item in range(count):
        lo = max(item * stride, tile_index * LANES)
        hi = min(item * stride + width, (tile_index + 1) * LANES)
        if lo < hi:
            spans.append((item, start_of(item) + lo - item * stride, lo - tile_index * LANES, hi - lo))
    return spans


def cut_kernel(field_ref, out_ref, wide, cut, *, seg, slot):
    chans, members, lats, lons = field_ref.shape
    rows = chans * members
    parts = -(-lons // LANES)
    segs = lons // seg
    tiles = lats * slot // LANES
    for a in range(parts):
        lo, hi = a * LANES, min((a + 1) * LANES, lons)
        piece = field_ref[:, :, :, lo:hi].astype(jnp.float32).reshape(rows * lats, hi - lo)
        wide[a, :, 0 : hi - lo] = piece
        if hi - lo < LANES:
            wide[a, :, hi - lo :] = jnp.zeros((rows * lats, LANES - hi + lo), jnp.float32)
    for s in range(segs):
        rolled = {}
        for t in range(tiles):
            spans = spans_of(lats, slot, seg, t, lambda item: s * seg)

            def load(lat, part):
                return wide[part, pl.ds(lat, rows, stride=lats), :]

            tile = moved_lanes(load, spans, rows, rolled)
            for c in range(chans):
                start = s * chans * tiles + c * tiles + t
                cut[pl.ds(start, members, stride=segs * chans * tiles), :] = tile[
                    c * members : (c + 1) * members
                ]
    out_ref[...] = cut[...].astype(jnp.bfloat16)


def paste_kernel(in_ref, out_ref, cut, wide, *, seg, slot):
    chans, members, lats, lons = out_ref.shape
    rows = chans * members
    parts = -(-lons // LANES)
    segs = lons // seg
    tiles = lats * slot // LANES
    cut[...] = in_ref[...].astype(jnp.float32)
    for lat in range(lats):
        rolled = {}
        for a in range(parts):
            spans = spans_of(segs, seg, seg, a, lambda item: lat * slot)

            def load(s, part):
                return jnp.concatenate(
                    [
                        cut[
                            pl.ds(
                                s * chans * tiles + c * tiles + part,
                                members,
                                stride=segs * chans * tiles,
                            ),
                            :,
                        ]
                        for c in range(chans)
                    ],
                    axis=0,
                )

            wide[a, pl.ds(lat, rows, stride=lats), :] = moved_lanes(load, spans, rows, rolled)
    for a in range(parts):
        lo, hi = a * LANES, min((a + 1) * LANES, lons)
        out_ref[:, :, :, lo:hi] = (
            wide[a, :, 0 : hi - lo].reshape(chans, members, lats, hi - lo).astype(jnp.bfloat16)
        )


def to_cells_kernel(in_ref, out_ref, north_ref, south_ref, rows32, *, tiles):
    cells, channels = out_ref.shape
    halves = in_ref.shape[0] // (channels * tiles)
    rows32[...] = in_ref[...].astype(jnp.float32)
    for half in range(halves):
        for t in range(tiles):
            block = rows32[pl.ds(half * channels * tiles + t, channels, stride=tiles), :]
            start = (half * tiles + t) * LANES
            out_ref[start : start + LANES, :] = block.T.astype(jnp.bfloat16)
    edge = north_ref.shape[0]
    north_ref[...] = out_ref[0:edge, :]
    south_ref[...] = out_ref[cells - edge :, :]


def depthwise(source, spread, mixed, layer, lats, rows, col_tiles, first_col):
    groups = source.shape[0]
    steps = -(-lats // rows)
    for k in range(col_tiles):

        def step_of(step, carry):
            g = step // steps
            row = jnp.minimum((step % steps) * rows, lats - rows)
            def column_of(j, sums):
                sums = list(sums)
                weights = [spread[layer, g, i * TAPS + j] for i in range(TAPS)]
                for r in range(rows + TAPS - 1):
                    value = source[g, row + r, pl.ds(first_col + 8 * k + j, 8), :]
                    for i in range(TAPS):
                        if 0 <= r - i < rows:
                            sums[r - i] = sums[r - i] + weights[i] * value
                return tuple(sums)

            start = (spread[layer, g, TAPS * TAPS],) * rows
            sums = lax.fori_loop(0, TAPS, column_of, start)
            for r in range(rows):
                mixed[g, row + r, 8 * k : 8 * k + 8, :] = sums[r]
            return carry

        lax.fori_loop(0, groups * steps, step_of, 0)


def pointwise(mixed, layer, lats, slot, residual, store, weights):
    mod_ref, up_ref, up_bias_ref, down_ref, down_bias_ref, scale_ref = weights
    groups = mixed.shape[0]
    channels = groups * LANES
    cells = ROWS * slot
    steps = -(-lats // ROWS)
    average_matrix = jnp.full((channels, channels), 1.0 / channels, jnp.bfloat16)

    def step_of(step, carry):
        row = jnp.minimum(step * ROWS, lats - ROWS)
        parts = [mixed[g, pl.ds(row, ROWS), 0:slot, :].reshape(cells, LANES) for g in range(groups)]
        rounded = jnp.concatenate(parts, axis=1).astype(jnp.bfloat16)
        average = jnp.dot(rounded, average_matrix, preferred_element_type=jnp.float32)
        centered = rounded.astype(jnp.float32) - average
        variance = jnp.dot(
            (centered * centered).astype(jnp.bfloat16),
            average_matrix,
            preferred_element_type=jnp.float32,
        )
        gain = 1.0 + mod_ref[2 * layer : 2 * layer + 1, :]
        shift = mod_ref[2 * layer + 1 : 2 * layer + 2, :]
        normed = (centered * lax.rsqrt(variance + EPS) * gain + shift).astype(jnp.bfloat16)
        hidden = (
            jnp.dot(normed, up_ref[layer], preferred_element_type=jnp.float32)
            + up_bias_ref[layer : layer + 1, :]
        )
        doubled = (hidden * (1.0 + lax.erf(hidden * 0.7071067811865476))).astype(jnp.bfloat16)
        result = (
            0.5 * jnp.dot(doubled, down_ref[layer], preferred_element_type=jnp.float32)
            + down_bias_ref[layer : layer + 1, :]
        )
        branch = (scale_ref[layer : layer + 1, :] * result).astype(jnp.bfloat16).astype(jnp.float32)
        for g in range(groups):
            part = branch[:, g * LANES : (g + 1) * LANES].reshape(ROWS, slot, LANES)
            store(g, row, (residual(g, row) + part).astype(jnp.bfloat16).astype(jnp.float32))
        return carry

    lax.fori_loop(0, steps, step_of, 0)


def blocks_kernel(
    edge_ref, x_ref, top_ref, bottom_ref, left_ref, right_ref, taps_ref, mod_ref,
    up_ref, up_bias_ref, down_ref, down_bias_ref, scale_ref,
    out_ref, first, second, spread, mixed, final, rows32, *, tiles,
):
    lats, slot, channels = x_ref.shape
    groups = channels // LANES
    reach = 2 * REACH
    wide = lats + reach
    right_at = LEFT + slot - REACH
    for g in range(groups):
        ch = slice(g * LANES, (g + 1) * LANES)
        first[g, 0:reach, LEFT : LEFT + slot, :] = top_ref[:, :, ch].astype(jnp.float32)
        first[g, reach : reach + lats, LEFT : LEFT + slot, :] = x_ref[:, :, ch].astype(jnp.float32)
        first[g, reach + lats :, LEFT : LEFT + slot, :] = bottom_ref[:, :, ch].astype(jnp.float32)
        first[g, :, LEFT + slot :, :] = jnp.zeros(
            (lats + 2 * reach, first.shape[2] - LEFT - slot, LANES), jnp.float32
        )
        first[g, :, LEFT - reach : LEFT, :] = left_ref[:, :, ch].astype(jnp.float32)
        first[g, :, right_at : right_at + reach, :] = right_ref[:, :, ch].astype(jnp.float32)
        for layer in range(taps_ref.shape[0]):
            for k in range(TAPS * TAPS + 1):
                spread[layer, g, k] = jnp.broadcast_to(taps_ref[layer, k : k + 1, ch], (8, LANES))
    weights = (mod_ref, up_ref, up_bias_ref, down_ref, down_bias_ref, scale_ref)

    wide_slot = slot + 8
    depthwise(first, spread, mixed, 0, wide, 19, wide_slot // 8, LEFT - reach)

    def first_store(g, row, value):
        second[g, pl.ds(row, ROWS), :, :] = value

    pointwise(
        mixed, 0, wide, wide_slot,
        lambda g, row: first[g, pl.ds(row + REACH, ROWS), LEFT - REACH : LEFT - REACH + wide_slot, :],
        first_store, weights,
    )

    @pl.when(edge_ref[0] == 1)
    def _():
        second[:, 0:REACH, :, :] = jnp.zeros((groups, REACH, wide_slot, LANES), jnp.float32)

    @pl.when(edge_ref[1] == 1)
    def _():
        second[:, REACH + lats :, :, :] = jnp.zeros((groups, REACH, wide_slot, LANES), jnp.float32)

    depthwise(second, spread, mixed, 1, lats, 32, slot // 8, 0)

    def final_store(g, row, value):
        final[g, pl.ds(row, ROWS), :, :] = value

    pointwise(
        mixed, 1, lats, slot,
        lambda g, row: second[g, pl.ds(row + REACH, ROWS), REACH : REACH + slot, :],
        final_store, weights,
    )
    flat = lats * slot // tiles // LANES
    rows_per = LANES * 3 // slot
    for half in range(flat):
        for g in range(groups):
            for part in range(tiles // 3):
                lat = (half * tiles + part * 3) * LANES // slot
                block = final[g, lat : lat + rows_per, :, :].reshape(rows_per * slot, LANES)
                for t in range(3):
                    start = half * channels * tiles + g * LANES * tiles + part * 3 + t
                    rows32[pl.ds(start, LANES, stride=tiles), :] = block[
                        t * LANES : (t + 1) * LANES
                    ].T
    out_ref[...] = rows32[...].astype(jnp.bfloat16)


def near(x):
    return pltpu.with_memory_space_constraint(x, pltpu.VMEM)


def run_cut(field, seg, slot):
    chans, members, lats, lons = field.shape
    tiles = lats * slot // LANES
    rows = members * (lons // seg) * chans * tiles
    return pl.pallas_call(
        lambda *refs: cut_kernel(*refs, seg=seg, slot=slot),
        out_shape=pltpu.VMEM((rows, LANES), jnp.bfloat16),
        scratch_shapes=[
            pltpu.VMEM((-(-lons // LANES), chans * members * lats, LANES), jnp.float32),
            pltpu.VMEM((rows, LANES), jnp.float32),
        ],
        name="cut",
    )(field)


def run_paste(pieces, shape, seg, slot):
    chans, members, lats, lons = shape
    return pl.pallas_call(
        lambda *refs: paste_kernel(*refs, seg=seg, slot=slot),
        out_shape=jax.ShapeDtypeStruct(shape, jnp.bfloat16),
        scratch_shapes=[
            pltpu.VMEM(pieces.shape, jnp.float32),
            pltpu.VMEM((-(-lons // LANES), chans * members * lats, LANES), jnp.float32),
        ],
        name="paste",
    )(near(pieces))


def run_to_cells(pieces, cells, channels, tiles, edge):
    outs = [(cells, channels), (edge, channels), (edge, channels)]
    return pl.pallas_call(
        lambda *refs: to_cells_kernel(*refs, tiles=tiles),
        out_shape=[pltpu.VMEM(out, jnp.bfloat16) for out in outs],
        scratch_shapes=[pltpu.VMEM(pieces.shape, jnp.float32)],
        name="to_cells",
    )(near(pieces))


def run_blocks(edges, x, halos, mods, up, up_bias, down, down_bias, scale, tiles):
    lats, slot, channels = x.shape
    groups = channels // LANES
    rows = lats * slot * channels // LANES
    vmem = pl.BlockSpec(memory_space=pltpu.VMEM)
    arrays = (x, *halos, mods, up, up_bias, down, down_bias, scale)
    wide_slot = slot + 8
    return pl.pallas_call(
        lambda *refs: blocks_kernel(*refs, tiles=tiles),
        out_shape=pltpu.VMEM((rows, LANES), jnp.bfloat16),
        in_specs=[pl.BlockSpec(memory_space=pltpu.SMEM)] + [vmem] * len(arrays),
        scratch_shapes=[
            pltpu.VMEM((groups, lats + 4 * REACH, LEFT + wide_slot, LANES), jnp.float32),
            pltpu.VMEM((groups, lats + 2 * REACH, wide_slot, LANES), jnp.float32),
            pltpu.VMEM((up.shape[0], groups, TAPS * TAPS + 1, 8, LANES), jnp.float32),
            pltpu.VMEM((groups, lats + 2 * REACH, wide_slot, LANES), jnp.float32),
            pltpu.VMEM((groups, lats, slot, LANES), jnp.float32),
            pltpu.VMEM((rows, LANES), jnp.float32),
        ],
        compiler_params=pltpu.CompilerParams(vmem_limit_bytes=24 * 2**20),
        name="blocks",
    )(edges, *[near(a) for a in arrays])


def halo_of(x, north, south, filters, seg):
    rows, segs = lax.axis_size("y"), lax.axis_size("xc")
    reach = 2 * REACH
    down = [(i, i + 1) for i in range(rows - 1)]
    up = [(j, i) for i, j in down]
    top = lax.ppermute(south, "y", down)
    bottom = lax.ppermute(north, "y", up)
    top, bottom, filters = lax.optimization_barrier((top, bottom, filters))
    east = [(i, (i + 1) % segs) for i in range(segs)]
    west = [(j, i) for i, j in east]

    def columns(lo):
        return jnp.concatenate(
            [part[:, lo : lo + reach] for part in (top, x, bottom)], axis=0
        )

    left = lax.ppermute(columns(seg - reach), "xc", east)
    right = lax.ppermute(columns(0), "xc", west)
    return top, bottom, left, right, filters


def on_device(
    field, noise_level, conv_kernel, conv_bias, modulation,
    expand_weight, expand_bias, project_weight, project_bias, layer_scale,
):
    chans, members, lats, lons = field.shape
    layers = conv_kernel.shape[0]
    halves = lax.axis_size("zh")
    segs = lax.axis_size("xc")
    peers = halves * lax.axis_size("zl") * segs
    channels = chans * lax.axis_size("zl") * segs
    seg = lons // segs
    slot = -(-seg // 8) * 8
    tiles = lats * slot // LANES
    member = lax.axis_index("zh") * lax.axis_size("zl") + lax.axis_index("zl")
    mods = modulation[:, noise_level[member]].reshape(2 * layers, channels)
    band = lax.axis_index("y")
    edges = jnp.stack([band == 0, band == lax.axis_size("y") - 1]).astype(jnp.int32)

    pieces = run_cut(field, seg, slot)
    pieces, conv_kernel, conv_bias = lax.optimization_barrier((pieces, conv_kernel, conv_bias))
    filters = jnp.concatenate(
        [conv_kernel.reshape(layers, chans, TAPS * TAPS), conv_bias[:, :, None]], axis=2
    )
    shape = (peers, chans * tiles, LANES)
    around = ("zh", "zl", "xc")
    pieces = lax.all_to_all(pieces.reshape(shape), around, 0, 0, tiled=True).reshape(-1, LANES)
    filters = jnp.broadcast_to(filters.reshape(1, -1), (channels // chans, filters.size))
    pieces, filters = lax.optimization_barrier((pieces, filters))
    filters = lax.all_to_all(filters, ("zl", "xc"), 0, 0, tiled=True)
    filters = filters.reshape(channels // chans, layers, chans, TAPS * TAPS + 1)
    filters = filters.transpose(1, 3, 0, 2).reshape(layers, TAPS * TAPS + 1, channels)

    cells = run_to_cells(pieces, halves * lats * slot, channels, tiles, 2 * REACH * slot)
    x, north, south = [part.reshape(-1, slot, channels) for part in cells]
    pieces = run_blocks(
        edges, x, halo_of(x, north, south, filters, seg), mods,
        expand_weight, expand_bias, project_weight, project_bias, layer_scale, tiles,
    )
    pieces = lax.all_to_all(pieces.reshape(shape), around, 0, 0, tiled=True).reshape(-1, LANES)
    return run_paste(pieces, field.shape, seg, slot)


def solution(mesh):
    bands, chan = mesh.shape["band"], mesh.shape["chan"]
    split = Mesh(mesh.devices.reshape(bands // 2, 2, chan // 8, 8), ("y", "zh", "zl", "xc"))
    band, group = ("y", "zh"), ("zl", "xc")
    return jax.shard_map(
        on_device,
        mesh=split,
        in_specs=(
            P(group, None, band, None),
            P(),
            P(None, group, None, None),
            P(None, group),
            P(), P(), P(), P(), P(), P(),
        ),
        out_specs=P(group, None, band, None),
        check_vma=False,
    )
```

```python
import jax
import jax.numpy as jnp
from jax import lax
from jax.experimental import pallas as pl
from jax.experimental.pallas import tpu as pltpu
from jax.sharding import Mesh, PartitionSpec as P

EPS = 1e-06
LANES = 128
TAPS = 7
REACH = 3
LEFT = 8
ROWS = 8
HALF_LANES = 64
TAP_ROWS = 56


def lane_iota(rows):
    return lax.broadcasted_iota(jnp.int32, (rows, LANES), 1)


def moved_lanes(load, spans, rows, rolled):
    lanes = lane_iota(rows)
    tile = None
    for source, src, dst, width in spans:
        done = 0
        while done < width:
            part, lane = divmod(src + done, LANES)
            take = min(width - done, LANES - lane)
            shift = (dst + done - lane) % LANES
            key = (source, part, shift)
            if key not in rolled:
                value = load(source, part)
                rolled[key] = pltpu.roll(value, shift, 1) if shift else value
            value = rolled[key]
            tile = value if tile is None else jnp.where(lanes >= dst + done, value, tile)
            done += take
    return tile


def spans_of(count, stride, width, tile_index, start_of):
    spans = []
    for item in range(count):
        lo = max(item * stride, tile_index * LANES)
        hi = min(item * stride + width, (tile_index + 1) * LANES)
        if lo < hi:
            spans.append((item, start_of(item) + lo - item * stride, lo - tile_index * LANES, hi - lo))
    return spans


def cut_kernel(field_ref, filter_ref, out_ref, wide, cut, *, seg, slot):
    chans, members, lats, lons = field_ref.shape
    rows = chans * members
    parts = -(-lons // LANES)
    segs = lons // seg
    tiles = lats * slot // LANES
    extra = filter_ref.shape[0]
    piece_rows = chans * tiles + extra
    for e in range(extra):
        cut[pl.ds(chans * tiles + e, members * segs, stride=piece_rows), :] = jnp.broadcast_to(
            filter_ref[e : e + 1, :], (members * segs, LANES)
        )
    for a in range(parts):
        lo, hi = a * LANES, min((a + 1) * LANES, lons)
        piece = field_ref[:, :, :, lo:hi].astype(jnp.float32).reshape(rows * lats, hi - lo)
        wide[a, :, 0 : hi - lo] = piece
        if hi - lo < LANES:
            wide[a, :, hi - lo :] = jnp.zeros((rows * lats, LANES - hi + lo), jnp.float32)
    for s in range(segs):
        rolled = {}
        for t in range(tiles):
            spans = spans_of(lats, slot, seg, t, lambda item: s * seg)

            def load(lat, part):
                return wide[part, pl.ds(lat, rows, stride=lats), :]

            tile = moved_lanes(load, spans, rows, rolled)
            for c in range(chans):
                start = s * piece_rows + c * tiles + t
                cut[pl.ds(start, members, stride=segs * piece_rows), :] = tile[
                    c * members : (c + 1) * members
                ]
    out_ref[...] = cut[...].astype(jnp.bfloat16)


def paste_kernel(in_ref, out_ref, cut, wide, *, seg, slot):
    chans, members, lats, lons = out_ref.shape
    rows = chans * members
    parts = -(-lons // LANES)
    segs = lons // seg
    tiles = lats * slot // LANES
    cut[...] = in_ref[...].astype(jnp.float32)
    for lat in range(lats):
        rolled = {}
        for a in range(parts):
            spans = spans_of(segs, seg, seg, a, lambda item: lat * slot)

            def load(s, part):
                return jnp.concatenate(
                    [
                        cut[
                            pl.ds(
                                s * chans * tiles + c * tiles + part,
                                members,
                                stride=segs * chans * tiles,
                            ),
                            :,
                        ]
                        for c in range(chans)
                    ],
                    axis=0,
                )

            wide[a, pl.ds(lat, rows, stride=lats), :] = moved_lanes(load, spans, rows, rolled)
    for a in range(parts):
        lo, hi = a * LANES, min((a + 1) * LANES, lons)
        out_ref[:, :, :, lo:hi] = (
            wide[a, :, 0 : hi - lo].reshape(chans, members, lats, hi - lo).astype(jnp.bfloat16)
        )


def to_cells_kernel(
    in_ref, out_ref, north_ref, south_ref, taps_ref, raw, rows32, *, tiles, sources
):
    cells, channels = out_ref.shape
    halves = taps_ref.shape[0]
    data = rows32.shape[0]
    piece_rows = in_ref.shape[0] // sources
    data_rows = data // sources
    raw[...] = in_ref[...].astype(jnp.float32)
    for src in range(sources):
        rows32[src * data_rows : (src + 1) * data_rows, :] = raw[
            src * piece_rows : src * piece_rows + data_rows, :
        ]
    for half in range(halves):
        for t in range(tiles):
            block = rows32[pl.ds(half * channels * tiles + t, channels, stride=tiles), :]
            start = (half * tiles + t) * LANES
            out_ref[start : start + LANES, :] = block.T.astype(jnp.bfloat16)
    edge = north_ref.shape[0]
    north_ref[...] = out_ref[0:edge, :]
    south_ref[...] = out_ref[cells - edge :, :]
    owners = sources // halves
    chans = channels // owners
    taps = taps_ref.shape[1]
    owner = lax.broadcasted_iota(jnp.int32, (owners, channels), 0)
    channel = lax.broadcasted_iota(jnp.int32, (owners, channels), 1)
    for half in range(halves):
        total = jnp.zeros((taps, channels), jnp.float32)
        for e in range(piece_rows - data_rows):
            start = half * owners * piece_rows + data_rows + e
            lines = raw[pl.ds(start, owners, stride=piece_rows), :].T.astype(jnp.bfloat16)
            for k in range(2):
                place = (channel == owner * chans + 2 * e + k).astype(jnp.float32)
                spread = jnp.dot(
                    lines, place.astype(jnp.bfloat16), preferred_element_type=jnp.float32
                )
                total = total + spread[k * HALF_LANES : k * HALF_LANES + taps, :]
        taps_ref[half] = total


def depthwise(source, spread, mixed, layer, lats, rows, col_tiles, first_col):
    groups = source.shape[0]
    steps = -(-lats // rows)
    for k in range(col_tiles):

        def step_of(step, carry):
            g = step // steps
            row = jnp.minimum((step % steps) * rows, lats - rows)
            def column_of(j, sums):
                sums = list(sums)
                weights = [spread[layer, g, i * TAPS + j] for i in range(TAPS)]
                for r in range(rows + TAPS - 1):
                    value = source[g, row + r, pl.ds(first_col + 8 * k + j, 8), :]
                    for i in range(TAPS):
                        if 0 <= r - i < rows:
                            sums[r - i] = sums[r - i] + weights[i] * value
                return tuple(sums)

            start = (spread[layer, g, TAPS * TAPS],) * rows
            sums = lax.fori_loop(0, TAPS, column_of, start)
            for r in range(rows):
                mixed[g, row + r, 8 * k : 8 * k + 8, :] = sums[r]
            return carry

        lax.fori_loop(0, groups * steps, step_of, 0)


def pointwise(mixed, layer, lats, slot, residual, store, weights):
    mod_ref, up_ref, up_bias_ref, down_ref, down_bias_ref, scale_ref = weights
    groups = mixed.shape[0]
    channels = groups * LANES
    cells = ROWS * slot
    steps = -(-lats // ROWS)
    average_matrix = jnp.full((channels, channels), 1.0 / channels, jnp.bfloat16)

    def step_of(step, carry):
        row = jnp.minimum(step * ROWS, lats - ROWS)
        parts = [mixed[g, pl.ds(row, ROWS), 0:slot, :].reshape(cells, LANES) for g in range(groups)]
        rounded = jnp.concatenate(parts, axis=1).astype(jnp.bfloat16)
        average = jnp.dot(rounded, average_matrix, preferred_element_type=jnp.float32)
        centered = rounded.astype(jnp.float32) - average
        variance = jnp.dot(
            (centered * centered).astype(jnp.bfloat16),
            average_matrix,
            preferred_element_type=jnp.float32,
        )
        gain = 1.0 + mod_ref[2 * layer : 2 * layer + 1, :]
        shift = mod_ref[2 * layer + 1 : 2 * layer + 2, :]
        normed = (centered * lax.rsqrt(variance + EPS) * gain + shift).astype(jnp.bfloat16)
        hidden = (
            jnp.dot(normed, up_ref[layer], preferred_element_type=jnp.float32)
            + up_bias_ref[layer : layer + 1, :]
        )
        doubled = (hidden * (1.0 + lax.erf(hidden * 0.7071067811865476))).astype(jnp.bfloat16)
        result = (
            0.5 * jnp.dot(doubled, down_ref[layer], preferred_element_type=jnp.float32)
            + down_bias_ref[layer : layer + 1, :]
        )
        branch = (scale_ref[layer : layer + 1, :] * result).astype(jnp.bfloat16).astype(jnp.float32)
        for g in range(groups):
            part = branch[:, g * LANES : (g + 1) * LANES].reshape(ROWS, slot, LANES)
            store(g, row, (residual(g, row) + part).astype(jnp.bfloat16).astype(jnp.float32))
        return carry

    lax.fori_loop(0, steps, step_of, 0)


def blocks_kernel(
    edge_ref, x_ref, top_ref, bottom_ref, left_ref, right_ref, taps_ref, mod_ref,
    up_ref, up_bias_ref, down_ref, down_bias_ref, scale_ref,
    out_ref, first, second, spread, mixed, final, rows32, *, tiles,
):
    lats, slot, channels = x_ref.shape
    groups = channels // LANES
    reach = 2 * REACH
    wide = lats + reach
    right_at = LEFT + slot - REACH
    for g in range(groups):
        ch = slice(g * LANES, (g + 1) * LANES)
        first[g, 0:reach, LEFT : LEFT + slot, :] = top_ref[:, :, ch].astype(jnp.float32)
        first[g, reach : reach + lats, LEFT : LEFT + slot, :] = x_ref[:, :, ch].astype(jnp.float32)
        first[g, reach + lats :, LEFT : LEFT + slot, :] = bottom_ref[:, :, ch].astype(jnp.float32)
        first[g, :, LEFT + slot :, :] = jnp.zeros(
            (lats + 2 * reach, first.shape[2] - LEFT - slot, LANES), jnp.float32
        )
        first[g, :, LEFT - reach : LEFT, :] = left_ref[:, :, ch].astype(jnp.float32)
        first[g, :, right_at : right_at + reach, :] = right_ref[:, :, ch].astype(jnp.float32)
        for layer in range(taps_ref.shape[0]):
            for k in range(TAPS * TAPS + 1):
                spread[layer, g, k] = jnp.broadcast_to(taps_ref[layer, k : k + 1, ch], (8, LANES))
    weights = (mod_ref, up_ref, up_bias_ref, down_ref, down_bias_ref, scale_ref)

    wide_slot = slot + 8
    depthwise(first, spread, mixed, 0, wide, 19, wide_slot // 8, LEFT - reach)

    def first_store(g, row, value):
        second[g, pl.ds(row, ROWS), :, :] = value

    pointwise(
        mixed, 0, wide, wide_slot,
        lambda g, row: first[g, pl.ds(row + REACH, ROWS), LEFT - REACH : LEFT - REACH + wide_slot, :],
        first_store, weights,
    )

    @pl.when(edge_ref[0] == 1)
    def _():
        second[:, 0:REACH, :, :] = jnp.zeros((groups, REACH, wide_slot, LANES), jnp.float32)

    @pl.when(edge_ref[1] == 1)
    def _():
        second[:, REACH + lats :, :, :] = jnp.zeros((groups, REACH, wide_slot, LANES), jnp.float32)

    depthwise(second, spread, mixed, 1, lats, 32, slot // 8, 0)

    def final_store(g, row, value):
        final[g, pl.ds(row, ROWS), :, :] = value

    pointwise(
        mixed, 1, lats, slot,
        lambda g, row: second[g, pl.ds(row + REACH, ROWS), REACH : REACH + slot, :],
        final_store, weights,
    )
    flat = lats * slot // tiles // LANES
    rows_per = LANES * 3 // slot
    for half in range(flat):
        for g in range(groups):
            for part in range(tiles // 3):
                lat = (half * tiles + part * 3) * LANES // slot
                block = final[g, lat : lat + rows_per, :, :].reshape(rows_per * slot, LANES)
                for t in range(3):
                    start = half * channels * tiles + g * LANES * tiles + part * 3 + t
                    rows32[pl.ds(start, LANES, stride=tiles), :] = block[
                        t * LANES : (t + 1) * LANES
                    ].T
    out_ref[...] = rows32[...].astype(jnp.bfloat16)


def near(x):
    return pltpu.with_memory_space_constraint(x, pltpu.VMEM)


def run_cut(field, filters, seg, slot):
    chans, members, lats, lons = field.shape
    tiles = lats * slot // LANES
    rows = members * (lons // seg) * (chans * tiles + filters.shape[0])
    return pl.pallas_call(
        lambda *refs: cut_kernel(*refs, seg=seg, slot=slot),
        out_shape=pltpu.VMEM((rows, LANES), jnp.bfloat16),
        scratch_shapes=[
            pltpu.VMEM((-(-lons // LANES), chans * members * lats, LANES), jnp.float32),
            pltpu.VMEM((rows, LANES), jnp.float32),
        ],
        name="cut",
    )(field, filters)


def run_paste(pieces, shape, seg, slot):
    chans, members, lats, lons = shape
    return pl.pallas_call(
        lambda *refs: paste_kernel(*refs, seg=seg, slot=slot),
        out_shape=jax.ShapeDtypeStruct(shape, jnp.bfloat16),
        scratch_shapes=[
            pltpu.VMEM(pieces.shape, jnp.float32),
            pltpu.VMEM((-(-lons // LANES), chans * members * lats, LANES), jnp.float32),
        ],
        name="paste",
    )(near(pieces))


def run_to_cells(pieces, cells, channels, tiles, edge, sources, layers):
    outs = [(cells, channels), (edge, channels), (edge, channels)]
    return pl.pallas_call(
        lambda *refs: to_cells_kernel(*refs, tiles=tiles, sources=sources),
        out_shape=[pltpu.VMEM(out, jnp.bfloat16) for out in outs]
        + [pltpu.VMEM((layers, TAP_ROWS, channels), jnp.float32)],
        scratch_shapes=[
            pltpu.VMEM(pieces.shape, jnp.float32),
            pltpu.VMEM((cells * channels // LANES, LANES), jnp.float32),
        ],
        name="to_cells",
    )(near(pieces))


def run_blocks(edges, x, halos, taps, mods, up, up_bias, down, down_bias, scale, tiles):
    lats, slot, channels = x.shape
    groups = channels // LANES
    rows = lats * slot * channels // LANES
    vmem = pl.BlockSpec(memory_space=pltpu.VMEM)
    arrays = (x, *halos, taps, mods, up, up_bias, down, down_bias, scale)
    wide_slot = slot + 8
    return pl.pallas_call(
        lambda *refs: blocks_kernel(*refs, tiles=tiles),
        out_shape=pltpu.VMEM((rows, LANES), jnp.bfloat16),
        in_specs=[pl.BlockSpec(memory_space=pltpu.SMEM)] + [vmem] * len(arrays),
        scratch_shapes=[
            pltpu.VMEM((groups, lats + 4 * REACH, LEFT + wide_slot, LANES), jnp.float32),
            pltpu.VMEM((groups, lats + 2 * REACH, wide_slot, LANES), jnp.float32),
            pltpu.VMEM((taps.shape[0], groups, TAPS * TAPS + 1, 8, LANES), jnp.float32),
            pltpu.VMEM((groups, lats + 2 * REACH, wide_slot, LANES), jnp.float32),
            pltpu.VMEM((groups, lats, slot, LANES), jnp.float32),
            pltpu.VMEM((rows, LANES), jnp.float32),
        ],
        compiler_params=pltpu.CompilerParams(vmem_limit_bytes=40 * 2**20),
        name="blocks",
    )(edges, *[near(a) for a in arrays])


def halo_of(x, north, south, seg):
    rows, segs = lax.axis_size("y"), lax.axis_size("xc")
    reach = 2 * REACH
    down = [(i, i + 1) for i in range(rows - 1)]
    up = [(j, i) for i, j in down]
    top = lax.ppermute(south, "y", down)
    bottom = lax.ppermute(north, "y", up)
    east = [(i, (i + 1) % segs) for i in range(segs)]
    west = [(j, i) for i, j in east]

    def columns(lo):
        return jnp.concatenate(
            [part[:, lo : lo + reach] for part in (top, x, bottom)], axis=0
        )

    left = lax.ppermute(columns(seg - reach), "xc", east)
    right = lax.ppermute(columns(0), "xc", west)
    return top, bottom, left, right


def on_device(
    field, noise_level, conv_kernel, conv_bias, modulation,
    expand_weight, expand_bias, project_weight, project_bias, layer_scale,
):
    chans, members, lats, lons = field.shape
    layers = conv_kernel.shape[0]
    halves = lax.axis_size("zh")
    segs = lax.axis_size("xc")
    peers = halves * lax.axis_size("zl") * segs
    channels = chans * lax.axis_size("zl") * segs
    seg = lons // segs
    slot = -(-seg // 8) * 8
    tiles = lats * slot // LANES
    member = lax.axis_index("zh") * lax.axis_size("zl") + lax.axis_index("zl")
    mods = modulation[:, noise_level[member]].reshape(2 * layers, channels)
    band = lax.axis_index("y")
    edges = jnp.stack([band == 0, band == lax.axis_size("y") - 1]).astype(jnp.int32)

    layer = lax.axis_index("zh")
    filters = jnp.concatenate(
        [
            conv_kernel.reshape(layers, chans, TAPS * TAPS),
            conv_bias[:, :, None],
            jnp.zeros((layers, chans, HALF_LANES - TAPS * TAPS - 1), jnp.float32),
        ],
        axis=2,
    )
    filters = lax.dynamic_index_in_dim(filters, layer, 0, False).reshape(-1, LANES)
    pieces = run_cut(field, filters, seg, slot)
    around = ("zh", "zl", "xc")
    pairs = pieces.reshape(peers, -1, 2, LANES)
    pieces = lax.all_to_all(pairs, around, 0, 0, tiled=True).reshape(-1, LANES)
    shape = (peers, chans * tiles, LANES)
    cells = run_to_cells(
        pieces, halves * lats * slot, channels, tiles, 2 * REACH * slot, peers, layers
    )
    x, north, south = [part.reshape(-1, slot, channels) for part in cells[:3]]
    filters = cells[3]
    pieces = run_blocks(
        edges, x, halo_of(x, north, south, seg), filters, mods,
        expand_weight, expand_bias, project_weight, project_bias, layer_scale, tiles,
    )
    pieces = lax.all_to_all(pieces.reshape(shape), around, 0, 0, tiled=True).reshape(-1, LANES)
    return run_paste(pieces, field.shape, seg, slot)


def solution(mesh):
    bands, chan = mesh.shape["band"], mesh.shape["chan"]
    split = Mesh(mesh.devices.reshape(bands // 2, 2, chan // 8, 8), ("y", "zh", "zl", "xc"))
    band, group = ("y", "zh"), ("zl", "xc")
    return jax.shard_map(
        on_device,
        mesh=split,
        in_specs=(
            P(group, None, band, None),
            P(),
            P(None, group, None, None),
            P(None, group),
            P(), P(), P(), P(), P(), P(),
        ),
        out_specs=P(group, None, band, None),
        check_vma=False,
    )
```

```python
import jax
import jax.numpy as jnp
from jax import lax
from jax.experimental import pallas as pl
from jax.experimental.pallas import tpu as pltpu
from jax.sharding import Mesh, PartitionSpec as P

EPS = 1e-06
LANES = 128
TAPS = 7
REACH = 3
LEFT = 8
ROWS = 8
HALF_LANES = 64
TAP_ROWS = 56


def lane_iota(rows):
    return lax.broadcasted_iota(jnp.int32, (rows, LANES), 1)


def moved_lanes(load, spans, rows, rolled):
    lanes = lane_iota(rows)
    tile = None
    for source, src, dst, width in spans:
        done = 0
        while done < width:
            part, lane = divmod(src + done, LANES)
            take = min(width - done, LANES - lane)
            shift = (dst + done - lane) % LANES
            key = (source, part, shift)
            if key not in rolled:
                value = load(source, part)
                rolled[key] = pltpu.roll(value, shift, 1) if shift else value
            value = rolled[key]
            tile = value if tile is None else jnp.where(lanes >= dst + done, value, tile)
            done += take
    return tile


def spans_of(count, stride, width, tile_index, start_of):
    spans = []
    for item in range(count):
        lo = max(item * stride, tile_index * LANES)
        hi = min(item * stride + width, (tile_index + 1) * LANES)
        if lo < hi:
            spans.append((item, start_of(item) + lo - item * stride, lo - tile_index * LANES, hi - lo))
    return spans


def cut_kernel(field_ref, filter_ref, out_ref, wide, cut, *, seg, slot):
    chans, members, lats, lons = field_ref.shape
    rows = chans * members
    parts = -(-lons // LANES)
    segs = lons // seg
    tiles = lats * slot // LANES
    extra = filter_ref.shape[0]
    piece_rows = chans * tiles + extra
    for e in range(extra):
        cut[pl.ds(chans * tiles + e, members * segs, stride=piece_rows), :] = jnp.broadcast_to(
            filter_ref[e : e + 1, :], (members * segs, LANES)
        )
    for a in range(parts):
        lo, hi = a * LANES, min((a + 1) * LANES, lons)
        piece = field_ref[:, :, :, lo:hi].astype(jnp.float32).reshape(rows * lats, hi - lo)
        wide[a, :, 0 : hi - lo] = piece
        if hi - lo < LANES:
            wide[a, :, hi - lo :] = jnp.zeros((rows * lats, LANES - hi + lo), jnp.float32)
    for s in range(segs):
        rolled = {}
        for t in range(tiles):
            spans = spans_of(lats, slot, seg, t, lambda item: s * seg)

            def load(lat, part):
                return wide[part, pl.ds(lat, rows, stride=lats), :]

            tile = moved_lanes(load, spans, rows, rolled)
            for c in range(chans):
                start = s * piece_rows + c * tiles + t
                cut[pl.ds(start, members, stride=segs * piece_rows), :] = tile[
                    c * members : (c + 1) * members
                ]
    out_ref[...] = cut[...].astype(jnp.bfloat16)


def paste_kernel(in_ref, out_ref, cut, wide, *, seg, slot):
    chans, members, lats, lons = out_ref.shape
    rows = chans * members
    parts = -(-lons // LANES)
    segs = lons // seg
    tiles = lats * slot // LANES
    cut[...] = in_ref[...].astype(jnp.float32)
    for lat in range(lats):
        rolled = {}
        for a in range(parts):
            spans = spans_of(segs, seg, seg, a, lambda item: lat * slot)

            def load(s, part):
                return jnp.concatenate(
                    [
                        cut[
                            pl.ds(
                                s * chans * tiles + c * tiles + part,
                                members,
                                stride=segs * chans * tiles,
                            ),
                            :,
                        ]
                        for c in range(chans)
                    ],
                    axis=0,
                )

            wide[a, pl.ds(lat, rows, stride=lats), :] = moved_lanes(load, spans, rows, rolled)
    for a in range(parts):
        lo, hi = a * LANES, min((a + 1) * LANES, lons)
        out_ref[:, :, :, lo:hi] = (
            wide[a, :, 0 : hi - lo].reshape(chans, members, lats, hi - lo).astype(jnp.bfloat16)
        )


def to_cells_kernel(
    in_ref, out_ref, north_ref, south_ref, taps_ref, raw, rows32, *, tiles, sources
):
    cells, channels = out_ref.shape
    halves = taps_ref.shape[0]
    data = rows32.shape[0]
    piece_rows = in_ref.shape[0] // sources
    data_rows = data // sources
    raw[...] = in_ref[...].astype(jnp.float32)
    for src in range(sources):
        rows32[src * data_rows : (src + 1) * data_rows, :] = raw[
            src * piece_rows : src * piece_rows + data_rows, :
        ]
    for half in range(halves):
        for t in range(tiles):
            block = rows32[pl.ds(half * channels * tiles + t, channels, stride=tiles), :]
            start = (half * tiles + t) * LANES
            out_ref[start : start + LANES, :] = block.T.astype(jnp.bfloat16)
    edge = north_ref.shape[0]
    north_ref[...] = out_ref[0:edge, :]
    south_ref[...] = out_ref[cells - edge :, :]
    owners = sources // halves
    chans = channels // owners
    taps = taps_ref.shape[1]
    owner = lax.broadcasted_iota(jnp.int32, (owners, channels), 0)
    channel = lax.broadcasted_iota(jnp.int32, (owners, channels), 1)
    for half in range(halves):
        total = jnp.zeros((taps, channels), jnp.float32)
        for e in range(piece_rows - data_rows):
            start = half * owners * piece_rows + data_rows + e
            lines = raw[pl.ds(start, owners, stride=piece_rows), :].T.astype(jnp.bfloat16)
            for k in range(2):
                place = (channel == owner * chans + 2 * e + k).astype(jnp.float32)
                spread = jnp.dot(
                    lines, place.astype(jnp.bfloat16), preferred_element_type=jnp.float32
                )
                total = total + spread[k * HALF_LANES : k * HALF_LANES + taps, :]
        taps_ref[half] = total


def depthwise(source, spread, mixed, layer, bands, tiles, first_col):
    packed = mixed.shape[1] == sum(count for _, count in bands)
    for k in tiles:

        def step_of(g, carry):
            def column_of(j, sums):
                sums = list(sums)
                weights = [spread[layer, g, i * TAPS + j] for i in range(TAPS)]
                at = 0
                for start, count in bands:
                    for r in range(count + TAPS - 1):
                        value = source[g, start + r, pl.ds(first_col + 8 * k + j, 8), :]
                        for i in range(TAPS):
                            if 0 <= r - i < count:
                                sums[at + r - i] = sums[at + r - i] + weights[i] * value
                    at += count
                return tuple(sums)

            total = sum(count for _, count in bands)
            sums = lax.fori_loop(0, TAPS, column_of, (spread[layer, g, TAPS * TAPS],) * total)
            at = 0
            for start, count in bands:
                for r in range(count):
                    row = at if packed else start + r
                    mixed[g, row, 8 * k : 8 * k + 8, :] = sums[at]
                    at += 1
            return carry

        lax.fori_loop(0, source.shape[0], step_of, 0)


def spread_taps(spread, taps_ref, layers):
    for g in range(spread.shape[1]):
        ch = slice(g * LANES, (g + 1) * LANES)
        for layer in range(layers):
            for k in range(TAPS * TAPS + 1):
                spread[layer, g, k] = jnp.broadcast_to(taps_ref[layer, k : k + 1, ch], (8, LANES))


def middle_kernel(*refs, bands, tiles):
    *part_refs, taps_ref, out_ref, source, spread = refs
    for g in range(source.shape[0]):
        row = 0
        for part_ref, lo, hi in part_refs_of(part_refs, source.shape[1]):
            ch = slice(g * LANES, (g + 1) * LANES)
            source[g, row : row + hi - lo, :, :] = part_ref[lo:hi, :, ch].astype(jnp.float32)
            row += hi - lo
    spread_taps(spread, taps_ref, 1)
    depthwise(source, spread, out_ref, 0, bands, range(tiles), 8 - 2 * REACH)


def part_refs_of(part_refs, rows):
    if len(part_refs) == 1:
        return [(part_refs[0], 0, rows)]
    top_ref, x_ref, bottom_ref = part_refs
    edge, lats = top_ref.shape[0], x_ref.shape[0]
    return [(top_ref, 0, edge), (x_ref, 0, edge), (x_ref, lats - edge, lats), (bottom_ref, 0, edge)]


def pointwise(mixed, layer, lats, slot, residual, store, weights):
    mod_ref, up_ref, up_bias_ref, down_ref, down_bias_ref, scale_ref = weights
    groups = mixed.shape[0]
    channels = groups * LANES
    cells = ROWS * slot
    steps = -(-lats // ROWS)
    average_matrix = jnp.full((channels, channels), 1.0 / channels, jnp.bfloat16)

    def step_of(step, carry):
        row = jnp.minimum(step * ROWS, lats - ROWS)
        parts = [mixed[g, pl.ds(row, ROWS), 0:slot, :].reshape(cells, LANES) for g in range(groups)]
        rounded = jnp.concatenate(parts, axis=1).astype(jnp.bfloat16)
        average = jnp.dot(rounded, average_matrix, preferred_element_type=jnp.float32)
        centered = rounded.astype(jnp.float32) - average
        variance = jnp.dot(
            (centered * centered).astype(jnp.bfloat16),
            average_matrix,
            preferred_element_type=jnp.float32,
        )
        gain = 1.0 + mod_ref[2 * layer : 2 * layer + 1, :]
        shift = mod_ref[2 * layer + 1 : 2 * layer + 2, :]
        normed = (centered * lax.rsqrt(variance + EPS) * gain + shift).astype(jnp.bfloat16)
        hidden = (
            jnp.dot(normed, up_ref[layer], preferred_element_type=jnp.float32)
            + up_bias_ref[layer : layer + 1, :]
        )
        doubled = (hidden * (1.0 + lax.erf(hidden * 0.7071067811865476))).astype(jnp.bfloat16)
        result = (
            0.5 * jnp.dot(doubled, down_ref[layer], preferred_element_type=jnp.float32)
            + down_bias_ref[layer : layer + 1, :]
        )
        branch = (scale_ref[layer : layer + 1, :] * result).astype(jnp.bfloat16).astype(jnp.float32)
        for g in range(groups):
            part = branch[:, g * LANES : (g + 1) * LANES].reshape(ROWS, slot, LANES)
            store(g, row, (residual(g, row) + part).astype(jnp.bfloat16).astype(jnp.float32))
        return carry

    lax.fori_loop(0, steps, step_of, 0)


def blocks_kernel(
    edge_ref, x_ref, top_ref, bottom_ref, left_ref, right_ref, taps_ref, inner_ref, outer_ref, mod_ref,
    up_bias_ref, down_bias_ref, scale_ref, up_hbm, down_hbm,
    out_ref, first, second, spread, mixed, final, rows32, up_ref, down_ref, arrived, *, tiles,
):
    lats, slot, channels = x_ref.shape
    groups = channels // LANES
    reach = 2 * REACH
    wide = lats + reach
    right_at = LEFT + slot - REACH
    copies = [
        pltpu.make_async_copy(up_hbm, up_ref, arrived.at[0]),
        pltpu.make_async_copy(down_hbm, down_ref, arrived.at[1]),
    ]
    for copy in copies:
        copy.start()
    for g in range(groups):
        ch = slice(g * LANES, (g + 1) * LANES)
        first[g, 0:reach, LEFT : LEFT + slot, :] = top_ref[:, :, ch].astype(jnp.float32)
        first[g, reach : reach + lats, LEFT : LEFT + slot, :] = x_ref[:, :, ch].astype(jnp.float32)
        first[g, reach + lats :, LEFT : LEFT + slot, :] = bottom_ref[:, :, ch].astype(jnp.float32)
        first[g, :, LEFT + slot :, :] = jnp.zeros(
            (lats + 2 * reach, first.shape[2] - LEFT - slot, LANES), jnp.float32
        )
        first[g, :, LEFT - reach : LEFT, :] = left_ref[:, :, ch].astype(jnp.float32)
        first[g, :, right_at : right_at + reach, :] = right_ref[:, :, ch].astype(jnp.float32)
        middle = slice(8, 8 + inner_ref.shape[2])
        mixed[g, 0:reach, middle, :] = outer_ref[g, 0:reach]
        mixed[g, reach:lats, middle, :] = inner_ref[g]
        mixed[g, lats:wide, middle, :] = outer_ref[g, reach:]
    spread_taps(spread, taps_ref, taps_ref.shape[0])
    weights = (mod_ref, up_ref, up_bias_ref, down_ref, down_bias_ref, scale_ref)

    wide_slot = slot + 8
    covered = inner_ref.shape[2] // 8
    sides = [k for k in range(wide_slot // 8) if not 1 <= k <= covered]
    depthwise(first, spread, mixed, 0, [(0, wide // 2)], sides, LEFT - reach)
    depthwise(first, spread, mixed, 0, [(wide // 2, wide - wide // 2)], sides, LEFT - reach)

    for copy in copies:
        copy.wait()

    def first_store(g, row, value):
        second[g, pl.ds(row, ROWS), :, :] = value

    pointwise(
        mixed, 0, wide, wide_slot,
        lambda g, row: first[g, pl.ds(row + REACH, ROWS), LEFT - REACH : LEFT - REACH + wide_slot, :],
        first_store, weights,
    )

    @pl.when(edge_ref[0] == 1)
    def _():
        second[:, 0:REACH, :, :] = jnp.zeros((groups, REACH, wide_slot, LANES), jnp.float32)

    @pl.when(edge_ref[1] == 1)
    def _():
        second[:, REACH + lats :, :, :] = jnp.zeros((groups, REACH, wide_slot, LANES), jnp.float32)

    depthwise(second, spread, mixed, 1, [(0, lats)], range(slot // 8), 0)

    def final_store(g, row, value):
        final[g, pl.ds(row, ROWS), :, :] = value

    pointwise(
        mixed, 1, lats, slot,
        lambda g, row: second[g, pl.ds(row + REACH, ROWS), REACH : REACH + slot, :],
        final_store, weights,
    )
    flat = lats * slot // tiles // LANES
    rows_per = LANES * 3 // slot
    for half in range(flat):
        for g in range(groups):
            for part in range(tiles // 3):
                lat = (half * tiles + part * 3) * LANES // slot
                block = final[g, lat : lat + rows_per, :, :].reshape(rows_per * slot, LANES)
                for t in range(3):
                    start = half * channels * tiles + g * LANES * tiles + part * 3 + t
                    rows32[pl.ds(start, LANES, stride=tiles), :] = block[
                        t * LANES : (t + 1) * LANES
                    ].T
    out_ref[...] = rows32[...].astype(jnp.bfloat16)


def near(x):
    return pltpu.with_memory_space_constraint(x, pltpu.VMEM)


def far(x):
    return pltpu.with_memory_space_constraint(x, pltpu.HBM)


def run_cut(field, filters, seg, slot):
    chans, members, lats, lons = field.shape
    tiles = lats * slot // LANES
    rows = members * (lons // seg) * (chans * tiles + filters.shape[0])
    return pl.pallas_call(
        lambda *refs: cut_kernel(*refs, seg=seg, slot=slot),
        out_shape=pltpu.VMEM((rows, LANES), jnp.bfloat16),
        scratch_shapes=[
            pltpu.VMEM((-(-lons // LANES), chans * members * lats, LANES), jnp.float32),
            pltpu.VMEM((rows, LANES), jnp.float32),
        ],
        name="cut",
    )(field, filters)


def run_paste(pieces, shape, seg, slot):
    chans, members, lats, lons = shape
    return pl.pallas_call(
        lambda *refs: paste_kernel(*refs, seg=seg, slot=slot),
        out_shape=jax.ShapeDtypeStruct(shape, jnp.bfloat16),
        scratch_shapes=[
            pltpu.VMEM(pieces.shape, jnp.float32),
            pltpu.VMEM((-(-lons // LANES), chans * members * lats, LANES), jnp.float32),
        ],
        name="paste",
    )(near(pieces))


def run_to_cells(pieces, cells, channels, tiles, edge, sources, layers):
    outs = [(cells, channels), (edge, channels), (edge, channels)]
    return pl.pallas_call(
        lambda *refs: to_cells_kernel(*refs, tiles=tiles, sources=sources),
        out_shape=[pltpu.VMEM(out, jnp.bfloat16) for out in outs]
        + [pltpu.VMEM((layers, TAP_ROWS, channels), jnp.float32)],
        scratch_shapes=[
            pltpu.VMEM(pieces.shape, jnp.float32),
            pltpu.VMEM((cells * channels // LANES, LANES), jnp.float32),
        ],
        name="to_cells",
    )(near(pieces))


def run_middle(parts, taps, rows, bands, cols):
    slot, channels = parts[0].shape[1:]
    groups = channels // LANES
    total = sum(count for _, count in bands)
    return pl.pallas_call(
        lambda *refs: middle_kernel(*refs, bands=bands, tiles=cols // 8),
        out_shape=pltpu.VMEM((groups, total, cols, LANES), jnp.float32),
        scratch_shapes=[
            pltpu.VMEM((groups, rows, slot, LANES), jnp.float32),
            pltpu.VMEM((1, groups, TAPS * TAPS + 1, 8, LANES), jnp.float32),
        ],
        compiler_params=pltpu.CompilerParams(vmem_limit_bytes=16 * 2**20),
        name="middle",
    )(*[near(part) for part in parts], near(taps))


def run_blocks(edges, x, halos, taps, middles, mods, up, up_bias, down, down_bias, scale, tiles):
    lats, slot, channels = x.shape
    groups = channels // LANES
    rows = lats * slot * channels // LANES
    vmem = pl.BlockSpec(memory_space=pltpu.VMEM)
    arrays = (x, *halos, taps, *middles, mods, up_bias, down_bias, scale)
    wide_slot = slot + 8
    return pl.pallas_call(
        lambda *refs: blocks_kernel(*refs, tiles=tiles),
        out_shape=pltpu.VMEM((rows, LANES), jnp.bfloat16),
        in_specs=[pl.BlockSpec(memory_space=pltpu.SMEM)]
        + [vmem] * len(arrays)
        + [pl.BlockSpec(memory_space=pltpu.HBM)] * 2,
        scratch_shapes=[
            pltpu.VMEM((groups, lats + 4 * REACH, LEFT + wide_slot, LANES), jnp.float32),
            pltpu.VMEM((groups, lats + 2 * REACH, wide_slot, LANES), jnp.float32),
            pltpu.VMEM((up.shape[0], groups, TAPS * TAPS + 1, 8, LANES), jnp.float32),
            pltpu.VMEM((groups, lats + 2 * REACH, wide_slot, LANES), jnp.float32),
            pltpu.VMEM((groups, lats, slot, LANES), jnp.float32),
            pltpu.VMEM((rows, LANES), jnp.float32),
            pltpu.VMEM(up.shape, up.dtype),
            pltpu.VMEM(down.shape, down.dtype),
            pltpu.SemaphoreType.DMA((2,)),
        ],
        compiler_params=pltpu.CompilerParams(vmem_limit_bytes=40 * 2**20),
        name="blocks",
    )(edges, *[near(a) for a in arrays], far(up), far(down))


def halo_of(x, north, south, inner, seg):
    rows, segs = lax.axis_size("y"), lax.axis_size("xc")
    reach = 2 * REACH
    down = [(i, i + 1) for i in range(rows - 1)]
    up = [(j, i) for i, j in down]
    top = lax.ppermute(south, "y", down)
    bottom = lax.ppermute(north, "y", up)
    top, bottom, inner = lax.optimization_barrier((top, bottom, inner))
    east = [(i, (i + 1) % segs) for i in range(segs)]
    west = [(j, i) for i, j in east]

    def columns(lo):
        return jnp.concatenate(
            [part[:, lo : lo + reach] for part in (top, x, bottom)], axis=0
        )

    left = lax.ppermute(columns(seg - reach), "xc", east)
    right = lax.ppermute(columns(0), "xc", west)
    return (top, bottom, left, right), inner


def on_device(
    field, noise_level, conv_kernel, conv_bias, modulation,
    expand_weight, expand_bias, project_weight, project_bias, layer_scale,
):
    chans, members, lats, lons = field.shape
    layers = conv_kernel.shape[0]
    halves = lax.axis_size("zh")
    segs = lax.axis_size("xc")
    peers = halves * lax.axis_size("zl") * segs
    channels = chans * lax.axis_size("zl") * segs
    seg = lons // segs
    slot = -(-seg // 8) * 8
    tiles = lats * slot // LANES
    member = lax.axis_index("zh") * lax.axis_size("zl") + lax.axis_index("zl")
    mods = modulation[:, noise_level[member]].reshape(2 * layers, channels)
    band = lax.axis_index("y")
    edges = jnp.stack([band == 0, band == lax.axis_size("y") - 1]).astype(jnp.int32)

    layer = lax.axis_index("zh")
    filters = jnp.concatenate(
        [
            conv_kernel.reshape(layers, chans, TAPS * TAPS),
            conv_bias[:, :, None],
            jnp.zeros((layers, chans, HALF_LANES - TAPS * TAPS - 1), jnp.float32),
        ],
        axis=2,
    )
    filters = lax.dynamic_index_in_dim(filters, layer, 0, False).reshape(-1, LANES)
    pieces = run_cut(field, filters, seg, slot)
    around = ("zh", "zl", "xc")
    pairs = pieces.reshape(peers, -1, 2, LANES)
    pieces = lax.all_to_all(pairs, around, 0, 0, tiled=True).reshape(-1, LANES)
    shape = (peers, chans * tiles, LANES)
    cells = run_to_cells(
        pieces, halves * lats * slot, channels, tiles, 2 * REACH * slot, peers, layers
    )
    x, north, south = [part.reshape(-1, slot, channels) for part in cells[:3]]
    filters = cells[3]
    edge = 2 * REACH
    reads = x.shape[0] - edge
    cols = slot - 2 * 8
    inner = run_middle([x], filters, x.shape[0], [(0, reads)], cols)
    halos, inner = halo_of(x, north, south, inner, seg)
    parts = [halos[0], x, halos[1]]
    outer = run_middle(parts, filters, 4 * edge, [(0, edge), (2 * edge, edge)], cols)
    pieces = run_blocks(
        edges, x, halos, filters, (inner, outer), mods,
        expand_weight, expand_bias, project_weight, project_bias, layer_scale, tiles,
    )
    pieces = lax.all_to_all(pieces.reshape(shape), around, 0, 0, tiled=True).reshape(-1, LANES)
    return run_paste(pieces, field.shape, seg, slot)


def solution(mesh):
    bands, chan = mesh.shape["band"], mesh.shape["chan"]
    split = Mesh(mesh.devices.reshape(bands // 2, 2, chan // 8, 8), ("y", "zh", "zl", "xc"))
    band, group = ("y", "zh"), ("zl", "xc")
    return jax.shard_map(
        on_device,
        mesh=split,
        in_specs=(
            P(group, None, band, None),
            P(),
            P(None, group, None, None),
            P(None, group),
            P(), P(), P(), P(), P(), P(),
        ),
        out_specs=P(group, None, band, None),
        check_vma=False,
    )
```

```python
import jax
import jax.numpy as jnp
from jax import lax
from jax.experimental import pallas as pl
from jax.experimental.pallas import tpu as pltpu
from jax.sharding import Mesh, PartitionSpec as P

EPS = 1e-06
LANES = 128
TAPS = 7
REACH = 3
LEFT = 8
ROWS = 8
HALF_LANES = 64
TAP_ROWS = 56


def lane_iota(rows):
    return lax.broadcasted_iota(jnp.int32, (rows, LANES), 1)


def moved_lanes(load, spans, rows, rolled):
    lanes = lane_iota(rows)
    tile = None
    for source, src, dst, width in spans:
        done = 0
        while done < width:
            part, lane = divmod(src + done, LANES)
            take = min(width - done, LANES - lane)
            shift = (dst + done - lane) % LANES
            key = (source, part, shift)
            if key not in rolled:
                value = load(source, part)
                rolled[key] = pltpu.roll(value, shift, 1) if shift else value
            value = rolled[key]
            tile = value if tile is None else jnp.where(lanes >= dst + done, value, tile)
            done += take
    return tile


def spans_of(count, stride, width, tile_index, start_of):
    spans = []
    for item in range(count):
        lo = max(item * stride, tile_index * LANES)
        hi = min(item * stride + width, (tile_index + 1) * LANES)
        if lo < hi:
            spans.append((item, start_of(item) + lo - item * stride, lo - tile_index * LANES, hi - lo))
    return spans


def filter_lines(taps, bias):
    chans = bias.shape[1]
    lines = jnp.zeros((chans, LANES), jnp.float32)
    column = lax.broadcasted_iota(jnp.int32, (TAPS, LANES), 0)
    lane = lax.broadcasted_iota(jnp.int32, (TAPS, LANES), 1)
    for i in range(TAPS):
        place = (lane == i * TAPS + column).astype(jnp.float32).astype(jnp.bfloat16)
        lines = lines + jnp.dot(
            taps[i].astype(jnp.bfloat16), place, preferred_element_type=jnp.float32
        )
    square = (chans, chans)
    same = lax.broadcasted_iota(jnp.int32, square, 0) == lax.broadcasted_iota(jnp.int32, square, 1)
    diagonal = jnp.where(same, jnp.broadcast_to(bias, square), 0.0)
    own = jnp.sum(diagonal, axis=1, keepdims=True)
    lanes = lane_iota(chans)
    lines = jnp.where(lanes == TAPS * TAPS, jnp.broadcast_to(own, lines.shape), lines)
    turned = pltpu.roll(lines, HALF_LANES, 1)
    first = lane_iota(1) < HALF_LANES
    return [
        jnp.where(first, lines[c : c + 1], turned[c + 1 : c + 2]) for c in range(0, chans, 2)
    ]


def cut_kernel(layer_ref, field_ref, taps_ref, bias_ref, out_ref, wide, cut, *, seg, slot):
    chans, members, lats, lons = field_ref.shape
    rows = chans * members
    parts = -(-lons // LANES)
    segs = lons // seg
    tiles = lats * slot // LANES
    layer = layer_ref[0]
    bias = jnp.where(layer == 0, bias_ref[0:1, :], bias_ref[1:2, :])
    lines = filter_lines([taps_ref[layer, i] for i in range(TAPS)], bias)
    piece_rows = chans * tiles + len(lines)
    for e, line in enumerate(lines):
        cut[pl.ds(chans * tiles + e, members * segs, stride=piece_rows), :] = jnp.broadcast_to(
            line, (members * segs, LANES)
        )
    for a in range(parts):
        lo, hi = a * LANES, min((a + 1) * LANES, lons)
        piece = field_ref[:, :, :, lo:hi].astype(jnp.float32).reshape(rows * lats, hi - lo)
        wide[a, :, 0 : hi - lo] = piece
        if hi - lo < LANES:
            wide[a, :, hi - lo :] = jnp.zeros((rows * lats, LANES - hi + lo), jnp.float32)
    for s in range(segs):
        rolled = {}
        for t in range(tiles):
            spans = spans_of(lats, slot, seg, t, lambda item: s * seg)

            def load(lat, part):
                return wide[part, pl.ds(lat, rows, stride=lats), :]

            tile = moved_lanes(load, spans, rows, rolled)
            for c in range(chans):
                start = s * piece_rows + c * tiles + t
                cut[pl.ds(start, members, stride=segs * piece_rows), :] = tile[
                    c * members : (c + 1) * members
                ]
    out_ref[...] = cut[...].astype(jnp.bfloat16)


def paste_kernel(in_ref, out_ref, cut, wide, *, seg, slot):
    chans, members, lats, lons = out_ref.shape
    rows = chans * members
    parts = -(-lons // LANES)
    segs = lons // seg
    tiles = lats * slot // LANES
    cut[...] = in_ref[...].astype(jnp.float32)
    for lat in range(lats):
        rolled = {}
        for a in range(parts):
            spans = spans_of(segs, seg, seg, a, lambda item: lat * slot)

            def load(s, part):
                return jnp.concatenate(
                    [
                        cut[
                            pl.ds(
                                s * chans * tiles + c * tiles + part,
                                members,
                                stride=segs * chans * tiles,
                            ),
                            :,
                        ]
                        for c in range(chans)
                    ],
                    axis=0,
                )

            wide[a, pl.ds(lat, rows, stride=lats), :] = moved_lanes(load, spans, rows, rolled)
    for a in range(parts):
        lo, hi = a * LANES, min((a + 1) * LANES, lons)
        out_ref[:, :, :, lo:hi] = (
            wide[a, :, 0 : hi - lo].reshape(chans, members, lats, hi - lo).astype(jnp.bfloat16)
        )


def to_cells_kernel(
    in_ref, out_ref, north_ref, south_ref, taps_ref, raw, rows32, *, tiles, sources
):
    cells, channels = out_ref.shape
    halves = taps_ref.shape[0]
    data = rows32.shape[0]
    piece_rows = in_ref.shape[0] // sources
    data_rows = data // sources
    raw[...] = in_ref[...].astype(jnp.float32)
    for src in range(sources):
        rows32[src * data_rows : (src + 1) * data_rows, :] = raw[
            src * piece_rows : src * piece_rows + data_rows, :
        ]
    for half in range(halves):
        for t in range(tiles):
            block = rows32[pl.ds(half * channels * tiles + t, channels, stride=tiles), :]
            start = (half * tiles + t) * LANES
            out_ref[start : start + LANES, :] = block.T.astype(jnp.bfloat16)
    edge = north_ref.shape[0]
    north_ref[...] = out_ref[0:edge, :]
    south_ref[...] = out_ref[cells - edge :, :]
    owners = sources // halves
    chans = channels // owners
    taps = taps_ref.shape[1]
    owner = lax.broadcasted_iota(jnp.int32, (owners, channels), 0)
    channel = lax.broadcasted_iota(jnp.int32, (owners, channels), 1)
    for half in range(halves):
        total = jnp.zeros((taps, channels), jnp.float32)
        for e in range(piece_rows - data_rows):
            start = half * owners * piece_rows + data_rows + e
            lines = raw[pl.ds(start, owners, stride=piece_rows), :].T.astype(jnp.bfloat16)
            for k in range(2):
                place = (channel == owner * chans + 2 * e + k).astype(jnp.float32)
                spread = jnp.dot(
                    lines, place.astype(jnp.bfloat16), preferred_element_type=jnp.float32
                )
                total = total + spread[k * HALF_LANES : k * HALF_LANES + taps, :]
        taps_ref[half] = total


def depthwise(source, spread, mixed, layer, bands, tiles, first_col):
    packed = mixed.shape[1] == sum(count for _, count in bands)
    for k in tiles:

        def step_of(g, carry):
            def column_of(j, sums):
                sums = list(sums)
                weights = [spread[layer, g, i * TAPS + j] for i in range(TAPS)]
                at = 0
                for start, count in bands:
                    for r in range(count + TAPS - 1):
                        value = source[g, start + r, pl.ds(first_col + 8 * k + j, 8), :]
                        for i in range(TAPS):
                            if 0 <= r - i < count:
                                sums[at + r - i] = sums[at + r - i] + weights[i] * value
                    at += count
                return tuple(sums)

            total = sum(count for _, count in bands)
            sums = lax.fori_loop(0, TAPS, column_of, (spread[layer, g, TAPS * TAPS],) * total)
            at = 0
            for start, count in bands:
                for r in range(count):
                    row = at if packed else start + r
                    mixed[g, row, 8 * k : 8 * k + 8, :] = sums[at]
                    at += 1
            return carry

        lax.fori_loop(0, source.shape[0], step_of, 0)


def spread_taps(spread, taps_ref, layers):
    for g in range(spread.shape[1]):
        ch = slice(g * LANES, (g + 1) * LANES)
        for layer in range(layers):
            for k in range(TAPS * TAPS + 1):
                spread[layer, g, k] = jnp.broadcast_to(taps_ref[layer, k : k + 1, ch], (8, LANES))


def middle_kernel(*refs, bands, tiles):
    *part_refs, taps_ref, out_ref, source, spread = refs
    for g in range(source.shape[0]):
        row = 0
        for part_ref, lo, hi in part_refs_of(part_refs, source.shape[1]):
            ch = slice(g * LANES, (g + 1) * LANES)
            source[g, row : row + hi - lo, :, :] = part_ref[lo:hi, :, ch].astype(jnp.float32)
            row += hi - lo
    spread_taps(spread, taps_ref, 1)
    depthwise(source, spread, out_ref, 0, bands, range(tiles), 8 - 2 * REACH)


def part_refs_of(part_refs, rows):
    if len(part_refs) == 1:
        return [(part_refs[0], 0, rows)]
    top_ref, x_ref, bottom_ref = part_refs
    edge, lats = top_ref.shape[0], x_ref.shape[0]
    return [(top_ref, 0, edge), (x_ref, 0, edge), (x_ref, lats - edge, lats), (bottom_ref, 0, edge)]


def pointwise(mixed, layer, lats, slot, residual, store, weights):
    mod_ref, up_ref, up_bias_ref, down_ref, down_bias_ref, scale_ref = weights
    groups = mixed.shape[0]
    channels = groups * LANES
    cells = ROWS * slot
    steps = -(-lats // ROWS)
    average_matrix = jnp.full((channels, channels), 1.0 / channels, jnp.bfloat16)

    def step_of(step, carry):
        row = jnp.minimum(step * ROWS, lats - ROWS)
        parts = [mixed[g, pl.ds(row, ROWS), 0:slot, :].reshape(cells, LANES) for g in range(groups)]
        rounded = jnp.concatenate(parts, axis=1).astype(jnp.bfloat16)
        average = jnp.dot(rounded, average_matrix, preferred_element_type=jnp.float32)
        centered = rounded.astype(jnp.float32) - average
        variance = jnp.mean(centered * centered, axis=1, keepdims=True)
        gain = 1.0 + mod_ref[2 * layer : 2 * layer + 1, :]
        shift = mod_ref[2 * layer + 1 : 2 * layer + 2, :]
        normed = (centered * lax.rsqrt(variance + EPS) * gain + shift).astype(jnp.bfloat16)
        hidden = (
            jnp.dot(normed, up_ref[layer], preferred_element_type=jnp.float32)
            + up_bias_ref[layer : layer + 1, :]
        )
        doubled = (hidden * (1.0 + lax.erf(hidden * 0.7071067811865476))).astype(jnp.bfloat16)
        result = (
            0.5 * jnp.dot(doubled, down_ref[layer], preferred_element_type=jnp.float32)
            + down_bias_ref[layer : layer + 1, :]
        )
        branch = (scale_ref[layer : layer + 1, :] * result).astype(jnp.bfloat16).astype(jnp.float32)
        for g in range(groups):
            part = branch[:, g * LANES : (g + 1) * LANES].reshape(ROWS, slot, LANES)
            store(g, row, (residual(g, row) + part).astype(jnp.bfloat16).astype(jnp.float32))
        return carry

    lax.fori_loop(0, steps, step_of, 0)


def blocks_kernel(
    edge_ref, x_ref, top_ref, bottom_ref, left_ref, right_ref, taps_ref, inner_ref, outer_ref, mod_ref,
    up_bias_ref, down_bias_ref, scale_ref, up_hbm, down_hbm,
    out_ref, first, second, spread, mixed, final, rows32, up_ref, down_ref, arrived, *, tiles,
):
    lats, slot, channels = x_ref.shape
    groups = channels // LANES
    reach = 2 * REACH
    wide = lats + reach
    right_at = LEFT + slot - REACH
    copies = [
        pltpu.make_async_copy(up_hbm, up_ref, arrived.at[0]),
        pltpu.make_async_copy(down_hbm, down_ref, arrived.at[1]),
    ]
    for copy in copies:
        copy.start()
    for g in range(groups):
        ch = slice(g * LANES, (g + 1) * LANES)
        first[g, 0:reach, LEFT : LEFT + slot, :] = top_ref[:, :, ch].astype(jnp.float32)
        first[g, reach : reach + lats, LEFT : LEFT + slot, :] = x_ref[:, :, ch].astype(jnp.float32)
        first[g, reach + lats :, LEFT : LEFT + slot, :] = bottom_ref[:, :, ch].astype(jnp.float32)
        first[g, :, LEFT + slot :, :] = jnp.zeros(
            (lats + 2 * reach, first.shape[2] - LEFT - slot, LANES), jnp.float32
        )
        first[g, :, LEFT - reach : LEFT, :] = left_ref[:, :, ch].astype(jnp.float32)
        first[g, :, right_at : right_at + reach, :] = right_ref[:, :, ch].astype(jnp.float32)
        middle = slice(8, 8 + inner_ref.shape[2])
        mixed[g, 0:reach, middle, :] = outer_ref[g, 0:reach]
        mixed[g, reach:lats, middle, :] = inner_ref[g]
        mixed[g, lats:wide, middle, :] = outer_ref[g, reach:]
    spread_taps(spread, taps_ref, taps_ref.shape[0])
    weights = (mod_ref, up_ref, up_bias_ref, down_ref, down_bias_ref, scale_ref)

    wide_slot = slot + 8
    covered = inner_ref.shape[2] // 8
    sides = [k for k in range(wide_slot // 8) if not 1 <= k <= covered]
    depthwise(first, spread, mixed, 0, [(0, wide // 2)], sides, LEFT - reach)
    depthwise(first, spread, mixed, 0, [(wide // 2, wide - wide // 2)], sides, LEFT - reach)

    for copy in copies:
        copy.wait()

    def first_store(g, row, value):
        second[g, pl.ds(row, ROWS), :, :] = value

    pointwise(
        mixed, 0, wide, wide_slot,
        lambda g, row: first[g, pl.ds(row + REACH, ROWS), LEFT - REACH : LEFT - REACH + wide_slot, :],
        first_store, weights,
    )

    @pl.when(edge_ref[0] == 1)
    def _():
        second[:, 0:REACH, :, :] = jnp.zeros((groups, REACH, wide_slot, LANES), jnp.float32)

    @pl.when(edge_ref[1] == 1)
    def _():
        second[:, REACH + lats :, :, :] = jnp.zeros((groups, REACH, wide_slot, LANES), jnp.float32)

    depthwise(second, spread, mixed, 1, [(0, lats)], range(slot // 8), 0)

    def final_store(g, row, value):
        final[g, pl.ds(row, ROWS), :, :] = value

    pointwise(
        mixed, 1, lats, slot,
        lambda g, row: second[g, pl.ds(row + REACH, ROWS), REACH : REACH + slot, :],
        final_store, weights,
    )
    flat = lats * slot // tiles // LANES
    rows_per = LANES * 3 // slot
    for half in range(flat):
        for g in range(groups):
            for part in range(tiles // 3):
                lat = (half * tiles + part * 3) * LANES // slot
                block = final[g, lat : lat + rows_per, :, :].reshape(rows_per * slot, LANES)
                for t in range(3):
                    start = half * channels * tiles + g * LANES * tiles + part * 3 + t
                    rows32[pl.ds(start, LANES, stride=tiles), :] = block[
                        t * LANES : (t + 1) * LANES
                    ].T
    out_ref[...] = rows32[...].astype(jnp.bfloat16)


def near(x):
    return pltpu.with_memory_space_constraint(x, pltpu.VMEM)


def far(x):
    return pltpu.with_memory_space_constraint(x, pltpu.HBM)


def run_cut(layer, field, taps, bias, seg, slot):
    chans, members, lats, lons = field.shape
    tiles = lats * slot // LANES
    rows = members * (lons // seg) * (chans * tiles + chans // 2)
    return pl.pallas_call(
        lambda *refs: cut_kernel(*refs, seg=seg, slot=slot),
        out_shape=pltpu.VMEM((rows, LANES), jnp.bfloat16),
        in_specs=[pl.BlockSpec(memory_space=pltpu.SMEM)]
        + [pl.BlockSpec(memory_space=pltpu.VMEM)] * 3,
        scratch_shapes=[
            pltpu.VMEM((-(-lons // LANES), chans * members * lats, LANES), jnp.float32),
            pltpu.VMEM((rows, LANES), jnp.float32),
        ],
        name="cut",
    )(layer, field, taps, bias)


def run_paste(pieces, shape, seg, slot):
    chans, members, lats, lons = shape
    return pl.pallas_call(
        lambda *refs: paste_kernel(*refs, seg=seg, slot=slot),
        out_shape=jax.ShapeDtypeStruct(shape, jnp.bfloat16),
        scratch_shapes=[
            pltpu.VMEM(pieces.shape, jnp.float32),
            pltpu.VMEM((-(-lons // LANES), chans * members * lats, LANES), jnp.float32),
        ],
        name="paste",
    )(near(pieces))


def run_to_cells(pieces, cells, channels, tiles, edge, sources, layers):
    outs = [(cells, channels), (edge, channels), (edge, channels)]
    return pl.pallas_call(
        lambda *refs: to_cells_kernel(*refs, tiles=tiles, sources=sources),
        out_shape=[pltpu.VMEM(out, jnp.bfloat16) for out in outs]
        + [pltpu.VMEM((layers, TAP_ROWS, channels), jnp.float32)],
        scratch_shapes=[
            pltpu.VMEM(pieces.shape, jnp.float32),
            pltpu.VMEM((cells * channels // LANES, LANES), jnp.float32),
        ],
        name="to_cells",
    )(near(pieces))


def run_middle(parts, taps, rows, bands, cols):
    slot, channels = parts[0].shape[1:]
    groups = channels // LANES
    total = sum(count for _, count in bands)
    return pl.pallas_call(
        lambda *refs: middle_kernel(*refs, bands=bands, tiles=cols // 8),
        out_shape=pltpu.VMEM((groups, total, cols, LANES), jnp.float32),
        scratch_shapes=[
            pltpu.VMEM((groups, rows, slot, LANES), jnp.float32),
            pltpu.VMEM((1, groups, TAPS * TAPS + 1, 8, LANES), jnp.float32),
        ],
        compiler_params=pltpu.CompilerParams(vmem_limit_bytes=16 * 2**20),
        name="middle",
    )(*[near(part) for part in parts], near(taps))


def run_blocks(edges, x, halos, taps, middles, mods, up, up_bias, down, down_bias, scale, tiles):
    lats, slot, channels = x.shape
    groups = channels // LANES
    rows = lats * slot * channels // LANES
    vmem = pl.BlockSpec(memory_space=pltpu.VMEM)
    arrays = (x, *halos, taps, *middles, mods, up_bias, down_bias, scale)
    wide_slot = slot + 8
    return pl.pallas_call(
        lambda *refs: blocks_kernel(*refs, tiles=tiles),
        out_shape=pltpu.VMEM((rows, LANES), jnp.bfloat16),
        in_specs=[pl.BlockSpec(memory_space=pltpu.SMEM)]
        + [vmem] * len(arrays)
        + [pl.BlockSpec(memory_space=pltpu.HBM)] * 2,
        scratch_shapes=[
            pltpu.VMEM((groups, lats + 4 * REACH, LEFT + wide_slot, LANES), jnp.float32),
            pltpu.VMEM((groups, lats + 2 * REACH, wide_slot, LANES), jnp.float32),
            pltpu.VMEM((up.shape[0], groups, TAPS * TAPS + 1, 8, LANES), jnp.float32),
            pltpu.VMEM((groups, lats + 2 * REACH, wide_slot, LANES), jnp.float32),
            pltpu.VMEM((groups, lats, slot, LANES), jnp.float32),
            pltpu.VMEM((rows, LANES), jnp.float32),
            pltpu.VMEM(up.shape, up.dtype),
            pltpu.VMEM(down.shape, down.dtype),
            pltpu.SemaphoreType.DMA((2,)),
        ],
        compiler_params=pltpu.CompilerParams(vmem_limit_bytes=40 * 2**20),
        name="blocks",
    )(edges, *[near(a) for a in arrays], far(up), far(down))


def halo_of(x, north, south, inner, seg):
    rows, segs = lax.axis_size("y"), lax.axis_size("xc")
    reach = 2 * REACH
    down = [(i, i + 1) for i in range(rows - 1)]
    up = [(j, i) for i, j in down]
    top = lax.ppermute(south, "y", down)
    bottom = lax.ppermute(north, "y", up)
    top, bottom, inner = lax.optimization_barrier((top, bottom, inner))
    east = [(i, (i + 1) % segs) for i in range(segs)]
    west = [(j, i) for i, j in east]

    def columns(lo):
        return jnp.concatenate(
            [part[:, lo : lo + reach] for part in (top, x, bottom)], axis=0
        )

    left = lax.ppermute(columns(seg - reach), "xc", east)
    right = lax.ppermute(columns(0), "xc", west)
    return (top, bottom, left, right), inner


def on_device(
    field, noise_level, conv_kernel, conv_bias, modulation,
    expand_weight, expand_bias, project_weight, project_bias, layer_scale,
):
    chans, members, lats, lons = field.shape
    layers = conv_kernel.shape[0]
    halves = lax.axis_size("zh")
    segs = lax.axis_size("xc")
    peers = halves * lax.axis_size("zl") * segs
    channels = chans * lax.axis_size("zl") * segs
    seg = lons // segs
    slot = -(-seg // 8) * 8
    tiles = lats * slot // LANES
    member = lax.axis_index("zh") * lax.axis_size("zl") + lax.axis_index("zl")
    mods = modulation[:, noise_level[member]].reshape(2 * layers, channels)
    band = lax.axis_index("y")
    edges = jnp.stack([band == 0, band == lax.axis_size("y") - 1]).astype(jnp.int32)

    layer = lax.axis_index("zh").astype(jnp.int32).reshape(1)
    pieces = run_cut(layer, field, conv_kernel.transpose(0, 2, 1, 3), conv_bias, seg, slot)
    around = ("zh", "zl", "xc")
    pairs = pieces.reshape(peers, -1, 2, LANES)
    pieces = lax.all_to_all(pairs, around, 0, 0, tiled=True).reshape(-1, LANES)
    shape = (peers, chans * tiles, LANES)
    cells = run_to_cells(
        pieces, halves * lats * slot, channels, tiles, 2 * REACH * slot, peers, layers
    )
    x, north, south = [part.reshape(-1, slot, channels) for part in cells[:3]]
    filters = cells[3]
    edge = 2 * REACH
    reads = x.shape[0] - edge
    cols = slot - 2 * 8
    inner = run_middle([x], filters, x.shape[0], [(0, reads)], cols)
    halos, inner = halo_of(x, north, south, inner, seg)
    parts = [halos[0], x, halos[1]]
    outer = run_middle(parts, filters, 4 * edge, [(0, edge), (2 * edge, edge)], cols)
    pieces = run_blocks(
        edges, x, halos, filters, (inner, outer), mods,
        expand_weight, expand_bias, project_weight, project_bias, layer_scale, tiles,
    )
    pieces = lax.all_to_all(pieces.reshape(shape), around, 0, 0, tiled=True).reshape(-1, LANES)
    return run_paste(pieces, field.shape, seg, slot)


def solution(mesh):
    bands, chan = mesh.shape["band"], mesh.shape["chan"]
    split = Mesh(mesh.devices.reshape(bands // 2, 2, chan // 8, 8), ("y", "zh", "zl", "xc"))
    band, group = ("y", "zh"), ("zl", "xc")
    return jax.shard_map(
        on_device,
        mesh=split,
        in_specs=(
            P(group, None, band, None),
            P(),
            P(None, group, None, None),
            P(None, group),
            P(), P(), P(), P(), P(), P(),
        ),
        out_specs=P(group, None, band, None),
        check_vma=False,
    )
```

```python
import jax
import jax.numpy as jnp
from jax import lax
from jax.experimental import pallas as pl
from jax.experimental.pallas import tpu as pltpu
from jax.sharding import Mesh, PartitionSpec as P

EPS = 1e-06
LANES = 128
TAPS = 7
REACH = 3
LEFT = 8
HALF_LANES = 64
TAP_ROWS = 56


def lane_iota(rows):
    return lax.broadcasted_iota(jnp.int32, (rows, LANES), 1)


def moved_lanes(load, spans, rows, rolled):
    lanes = lane_iota(rows)
    tile = None
    for source, src, dst, width in spans:
        done = 0
        while done < width:
            part, lane = divmod(src + done, LANES)
            take = min(width - done, LANES - lane)
            shift = (dst + done - lane) % LANES
            key = (source, part, shift)
            if key not in rolled:
                value = load(source, part)
                rolled[key] = pltpu.roll(value, shift, 1) if shift else value
            value = rolled[key]
            tile = value if tile is None else jnp.where(lanes >= dst + done, value, tile)
            done += take
    return tile


def spans_of(count, stride, width, tile_index, start_of):
    spans = []
    for item in range(count):
        lo = max(item * stride, tile_index * LANES)
        hi = min(item * stride + width, (tile_index + 1) * LANES)
        if lo < hi:
            spans.append((item, start_of(item) + lo - item * stride, lo - tile_index * LANES, hi - lo))
    return spans


def filter_lines(taps, bias):
    chans = bias.shape[1]
    lines = jnp.zeros((chans, LANES), jnp.float32)
    column = lax.broadcasted_iota(jnp.int32, (TAPS, LANES), 0)
    lane = lax.broadcasted_iota(jnp.int32, (TAPS, LANES), 1)
    for i in range(TAPS):
        place = (lane == i * TAPS + column).astype(jnp.float32).astype(jnp.bfloat16)
        lines = lines + jnp.dot(
            taps[i].astype(jnp.bfloat16), place, preferred_element_type=jnp.float32
        )
    square = (chans, chans)
    same = lax.broadcasted_iota(jnp.int32, square, 0) == lax.broadcasted_iota(jnp.int32, square, 1)
    diagonal = jnp.where(same, jnp.broadcast_to(bias, square), 0.0)
    own = jnp.sum(diagonal, axis=1, keepdims=True)
    lanes = lane_iota(chans)
    lines = jnp.where(lanes == TAPS * TAPS, jnp.broadcast_to(own, lines.shape), lines)
    turned = pltpu.roll(lines, HALF_LANES, 1)
    first = lane_iota(1) < HALF_LANES
    return [
        jnp.where(first, lines[c : c + 1], turned[c + 1 : c + 2]) for c in range(0, chans, 2)
    ]


def cut_kernel(layer_ref, field_ref, taps_ref, bias_ref, out_ref, wide, cut, *, seg, slot):
    chans, members, lats, lons = field_ref.shape
    rows = chans * members
    parts = -(-lons // LANES)
    segs = lons // seg
    tiles = lats * slot // LANES
    layer = layer_ref[0]
    bias = jnp.where(layer == 0, bias_ref[0:1, :], bias_ref[1:2, :])
    lines = filter_lines([taps_ref[layer, i] for i in range(TAPS)], bias)
    piece_rows = chans * tiles + len(lines)
    for e, line in enumerate(lines):
        cut[pl.ds(chans * tiles + e, members * segs, stride=piece_rows), :] = jnp.broadcast_to(
            line, (members * segs, LANES)
        )
    for a in range(parts):
        lo, hi = a * LANES, min((a + 1) * LANES, lons)
        piece = field_ref[:, :, :, lo:hi].astype(jnp.float32).reshape(rows * lats, hi - lo)
        wide[a, :, 0 : hi - lo] = piece
        if hi - lo < LANES:
            wide[a, :, hi - lo :] = jnp.zeros((rows * lats, LANES - hi + lo), jnp.float32)
    for s in range(segs):
        rolled = {}
        for t in range(tiles):
            spans = spans_of(lats, slot, seg, t, lambda item: s * seg)

            def load(lat, part):
                return wide[part, pl.ds(lat, rows, stride=lats), :]

            tile = moved_lanes(load, spans, rows, rolled)
            for c in range(chans):
                start = s * piece_rows + c * tiles + t
                cut[pl.ds(start, members, stride=segs * piece_rows), :] = tile[
                    c * members : (c + 1) * members
                ]
    out_ref[...] = cut[...].astype(jnp.bfloat16)


def paste_kernel(in_ref, out_ref, cut, wide, *, seg, slot):
    chans, members, lats, lons = out_ref.shape
    rows = chans * members
    parts = -(-lons // LANES)
    segs = lons // seg
    tiles = lats * slot // LANES
    cut[...] = in_ref[...].astype(jnp.float32)
    for lat in range(lats):
        rolled = {}
        for a in range(parts):
            spans = spans_of(segs, seg, seg, a, lambda item: lat * slot)

            def load(s, part):
                return jnp.concatenate(
                    [
                        cut[
                            pl.ds(
                                s * chans * tiles + c * tiles + part,
                                members,
                                stride=segs * chans * tiles,
                            ),
                            :,
                        ]
                        for c in range(chans)
                    ],
                    axis=0,
                )

            wide[a, pl.ds(lat, rows, stride=lats), :] = moved_lanes(load, spans, rows, rolled)
    for a in range(parts):
        lo, hi = a * LANES, min((a + 1) * LANES, lons)
        out_ref[:, :, :, lo:hi] = (
            wide[a, :, 0 : hi - lo].reshape(chans, members, lats, hi - lo).astype(jnp.bfloat16)
        )


def to_cells_kernel(
    in_ref, out_ref, north_ref, south_ref, taps_ref, raw, rows32, *, tiles, sources
):
    cells, channels = out_ref.shape
    halves = taps_ref.shape[0]
    data = rows32.shape[0]
    piece_rows = in_ref.shape[0] // sources
    data_rows = data // sources
    raw[...] = in_ref[...].astype(jnp.float32)
    for src in range(sources):
        rows32[src * data_rows : (src + 1) * data_rows, :] = raw[
            src * piece_rows : src * piece_rows + data_rows, :
        ]
    for half in range(halves):
        for t in range(tiles):
            block = rows32[pl.ds(half * channels * tiles + t, channels, stride=tiles), :]
            start = (half * tiles + t) * LANES
            out_ref[start : start + LANES, :] = block.T.astype(jnp.bfloat16)
    edge = north_ref.shape[0]
    north_ref[...] = out_ref[0:edge, :]
    south_ref[...] = out_ref[cells - edge :, :]
    owners = sources // halves
    chans = channels // owners
    taps = taps_ref.shape[1]
    owner = lax.broadcasted_iota(jnp.int32, (owners, channels), 0)
    channel = lax.broadcasted_iota(jnp.int32, (owners, channels), 1)
    for half in range(halves):
        total = jnp.zeros((taps, channels), jnp.float32)
        for e in range(piece_rows - data_rows):
            start = half * owners * piece_rows + data_rows + e
            lines = raw[pl.ds(start, owners, stride=piece_rows), :].T.astype(jnp.bfloat16)
            for k in range(2):
                place = (channel == owner * chans + 2 * e + k).astype(jnp.float32)
                spread = jnp.dot(
                    lines, place.astype(jnp.bfloat16), preferred_element_type=jnp.float32
                )
                total = total + spread[k * HALF_LANES : k * HALF_LANES + taps, :]
        taps_ref[half] = total


def depthwise(source, spread, mixed, layer, bands, tiles, first_col):
    packed = mixed.shape[1] == sum(count for _, count in bands)
    for k in tiles:

        def step_of(g, carry):
            def column_of(j, sums):
                sums = list(sums)
                weights = [spread[layer, g, i * TAPS + j] for i in range(TAPS)]
                at = 0
                for start, count in bands:
                    for r in range(count + TAPS - 1):
                        value = source[g, start + r, pl.ds(first_col + 8 * k + j, 8), :]
                        for i in range(TAPS):
                            if 0 <= r - i < count:
                                sums[at + r - i] = sums[at + r - i] + weights[i] * value
                    at += count
                return tuple(sums)

            total = sum(count for _, count in bands)
            sums = lax.fori_loop(0, TAPS, column_of, (spread[layer, g, TAPS * TAPS],) * total)
            at = 0
            for start, count in bands:
                for r in range(count):
                    row = at if packed else start + r
                    mixed[g, row, 8 * k : 8 * k + 8, :] = sums[at]
                    at += 1
            return carry

        lax.fori_loop(0, source.shape[0], step_of, 0)


def spread_taps(spread, taps_ref, layers):
    for g in range(spread.shape[1]):
        ch = slice(g * LANES, (g + 1) * LANES)
        for layer in range(layers):
            for k in range(TAPS * TAPS + 1):
                spread[layer, g, k] = jnp.broadcast_to(taps_ref[layer, k : k + 1, ch], (8, LANES))


def middle_kernel(*refs, bands, tiles):
    *part_refs, taps_ref, out_ref, source, spread = refs
    for g in range(source.shape[0]):
        row = 0
        for part_ref, lo, hi in part_refs_of(part_refs, source.shape[1]):
            ch = slice(g * LANES, (g + 1) * LANES)
            source[g, row : row + hi - lo, :, :] = part_ref[lo:hi, :, ch].astype(jnp.float32)
            row += hi - lo
    spread_taps(spread, taps_ref, 1)
    depthwise(source, spread, out_ref, 0, bands, range(tiles), 8 - 2 * REACH)


def part_refs_of(part_refs, rows):
    if len(part_refs) == 1:
        return [(part_refs[0], 0, rows)]
    top_ref, x_ref, bottom_ref = part_refs
    edge, lats = top_ref.shape[0], x_ref.shape[0]
    return [(top_ref, 0, edge), (x_ref, 0, edge), (x_ref, lats - edge, lats), (bottom_ref, 0, edge)]


def pointwise(mixed, layer, lats, rows, slot, residual, store, weights):
    mod_ref, up_ref, up_bias_ref, down_ref, down_bias_ref, scale_ref = weights
    groups = mixed.shape[0]
    channels = groups * LANES
    cells = rows * slot
    steps = -(-lats // rows)
    average_matrix = jnp.full((channels, channels), 1.0 / channels, jnp.bfloat16)

    def step_of(step, carry):
        row = jnp.minimum(step * rows, lats - rows)
        parts = [mixed[g, pl.ds(row, rows), 0:slot, :].reshape(cells, LANES) for g in range(groups)]
        rounded = jnp.concatenate(parts, axis=1).astype(jnp.bfloat16)
        average = jnp.dot(rounded, average_matrix, preferred_element_type=jnp.float32)
        centered = rounded.astype(jnp.float32) - average
        variance = jnp.mean(centered * centered, axis=1, keepdims=True)
        gain = 1.0 + mod_ref[2 * layer : 2 * layer + 1, :]
        shift = mod_ref[2 * layer + 1 : 2 * layer + 2, :]
        normed = (centered * lax.rsqrt(variance + EPS) * gain + shift).astype(jnp.bfloat16)
        hidden = (
            jnp.dot(normed, up_ref[layer], preferred_element_type=jnp.float32)
            + up_bias_ref[layer : layer + 1, :]
        )
        doubled = (hidden * (1.0 + lax.erf(hidden * 0.7071067811865476))).astype(jnp.bfloat16)
        result = (
            0.5 * jnp.dot(doubled, down_ref[layer], preferred_element_type=jnp.float32)
            + down_bias_ref[layer : layer + 1, :]
        )
        branch = (scale_ref[layer : layer + 1, :] * result).astype(jnp.bfloat16).astype(jnp.float32)
        for g in range(groups):
            part = branch[:, g * LANES : (g + 1) * LANES].reshape(rows, slot, LANES)
            store(g, row, (residual(g, row) + part).astype(jnp.bfloat16).astype(jnp.float32))
        return carry

    lax.fori_loop(0, steps, step_of, 0)


def blocks_kernel(
    edge_ref, x_ref, top_ref, bottom_ref, left_ref, right_ref, taps_ref, inner_ref, outer_ref, mod_ref,
    up_bias_ref, down_bias_ref, scale_ref, up_hbm, down_hbm,
    out_ref, first, second, spread, mixed, final, rows32, up_ref, down_ref, arrived, *, tiles,
):
    lats, slot, channels = x_ref.shape
    groups = channels // LANES
    reach = 2 * REACH
    wide = lats + reach
    right_at = LEFT + slot - REACH
    copies = [
        pltpu.make_async_copy(up_hbm, up_ref, arrived.at[0]),
        pltpu.make_async_copy(down_hbm, down_ref, arrived.at[1]),
    ]
    for copy in copies:
        copy.start()
    for g in range(groups):
        ch = slice(g * LANES, (g + 1) * LANES)
        first[g, 0:reach, LEFT : LEFT + slot, :] = top_ref[:, :, ch].astype(jnp.float32)
        first[g, reach : reach + lats, LEFT : LEFT + slot, :] = x_ref[:, :, ch].astype(jnp.float32)
        first[g, reach + lats :, LEFT : LEFT + slot, :] = bottom_ref[:, :, ch].astype(jnp.float32)
        first[g, :, LEFT + slot :, :] = jnp.zeros(
            (lats + 2 * reach, first.shape[2] - LEFT - slot, LANES), jnp.float32
        )
        first[g, :, LEFT - reach : LEFT, :] = left_ref[:, :, ch].astype(jnp.float32)
        first[g, :, right_at : right_at + reach, :] = right_ref[:, :, ch].astype(jnp.float32)
        middle = slice(8, 8 + inner_ref.shape[2])
        mixed[g, 0:reach, middle, :] = outer_ref[g, 0:reach]
        mixed[g, reach:lats, middle, :] = inner_ref[g]
        mixed[g, lats:wide, middle, :] = outer_ref[g, reach:]
    spread_taps(spread, taps_ref, taps_ref.shape[0])
    weights = (mod_ref, up_ref, up_bias_ref, down_ref, down_bias_ref, scale_ref)

    wide_slot = slot + 8
    covered = inner_ref.shape[2] // 8
    sides = [k for k in range(wide_slot // 8) if not 1 <= k <= covered]
    depthwise(first, spread, mixed, 0, [(0, wide // 2)], sides, LEFT - reach)
    depthwise(first, spread, mixed, 0, [(wide // 2, wide - wide // 2)], sides, LEFT - reach)

    for copy in copies:
        copy.wait()

    def first_store(g, row, value):
        second[g, pl.ds(row, 19), :, :] = value

    pointwise(
        mixed, 0, wide, 19, wide_slot,
        lambda g, row: first[g, pl.ds(row + REACH, 19), LEFT - REACH : LEFT - REACH + wide_slot, :],
        first_store, weights,
    )

    @pl.when(edge_ref[0] == 1)
    def _():
        second[:, 0:REACH, :, :] = jnp.zeros((groups, REACH, wide_slot, LANES), jnp.float32)

    @pl.when(edge_ref[1] == 1)
    def _():
        second[:, REACH + lats :, :, :] = jnp.zeros((groups, REACH, wide_slot, LANES), jnp.float32)

    depthwise(second, spread, mixed, 1, [(0, lats)], range(slot // 8), 0)

    def final_store(g, row, value):
        final[g, pl.ds(row, 32), :, :] = value

    pointwise(
        mixed, 1, lats, 32, slot,
        lambda g, row: second[g, pl.ds(row + REACH, 32), REACH : REACH + slot, :],
        final_store, weights,
    )
    flat = lats * slot // tiles // LANES
    rows_per = LANES * 3 // slot
    for half in range(flat):
        for g in range(groups):
            for part in range(tiles // 3):
                lat = (half * tiles + part * 3) * LANES // slot
                block = final[g, lat : lat + rows_per, :, :].reshape(rows_per * slot, LANES)
                for t in range(3):
                    start = half * channels * tiles + g * LANES * tiles + part * 3 + t
                    rows32[pl.ds(start, LANES, stride=tiles), :] = block[
                        t * LANES : (t + 1) * LANES
                    ].T
    out_ref[...] = rows32[...].astype(jnp.bfloat16)


def near(x):
    return pltpu.with_memory_space_constraint(x, pltpu.VMEM)


def far(x):
    return pltpu.with_memory_space_constraint(x, pltpu.HBM)


def run_cut(layer, field, taps, bias, seg, slot):
    chans, members, lats, lons = field.shape
    tiles = lats * slot // LANES
    rows = members * (lons // seg) * (chans * tiles + chans // 2)
    return pl.pallas_call(
        lambda *refs: cut_kernel(*refs, seg=seg, slot=slot),
        out_shape=pltpu.VMEM((rows, LANES), jnp.bfloat16),
        in_specs=[pl.BlockSpec(memory_space=pltpu.SMEM)]
        + [pl.BlockSpec(memory_space=pltpu.VMEM)] * 3,
        scratch_shapes=[
            pltpu.VMEM((-(-lons // LANES), chans * members * lats, LANES), jnp.float32),
            pltpu.VMEM((rows, LANES), jnp.float32),
        ],
        name="cut",
    )(layer, field, taps, bias)


def run_paste(pieces, shape, seg, slot):
    chans, members, lats, lons = shape
    return pl.pallas_call(
        lambda *refs: paste_kernel(*refs, seg=seg, slot=slot),
        out_shape=jax.ShapeDtypeStruct(shape, jnp.bfloat16),
        scratch_shapes=[
            pltpu.VMEM(pieces.shape, jnp.float32),
            pltpu.VMEM((-(-lons // LANES), chans * members * lats, LANES), jnp.float32),
        ],
        name="paste",
    )(near(pieces))


def run_to_cells(pieces, cells, channels, tiles, edge, sources, layers):
    outs = [(cells, channels), (edge, channels), (edge, channels)]
    return pl.pallas_call(
        lambda *refs: to_cells_kernel(*refs, tiles=tiles, sources=sources),
        out_shape=[pltpu.VMEM(out, jnp.bfloat16) for out in outs]
        + [pltpu.VMEM((layers, TAP_ROWS, channels), jnp.float32)],
        scratch_shapes=[
            pltpu.VMEM(pieces.shape, jnp.float32),
            pltpu.VMEM((cells * channels // LANES, LANES), jnp.float32),
        ],
        name="to_cells",
    )(near(pieces))


def run_middle(parts, taps, rows, bands, cols):
    slot, channels = parts[0].shape[1:]
    groups = channels // LANES
    total = sum(count for _, count in bands)
    return pl.pallas_call(
        lambda *refs: middle_kernel(*refs, bands=bands, tiles=cols // 8),
        out_shape=pltpu.VMEM((groups, total, cols, LANES), jnp.float32),
        scratch_shapes=[
            pltpu.VMEM((groups, rows, slot, LANES), jnp.float32),
            pltpu.VMEM((1, groups, TAPS * TAPS + 1, 8, LANES), jnp.float32),
        ],
        compiler_params=pltpu.CompilerParams(vmem_limit_bytes=16 * 2**20),
        name="middle",
    )(*[near(part) for part in parts], near(taps))


def run_blocks(edges, x, halos, taps, middles, mods, up, up_bias, down, down_bias, scale, tiles):
    lats, slot, channels = x.shape
    groups = channels // LANES
    rows = lats * slot * channels // LANES
    vmem = pl.BlockSpec(memory_space=pltpu.VMEM)
    arrays = (x, *halos, taps, *middles, mods, up_bias, down_bias, scale)
    wide_slot = slot + 8
    return pl.pallas_call(
        lambda *refs: blocks_kernel(*refs, tiles=tiles),
        out_shape=pltpu.VMEM((rows, LANES), jnp.bfloat16),
        in_specs=[pl.BlockSpec(memory_space=pltpu.SMEM)]
        + [vmem] * len(arrays)
        + [pl.BlockSpec(memory_space=pltpu.HBM)] * 2,
        scratch_shapes=[
            pltpu.VMEM((groups, lats + 4 * REACH, LEFT + wide_slot, LANES), jnp.float32),
            pltpu.VMEM((groups, lats + 2 * REACH, wide_slot, LANES), jnp.float32),
            pltpu.VMEM((up.shape[0], groups, TAPS * TAPS + 1, 8, LANES), jnp.float32),
            pltpu.VMEM((groups, lats + 2 * REACH, wide_slot, LANES), jnp.float32),
            pltpu.VMEM((groups, lats, slot, LANES), jnp.float32),
            pltpu.VMEM((rows, LANES), jnp.float32),
            pltpu.VMEM(up.shape, up.dtype),
            pltpu.VMEM(down.shape, down.dtype),
            pltpu.SemaphoreType.DMA((2,)),
        ],
        compiler_params=pltpu.CompilerParams(vmem_limit_bytes=40 * 2**20),
        name="blocks",
    )(edges, *[near(a) for a in arrays], far(up), far(down))


def halo_of(x, north, south, inner, seg):
    rows, segs = lax.axis_size("y"), lax.axis_size("xc")
    reach = 2 * REACH
    down = [(i, i + 1) for i in range(rows - 1)]
    up = [(j, i) for i, j in down]
    top = lax.ppermute(south, "y", down)
    bottom = lax.ppermute(north, "y", up)
    top, bottom, inner = lax.optimization_barrier((top, bottom, inner))
    east = [(i, (i + 1) % segs) for i in range(segs)]
    west = [(j, i) for i, j in east]

    def columns(lo):
        return jnp.concatenate(
            [part[:, lo : lo + reach] for part in (top, x, bottom)], axis=0
        )

    left = lax.ppermute(columns(seg - reach), "xc", east)
    right = lax.ppermute(columns(0), "xc", west)
    return (top, bottom, left, right), inner


def on_device(
    field, noise_level, conv_kernel, conv_bias, modulation,
    expand_weight, expand_bias, project_weight, project_bias, layer_scale,
):
    chans, members, lats, lons = field.shape
    layers = conv_kernel.shape[0]
    halves = lax.axis_size("zh")
    segs = lax.axis_size("xc")
    peers = halves * lax.axis_size("zl") * segs
    channels = chans * lax.axis_size("zl") * segs
    seg = lons // segs
    slot = -(-seg // 8) * 8
    tiles = lats * slot // LANES
    member = lax.axis_index("zh") * lax.axis_size("zl") + lax.axis_index("zl")
    mods = modulation[:, noise_level[member]].reshape(2 * layers, channels)
    band = lax.axis_index("y")
    edges = jnp.stack([band == 0, band == lax.axis_size("y") - 1]).astype(jnp.int32)

    layer = lax.axis_index("zh").astype(jnp.int32).reshape(1)
    pieces = run_cut(layer, field, conv_kernel.transpose(0, 2, 1, 3), conv_bias, seg, slot)
    around = ("zh", "zl", "xc")
    pairs = pieces.reshape(peers, -1, 2, LANES)
    pieces = lax.all_to_all(pairs, around, 0, 0, tiled=True).reshape(-1, LANES)
    shape = (peers, chans * tiles, LANES)
    cells = run_to_cells(
        pieces, halves * lats * slot, channels, tiles, 2 * REACH * slot, peers, layers
    )
    x, north, south = [part.reshape(-1, slot, channels) for part in cells[:3]]
    filters = cells[3]
    edge = 2 * REACH
    reads = x.shape[0] - edge
    cols = slot - 2 * 8
    inner = run_middle([x], filters, x.shape[0], [(0, reads)], cols)
    halos, inner = halo_of(x, north, south, inner, seg)
    parts = [halos[0], x, halos[1]]
    outer = run_middle(parts, filters, 4 * edge, [(0, edge), (2 * edge, edge)], cols)
    pieces = run_blocks(
        edges, x, halos, filters, (inner, outer), mods,
        expand_weight, expand_bias, project_weight, project_bias, layer_scale, tiles,
    )
    pieces = lax.all_to_all(pieces.reshape(shape), around, 0, 0, tiled=True).reshape(-1, LANES)
    return run_paste(pieces, field.shape, seg, slot)


def solution(mesh):
    bands, chan = mesh.shape["band"], mesh.shape["chan"]
    split = Mesh(mesh.devices.reshape(bands // 2, 2, chan // 8, 8), ("y", "zh", "zl", "xc"))
    band, group = ("y", "zh"), ("zl", "xc")
    return jax.shard_map(
        on_device,
        mesh=split,
        in_specs=(
            P(group, None, band, None),
            P(),
            P(None, group, None, None),
            P(None, group),
            P(), P(), P(), P(), P(), P(),
        ),
        out_specs=P(group, None, band, None),
        check_vma=False,
    )
```

```python
import jax
import jax.numpy as jnp
from jax import lax
from jax.experimental import pallas as pl
from jax.experimental.pallas import tpu as pltpu
from jax.sharding import Mesh, PartitionSpec as P

EPS = 1e-06
LANES = 128
TAPS = 7
REACH = 3
LEFT = 8
HALF_LANES = 64
TAP_ROWS = 56


def lane_iota(rows):
    return lax.broadcasted_iota(jnp.int32, (rows, LANES), 1)


def moved_lanes(load, spans, rows, rolled):
    lanes = lane_iota(rows)
    tile = None
    for source, src, dst, width in spans:
        done = 0
        while done < width:
            part, lane = divmod(src + done, LANES)
            take = min(width - done, LANES - lane)
            shift = (dst + done - lane) % LANES
            key = (source, part, shift)
            if key not in rolled:
                value = load(source, part)
                rolled[key] = pltpu.roll(value, shift, 1) if shift else value
            value = rolled[key]
            tile = value if tile is None else jnp.where(lanes >= dst + done, value, tile)
            done += take
    return tile


def spans_of(count, stride, width, tile_index, start_of):
    spans = []
    for item in range(count):
        lo = max(item * stride, tile_index * LANES)
        hi = min(item * stride + width, (tile_index + 1) * LANES)
        if lo < hi:
            spans.append((item, start_of(item) + lo - item * stride, lo - tile_index * LANES, hi - lo))
    return spans


def filter_lines(taps, bias):
    chans = bias.shape[1]
    lines = jnp.zeros((chans, LANES), jnp.float32)
    column = lax.broadcasted_iota(jnp.int32, (TAPS, LANES), 0)
    lane = lax.broadcasted_iota(jnp.int32, (TAPS, LANES), 1)
    for i in range(TAPS):
        place = (lane == i * TAPS + column).astype(jnp.float32).astype(jnp.bfloat16)
        lines = lines + jnp.dot(
            taps[i].astype(jnp.bfloat16), place, preferred_element_type=jnp.float32
        )
    square = (chans, chans)
    same = lax.broadcasted_iota(jnp.int32, square, 0) == lax.broadcasted_iota(jnp.int32, square, 1)
    diagonal = jnp.where(same, jnp.broadcast_to(bias, square), 0.0)
    own = jnp.sum(diagonal, axis=1, keepdims=True)
    lanes = lane_iota(chans)
    lines = jnp.where(lanes == TAPS * TAPS, jnp.broadcast_to(own, lines.shape), lines)
    turned = pltpu.roll(lines, HALF_LANES, 1)
    first = lane_iota(1) < HALF_LANES
    return [
        jnp.where(first, lines[c : c + 1], turned[c + 1 : c + 2]) for c in range(0, chans, 2)
    ]


def cut_kernel(layer_ref, field_ref, taps_ref, bias_ref, out_ref, wide, cut, *, seg, slot):
    chans, members, lats, lons = field_ref.shape
    rows = chans * members
    parts = -(-lons // LANES)
    segs = lons // seg
    tiles = lats * slot // LANES
    layer = layer_ref[0]
    bias = jnp.where(layer == 0, bias_ref[0:1, :], bias_ref[1:2, :])
    lines = filter_lines([taps_ref[layer, i] for i in range(TAPS)], bias)
    piece_rows = chans * tiles + len(lines)
    for e, line in enumerate(lines):
        cut[pl.ds(chans * tiles + e, members * segs, stride=piece_rows), :] = jnp.broadcast_to(
            line, (members * segs, LANES)
        )
    for a in range(parts):
        lo, hi = a * LANES, min((a + 1) * LANES, lons)
        piece = field_ref[:, :, :, lo:hi].astype(jnp.float32).reshape(rows * lats, hi - lo)
        wide[a, :, 0 : hi - lo] = piece
        if hi - lo < LANES:
            wide[a, :, hi - lo :] = jnp.zeros((rows * lats, LANES - hi + lo), jnp.float32)
    for s in range(segs):
        rolled = {}
        for t in range(tiles):
            spans = spans_of(lats, slot, seg, t, lambda item: s * seg)

            def load(lat, part):
                return wide[part, pl.ds(lat, rows, stride=lats), :]

            tile = moved_lanes(load, spans, rows, rolled)
            for c in range(chans):
                start = s * piece_rows + c * tiles + t
                cut[pl.ds(start, members, stride=segs * piece_rows), :] = tile[
                    c * members : (c + 1) * members
                ]
    out_ref[...] = cut[...].astype(jnp.bfloat16)


def paste_kernel(in_ref, out_ref, cut, wide, *, seg, slot):
    chans, members, lats, lons = out_ref.shape
    rows = chans * members
    parts = -(-lons // LANES)
    segs = lons // seg
    tiles = lats * slot // LANES
    cut[...] = in_ref[...].astype(jnp.float32)
    for lat in range(lats):
        rolled = {}
        for a in range(parts):
            spans = spans_of(segs, seg, seg, a, lambda item: lat * slot)

            def load(s, part):
                return jnp.concatenate(
                    [
                        cut[
                            pl.ds(
                                s * chans * tiles + c * tiles + part,
                                members,
                                stride=segs * chans * tiles,
                            ),
                            :,
                        ]
                        for c in range(chans)
                    ],
                    axis=0,
                )

            wide[a, pl.ds(lat, rows, stride=lats), :] = moved_lanes(load, spans, rows, rolled)
    for a in range(parts):
        lo, hi = a * LANES, min((a + 1) * LANES, lons)
        out_ref[:, :, :, lo:hi] = (
            wide[a, :, 0 : hi - lo].reshape(chans, members, lats, hi - lo).astype(jnp.bfloat16)
        )


def to_cells_kernel(
    in_ref, out_ref, north_ref, south_ref, taps_ref, raw, rows32, *, tiles, sources
):
    cells, channels = out_ref.shape
    halves = taps_ref.shape[0]
    data = rows32.shape[0]
    piece_rows = in_ref.shape[0] // sources
    data_rows = data // sources
    raw[...] = in_ref[...].astype(jnp.float32)
    for src in range(sources):
        rows32[src * data_rows : (src + 1) * data_rows, :] = raw[
            src * piece_rows : src * piece_rows + data_rows, :
        ]
    for half in range(halves):
        for t in range(tiles):
            block = rows32[pl.ds(half * channels * tiles + t, channels, stride=tiles), :]
            start = (half * tiles + t) * LANES
            out_ref[start : start + LANES, :] = block.T.astype(jnp.bfloat16)
    edge = north_ref.shape[0]
    north_ref[...] = out_ref[0:edge, :]
    south_ref[...] = out_ref[cells - edge :, :]
    owners = sources // halves
    chans = channels // owners
    taps = taps_ref.shape[1]
    owner = lax.broadcasted_iota(jnp.int32, (owners, channels), 0)
    channel = lax.broadcasted_iota(jnp.int32, (owners, channels), 1)
    for half in range(halves):
        total = jnp.zeros((taps, channels), jnp.float32)
        for e in range(piece_rows - data_rows):
            start = half * owners * piece_rows + data_rows + e
            lines = raw[pl.ds(start, owners, stride=piece_rows), :].T.astype(jnp.bfloat16)
            for k in range(2):
                place = (channel == owner * chans + 2 * e + k).astype(jnp.float32)
                spread = jnp.dot(
                    lines, place.astype(jnp.bfloat16), preferred_element_type=jnp.float32
                )
                total = total + spread[k * HALF_LANES : k * HALF_LANES + taps, :]
        taps_ref[half] = total


def depthwise(source, spread, mixed, layer, bands, tiles, first_col):
    packed = mixed.shape[1] == sum(count for _, count in bands)
    for k in tiles:

        def step_of(g, carry):
            def column_of(j, sums):
                sums = list(sums)
                weights = [spread[layer, g, i * TAPS + j] for i in range(TAPS)]
                at = 0
                for start, count in bands:
                    for r in range(count + TAPS - 1):
                        value = source[g, start + r, pl.ds(first_col + 8 * k + j, 8), :]
                        for i in range(TAPS):
                            if 0 <= r - i < count:
                                sums[at + r - i] = sums[at + r - i] + weights[i] * value
                    at += count
                return tuple(sums)

            total = sum(count for _, count in bands)
            sums = lax.fori_loop(0, TAPS, column_of, (spread[layer, g, TAPS * TAPS],) * total)
            at = 0
            for start, count in bands:
                for r in range(count):
                    row = at if packed else start + r
                    mixed[g, row, 8 * k : 8 * k + 8, :] = sums[at]
                    at += 1
            return carry

        lax.fori_loop(0, source.shape[0], step_of, 0)


def spread_taps(spread, taps_ref, layers):
    for g in range(spread.shape[1]):
        ch = slice(g * LANES, (g + 1) * LANES)
        for layer in range(layers):
            for k in range(TAPS * TAPS + 1):
                spread[layer, g, k] = jnp.broadcast_to(taps_ref[layer, k : k + 1, ch], (8, LANES))


def middle_kernel(*refs, bands, tiles):
    *part_refs, taps_ref, out_ref, source, spread = refs
    for g in range(source.shape[0]):
        row = 0
        for part_ref, lo, hi in part_refs_of(part_refs, source.shape[1]):
            ch = slice(g * LANES, (g + 1) * LANES)
            source[g, row : row + hi - lo, :, :] = part_ref[lo:hi, :, ch].astype(jnp.float32)
            row += hi - lo
    spread_taps(spread, taps_ref, 1)
    depthwise(source, spread, out_ref, 0, bands, range(tiles), 8 - 2 * REACH)


def part_refs_of(part_refs, rows):
    if len(part_refs) == 1:
        return [(part_refs[0], 0, rows)]
    top_ref, x_ref, bottom_ref = part_refs
    edge, lats = top_ref.shape[0], x_ref.shape[0]
    return [(top_ref, 0, edge), (x_ref, 0, edge), (x_ref, lats - edge, lats), (bottom_ref, 0, edge)]


def pointwise(mixed, layer, lats, rows, slot, residual, store, weights):
    mod_ref, up_ref, up_bias_ref, down_ref, down_bias_ref, scale_ref = weights
    groups = mixed.shape[0]
    channels = groups * LANES
    cells = rows * slot
    steps = -(-lats // rows)
    average_matrix = jnp.full((channels, channels), 1.0 / channels, jnp.bfloat16)

    def step_of(step, carry):
        row = jnp.minimum(step * rows, lats - rows)
        parts = [mixed[g, pl.ds(row, rows), 0:slot, :].reshape(cells, LANES) for g in range(groups)]
        rounded = jnp.concatenate(parts, axis=1).astype(jnp.bfloat16)
        average = jnp.dot(rounded, average_matrix, preferred_element_type=jnp.float32)
        centered = rounded.astype(jnp.float32) - average
        variance = jnp.mean(centered * centered, axis=1, keepdims=True)
        gain = 1.0 + mod_ref[2 * layer : 2 * layer + 1, :]
        shift = mod_ref[2 * layer + 1 : 2 * layer + 2, :]
        normed = (centered * lax.rsqrt(variance + EPS) * gain + shift).astype(jnp.bfloat16)
        hidden = (
            jnp.dot(normed, up_ref[layer], preferred_element_type=jnp.float32)
            + up_bias_ref[layer : layer + 1, :]
        )
        doubled = (hidden * (1.0 + lax.erf(hidden * 0.7071067811865476))).astype(jnp.bfloat16)
        result = (
            0.5 * jnp.dot(doubled, down_ref[layer], preferred_element_type=jnp.float32)
            + down_bias_ref[layer : layer + 1, :]
        )
        branch = (scale_ref[layer : layer + 1, :] * result).astype(jnp.bfloat16).astype(jnp.float32)
        for g in range(groups):
            part = branch[:, g * LANES : (g + 1) * LANES].reshape(rows, slot, LANES)
            store(g, row, (residual(g, row) + part).astype(jnp.bfloat16).astype(jnp.float32))
        return carry

    lax.fori_loop(0, steps, step_of, 0)


def blocks_kernel(
    edge_ref, x_ref, top_ref, bottom_ref, left_ref, right_ref, taps_ref, inner_ref, outer_ref, mod_ref,
    up_bias_ref, down_bias_ref, scale_ref, up_hbm, down_hbm,
    out_ref, first, second, spread, mixed, final, rows32, up_ref, down_ref, arrived, *, tiles,
):
    lats, slot, channels = x_ref.shape
    groups = channels // LANES
    reach = 2 * REACH
    wide = lats + reach
    right_at = LEFT + slot - REACH
    copies = [
        pltpu.make_async_copy(up_hbm, up_ref, arrived.at[0]),
        pltpu.make_async_copy(down_hbm, down_ref, arrived.at[1]),
    ]
    for copy in copies:
        copy.start()
    for g in range(groups):
        ch = slice(g * LANES, (g + 1) * LANES)
        first[g, 0:reach, LEFT : LEFT + slot, :] = top_ref[:, :, ch].astype(jnp.float32)
        first[g, reach : reach + lats, LEFT : LEFT + slot, :] = x_ref[:, :, ch].astype(jnp.float32)
        first[g, reach + lats :, LEFT : LEFT + slot, :] = bottom_ref[:, :, ch].astype(jnp.float32)
        first[g, :, LEFT + slot :, :] = jnp.zeros(
            (lats + 2 * reach, first.shape[2] - LEFT - slot, LANES), jnp.float32
        )
        first[g, :, LEFT - reach : LEFT, :] = left_ref[:, :, ch].astype(jnp.float32)
        first[g, :, right_at : right_at + reach, :] = right_ref[:, :, ch].astype(jnp.float32)
        middle = slice(8, 8 + inner_ref.shape[2])
        mixed[g, 0:reach, middle, :] = outer_ref[g, 0:reach]
        mixed[g, reach:lats, middle, :] = inner_ref[g]
        mixed[g, lats:wide, middle, :] = outer_ref[g, reach:]
    spread_taps(spread, taps_ref, taps_ref.shape[0])
    weights = (mod_ref, up_ref, up_bias_ref, down_ref, down_bias_ref, scale_ref)

    wide_slot = slot + 8
    covered = inner_ref.shape[2] // 8
    sides = [k for k in range(wide_slot // 8) if not 1 <= k <= covered]
    depthwise(first, spread, mixed, 0, [(0, wide)], sides, LEFT - reach)

    for copy in copies:
        copy.wait()

    def first_store(g, row, value):
        second[g, pl.ds(row, 38), :, :] = value

    pointwise(
        mixed, 0, wide, 38, wide_slot,
        lambda g, row: first[g, pl.ds(row + REACH, 38), LEFT - REACH : LEFT - REACH + wide_slot, :],
        first_store, weights,
    )

    @pl.when(edge_ref[0] == 1)
    def _():
        second[:, 0:REACH, :, :] = jnp.zeros((groups, REACH, wide_slot, LANES), jnp.float32)

    @pl.when(edge_ref[1] == 1)
    def _():
        second[:, REACH + lats :, :, :] = jnp.zeros((groups, REACH, wide_slot, LANES), jnp.float32)

    depthwise(second, spread, mixed, 1, [(0, lats)], range(slot // 8), 0)

    def final_store(g, row, value):
        final[g, pl.ds(row, 32), :, :] = value

    pointwise(
        mixed, 1, lats, 32, slot,
        lambda g, row: second[g, pl.ds(row + REACH, 32), REACH : REACH + slot, :],
        final_store, weights,
    )
    flat = lats * slot // tiles // LANES
    rows_per = LANES * 3 // slot
    for half in range(flat):
        for g in range(groups):
            for part in range(tiles // 3):
                lat = (half * tiles + part * 3) * LANES // slot
                block = final[g, lat : lat + rows_per, :, :].reshape(rows_per * slot, LANES)
                for t in range(3):
                    start = half * channels * tiles + g * LANES * tiles + part * 3 + t
                    rows32[pl.ds(start, LANES, stride=tiles), :] = block[
                        t * LANES : (t + 1) * LANES
                    ].T
    out_ref[...] = rows32[...].astype(jnp.bfloat16)


def near(x):
    return pltpu.with_memory_space_constraint(x, pltpu.VMEM)


def far(x):
    return pltpu.with_memory_space_constraint(x, pltpu.HBM)


def run_cut(layer, field, taps, bias, seg, slot):
    chans, members, lats, lons = field.shape
    tiles = lats * slot // LANES
    rows = members * (lons // seg) * (chans * tiles + chans // 2)
    return pl.pallas_call(
        lambda *refs: cut_kernel(*refs, seg=seg, slot=slot),
        out_shape=pltpu.VMEM((rows, LANES), jnp.bfloat16),
        in_specs=[pl.BlockSpec(memory_space=pltpu.SMEM)]
        + [pl.BlockSpec(memory_space=pltpu.VMEM)] * 3,
        scratch_shapes=[
            pltpu.VMEM((-(-lons // LANES), chans * members * lats, LANES), jnp.float32),
            pltpu.VMEM((rows, LANES), jnp.float32),
        ],
        name="cut",
    )(layer, field, taps, bias)


def run_paste(pieces, shape, seg, slot):
    chans, members, lats, lons = shape
    return pl.pallas_call(
        lambda *refs: paste_kernel(*refs, seg=seg, slot=slot),
        out_shape=jax.ShapeDtypeStruct(shape, jnp.bfloat16),
        scratch_shapes=[
            pltpu.VMEM(pieces.shape, jnp.float32),
            pltpu.VMEM((-(-lons // LANES), chans * members * lats, LANES), jnp.float32),
        ],
        name="paste",
    )(near(pieces))


def run_to_cells(pieces, cells, channels, tiles, edge, sources, layers):
    outs = [(cells, channels), (edge, channels), (edge, channels)]
    return pl.pallas_call(
        lambda *refs: to_cells_kernel(*refs, tiles=tiles, sources=sources),
        out_shape=[pltpu.VMEM(out, jnp.bfloat16) for out in outs]
        + [pltpu.VMEM((layers, TAP_ROWS, channels), jnp.float32)],
        scratch_shapes=[
            pltpu.VMEM(pieces.shape, jnp.float32),
            pltpu.VMEM((cells * channels // LANES, LANES), jnp.float32),
        ],
        name="to_cells",
    )(near(pieces))


def run_middle(parts, taps, rows, bands, cols):
    slot, channels = parts[0].shape[1:]
    groups = channels // LANES
    total = sum(count for _, count in bands)
    return pl.pallas_call(
        lambda *refs: middle_kernel(*refs, bands=bands, tiles=cols // 8),
        out_shape=pltpu.VMEM((groups, total, cols, LANES), jnp.float32),
        scratch_shapes=[
            pltpu.VMEM((groups, rows, slot, LANES), jnp.float32),
            pltpu.VMEM((1, groups, TAPS * TAPS + 1, 8, LANES), jnp.float32),
        ],
        compiler_params=pltpu.CompilerParams(vmem_limit_bytes=16 * 2**20),
        name="middle",
    )(*[near(part) for part in parts], near(taps))


def run_blocks(edges, x, halos, taps, middles, mods, up, up_bias, down, down_bias, scale, tiles):
    lats, slot, channels = x.shape
    groups = channels // LANES
    rows = lats * slot * channels // LANES
    vmem = pl.BlockSpec(memory_space=pltpu.VMEM)
    arrays = (x, *halos, taps, *middles, mods, up_bias, down_bias, scale)
    wide_slot = slot + 8
    return pl.pallas_call(
        lambda *refs: blocks_kernel(*refs, tiles=tiles),
        out_shape=pltpu.VMEM((rows, LANES), jnp.bfloat16),
        in_specs=[pl.BlockSpec(memory_space=pltpu.SMEM)]
        + [vmem] * len(arrays)
        + [pl.BlockSpec(memory_space=pltpu.HBM)] * 2,
        scratch_shapes=[
            pltpu.VMEM((groups, lats + 4 * REACH, LEFT + wide_slot, LANES), jnp.float32),
            pltpu.VMEM((groups, lats + 2 * REACH, wide_slot, LANES), jnp.float32),
            pltpu.VMEM((up.shape[0], groups, TAPS * TAPS + 1, 8, LANES), jnp.float32),
            pltpu.VMEM((groups, lats + 2 * REACH, wide_slot, LANES), jnp.float32),
            pltpu.VMEM((groups, lats, slot, LANES), jnp.float32),
            pltpu.VMEM((rows, LANES), jnp.float32),
            pltpu.VMEM(up.shape, up.dtype),
            pltpu.VMEM(down.shape, down.dtype),
            pltpu.SemaphoreType.DMA((2,)),
        ],
        compiler_params=pltpu.CompilerParams(vmem_limit_bytes=40 * 2**20),
        name="blocks",
    )(edges, *[near(a) for a in arrays], far(up), far(down))


def halo_of(x, north, south, inner, seg):
    rows, segs = lax.axis_size("y"), lax.axis_size("xc")
    reach = 2 * REACH
    down = [(i, i + 1) for i in range(rows - 1)]
    up = [(j, i) for i, j in down]
    top = lax.ppermute(south, "y", down)
    bottom = lax.ppermute(north, "y", up)
    top, bottom, inner = lax.optimization_barrier((top, bottom, inner))
    east = [(i, (i + 1) % segs) for i in range(segs)]
    west = [(j, i) for i, j in east]

    def columns(lo):
        return jnp.concatenate(
            [part[:, lo : lo + reach] for part in (top, x, bottom)], axis=0
        )

    left = lax.ppermute(columns(seg - reach), "xc", east)
    right = lax.ppermute(columns(0), "xc", west)
    return (top, bottom, left, right), inner


def on_device(
    field, noise_level, conv_kernel, conv_bias, modulation,
    expand_weight, expand_bias, project_weight, project_bias, layer_scale,
):
    chans, members, lats, lons = field.shape
    layers = conv_kernel.shape[0]
    halves = lax.axis_size("zh")
    segs = lax.axis_size("xc")
    peers = halves * lax.axis_size("zl") * segs
    channels = chans * lax.axis_size("zl") * segs
    seg = lons // segs
    slot = -(-seg // 8) * 8
    tiles = lats * slot // LANES
    member = lax.axis_index("zh") * lax.axis_size("zl") + lax.axis_index("zl")
    mods = modulation[:, noise_level[member]].reshape(2 * layers, channels)
    band = lax.axis_index("y")
    edges = jnp.stack([band == 0, band == lax.axis_size("y") - 1]).astype(jnp.int32)

    layer = lax.axis_index("zh").astype(jnp.int32).reshape(1)
    pieces = run_cut(layer, field, conv_kernel.transpose(0, 2, 1, 3), conv_bias, seg, slot)
    around = ("zh", "zl", "xc")
    pairs = pieces.reshape(peers, -1, 2, LANES)
    pieces = lax.all_to_all(pairs, around, 0, 0, tiled=True).reshape(-1, LANES)
    shape = (peers, chans * tiles, LANES)
    cells = run_to_cells(
        pieces, halves * lats * slot, channels, tiles, 2 * REACH * slot, peers, layers
    )
    x, north, south = [part.reshape(-1, slot, channels) for part in cells[:3]]
    filters = cells[3]
    edge = 2 * REACH
    reads = x.shape[0] - edge
    cols = slot - 2 * 8
    inner = run_middle([x], filters, x.shape[0], [(0, reads)], cols)
    halos, inner = halo_of(x, north, south, inner, seg)
    parts = [halos[0], x, halos[1]]
    outer = run_middle(parts, filters, 4 * edge, [(0, edge), (2 * edge, edge)], cols)
    pieces = run_blocks(
        edges, x, halos, filters, (inner, outer), mods,
        expand_weight, expand_bias, project_weight, project_bias, layer_scale, tiles,
    )
    pieces = lax.all_to_all(pieces.reshape(shape), around, 0, 0, tiled=True).reshape(-1, LANES)
    return run_paste(pieces, field.shape, seg, slot)


def solution(mesh):
    bands, chan = mesh.shape["band"], mesh.shape["chan"]
    split = Mesh(mesh.devices.reshape(bands // 2, 2, chan // 8, 8), ("y", "zh", "zl", "xc"))
    band, group = ("y", "zh"), ("zl", "xc")
    return jax.shard_map(
        on_device,
        mesh=split,
        in_specs=(
            P(group, None, band, None),
            P(),
            P(None, group, None, None),
            P(None, group),
            P(), P(), P(), P(), P(), P(),
        ),
        out_specs=P(group, None, band, None),
        check_vma=False,
    )
```
